128 devices in a mesh: rows: 16 (over y, x), cols: 8 (over z, core).
Axes of the slice: x: 4, y: 4, z: 4, core: 2. Of those that a mesh axis runs over, the one named last changes fastest.
Arguments:
- affiliations: float32 [131072, 512], P(('rows', 'cols')), as said below
- tile_block: int32 [128, 240], P(('rows', 'cols')), may hold values from 0 to 1023, as said below
- tile_target: int32 [128, 240], P(('rows', 'cols')), may hold values from 0 to 7
- tile_pattern: int32 [128, 240], P(('rows', 'cols')), may hold values from 0 to 191
- tile_count: int32 [128], P(('rows', 'cols')), may hold values from 15 to 240, as said below
- block_home: int32 [1024], replicated, may hold values from 0 to 1023, as said below
- patterns: int32 [192, 5, 128], replicated, may hold values from 0 to 1073741823, as said below
Outputs:
- updated_affiliations: float32 [131072, 512], P(('rows', 'cols'))
The draws below stay inside these ranges and needn't reach their ends.
Inputs may be any that keep to these rules, and one draw needn't show every extreme that they name: Live tiles of a device are the first tile_count of its slots, in order of their neighbour's owner row (storage block // 64); some device has exactly 240. `tile_block`: A live tile's neighbour is stored on a device of the same cols index and another rows index; a device's live tiles name at most 4 distinct blocks of one owner row, and in every draw some device names exactly 4 of every other owner row; a (target, neighbour) pair is live at most once on a device; slots past the count hold valid block numbers. `block_home`: A permutation of the node blocks. `patterns`: bits at rows 128 and beyond are zero. `affiliations`: Positive.
All inputs are finite; a program needn't handle non-finite values.
Results may differ from the reference program's by a relative error of at most 0.0003.
Values may be sent and summed in bfloat16 or wider, within the bound.
No kernel may reach another device: no remote copies, remote signals or barrier semaphores. Data moves between devices by JAX's collectives and lax.ppermute only.
A program may use at most 192 MiB of HBM per device.

```python
import jax
import jax.numpy as jnp
from jax import lax

C = 512
BLOCK = 128
BPD = 8
LINKS = 4
PATTERNS = 192
STEPS = 2
PEER_CAP = 4
TILE_CAP = 240
NBLOCKS = 1024
NODES = 131072
WORDS = 5
UNIT = 1572864
N_ROWS = 16
N_COLS = 8
DEVICES = 128


def tile_plan(key):
    device_total = N_ROWS * N_COLS
    home_slots = jax.random.permutation(jax.random.fold_in(key, 11), NBLOCKS).astype(jnp.int32)
    inverse = jnp.argsort(home_slots).astype(jnp.int32)
    levels_j = jax.random.randint(jax.random.fold_in(key, 12), (device_total, N_ROWS), 1, PEER_CAP + 1)
    levels_l = jax.random.randint(jax.random.fold_in(key, 13), (device_total, N_ROWS, PEER_CAP), 1, LINKS + 1)
    heavy_device = jax.random.randint(jax.random.fold_in(key, 14), (), 0, device_total)
    is_heavy = jnp.arange(device_total) == heavy_device
    levels_j = jnp.where(is_heavy[:, None], PEER_CAP, levels_j)
    levels_l = jnp.where(is_heavy[:, None, None], LINKS, levels_l)
    score_j = jax.random.randint(jax.random.fold_in(key, 15), (device_total, N_ROWS, BPD), 0, 2 ** 20) * BPD + jnp.arange(BPD)
    pick_j = jnp.argsort(score_j, axis=-1)[..., :PEER_CAP].astype(jnp.int32)
    score_u = jax.random.randint(jax.random.fold_in(key, 16), (device_total, N_ROWS, PEER_CAP, BPD), 0, 2 ** 20) * BPD + jnp.arange(BPD)
    pick_u = jnp.argsort(score_u, axis=-1)[..., :LINKS].astype(jnp.int32)
    device_ids = jnp.arange(device_total)
    row_of = device_ids // N_COLS
    col_of = device_ids % N_COLS
    owners = jnp.arange(N_ROWS)
    valid_tiles = (owners[None, :, None, None] != row_of[:, None, None, None]) & (jnp.arange(PEER_CAP)[None, None, :, None] < levels_j[:, :, None, None]) & (jnp.arange(LINKS)[None, None, None, :] < levels_l[:, :, :, None])
    slot_ids = (owners[None, :, None] * N_COLS + col_of[:, None, None]) * BPD + pick_j
    block_ids = jnp.broadcast_to(inverse[slot_ids][..., None], (device_total, N_ROWS, PEER_CAP, LINKS))
    flat_valid = valid_tiles.reshape(device_total, -1).astype(jnp.int32)
    flat_blocks = block_ids.reshape(device_total, -1)
    flat_targets = pick_u.reshape(device_total, -1)
    width_all = flat_valid.shape[1]
    ordering = jnp.argsort((1 - flat_valid) * width_all + jnp.arange(width_all)[None, :], axis=1)[:, :TILE_CAP]
    tile_blocks = jnp.take_along_axis(flat_blocks, ordering, axis=1).astype(jnp.int32)
    tile_targets = jnp.take_along_axis(flat_targets, ordering, axis=1).astype(jnp.int32)
    live_count = jnp.sum(flat_valid, axis=1).astype(jnp.int32)
    return (home_slots, tile_blocks, tile_targets, live_count)


def draw_block_home(key, part):
    return tile_plan(key)[0]


def draw_tile_block(key, part):
    return tile_plan(key)[1]


def draw_tile_target(key, part):
    return tile_plan(key)[2]


def draw_tile_count(key, part):
    return tile_plan(key)[3]


def draw_patterns(key, part):
    full_words = jax.random.randint(jax.random.fold_in(key, 1), (PATTERNS, WORDS - 1, BLOCK), 0, 2 ** 30)
    tail_words = jax.random.randint(jax.random.fold_in(key, 2), (PATTERNS, 1, BLOCK), 0, 2 ** (BLOCK - 30 * (WORDS - 1)))
    return jnp.concatenate([full_words, tail_words], axis=1).astype(jnp.int32)


def draw_affiliations(key, part):
    total_nodes = NBLOCKS * BLOCK
    node_slot = jnp.arange(total_nodes) // BLOCK
    growth = 1.0 + 2.0 * node_slot.astype(jnp.float32) / max(NBLOCKS - 1, 1)
    member_bits = jax.random.randint(jax.random.fold_in(key, 7), (NBLOCKS, C), 0, 32)
    membership = (member_bits == 0).astype(jnp.float32)
    block_profile = 1.0 + 31.0 * membership
    row_scale = jnp.exp(jax.random.uniform(jax.random.fold_in(key, 3), (total_nodes,), jnp.float32, jnp.log(0.3), jnp.log(3.0)))
    community_scale = jnp.exp(jax.random.uniform(jax.random.fold_in(key, 4), (C,), jnp.float32, jnp.log(0.5), jnp.log(2.0)))
    roughness = jax.random.uniform(jax.random.fold_in(key, 6), (total_nodes, C), jnp.float32, 0.2, 1.8)
    profile_rows = block_profile[node_slot] * community_scale[None, :]
    values = roughness * profile_rows * (row_scale * growth)[:, None]
    return values.astype(jnp.float32)


def set_ends(entries, stream_key, smallest, top_value):
    longest = entries.shape.index(max(entries.shape))
    spots = []
    for shift in (0, 1):
        where = [jax.random.randint(jax.random.fold_in(stream_key, axis), (), 0, length) for axis, length in enumerate(entries.shape)]
        where[longest] = (where[longest] + shift) % entries.shape[longest]
        spots.append(tuple(where))
    return entries.at[spots[0]].set(smallest).at[spots[1]].set(top_value)


def setup_inputs(seed: int = 0) -> dict:
    keys = jax.random.split(jax.random.key(seed), 8)
    return {
        "affiliations": draw_affiliations(jax.random.fold_in(keys[7], 71), 0),
        "tile_block": draw_tile_block(jax.random.fold_in(keys[7], 71), 0),
        "tile_target": draw_tile_target(jax.random.fold_in(keys[7], 71), 0),
        "tile_pattern": set_ends(jax.random.randint(keys[3], (DEVICES, TILE_CAP), 0, PATTERNS), jax.random.fold_in(keys[3], 1), 0, PATTERNS - 1).astype(jnp.int32),
        "tile_count": draw_tile_count(jax.random.fold_in(keys[7], 71), 0),
        "block_home": draw_block_home(jax.random.fold_in(keys[7], 71), 0),
        "patterns": draw_patterns(jax.random.fold_in(keys[7], 71), 0),
    }


floor_value = 0.001


def unpack_masks(packed):
    shifts = jnp.arange(30, dtype=jnp.int32)
    bit_values = jnp.right_shift(packed[:, :, None, :], shifts[None, None, :, None]) & 1
    bit_values = bit_values.reshape(packed.shape[0], packed.shape[1] * 30, packed.shape[2])
    return bit_values[:, :BLOCK, :].astype(jnp.float32)


def tile_terms(own_rows, remote_rows, tile_masks):
    own_wide = own_rows.astype(jnp.float32)
    remote_wide = remote_rows.astype(jnp.float32)
    scores = jnp.einsum("tnc,tmc->tnm", own_wide, remote_wide, precision=lax.Precision.HIGHEST) / UNIT
    weights = (tile_masks / (1.0 - jnp.exp(-jnp.maximum(scores, floor_value)))).astype(jnp.bfloat16)
    return jnp.einsum("tnm,tmc->tnc", weights.astype(jnp.float32), remote_wide, precision=lax.Precision.HIGHEST)


def reference(affiliations, tile_block, tile_target, tile_pattern, tile_count, block_home, patterns):
    step_size = 0.3 / NODES
    current = affiliations
    device_ids = jnp.arange(N_ROWS * N_COLS, dtype=jnp.int32)
    for step_number in range(STEPS):
        col_sums = jnp.sum(current, axis=0)
        blocks_bf = current.astype(jnp.bfloat16).reshape(NBLOCKS, BLOCK, C)

        def per_device(running, inputs):
            device_index, block_ids, targets, pattern_ids, live_count = inputs
            own_blocks = lax.dynamic_slice_in_dim(blocks_bf, (device_index * BPD).astype(jnp.int32), BPD, 0)
            remote_rows = blocks_bf[block_home[block_ids]]
            own_rows = own_blocks[targets]
            terms = tile_terms(own_rows, remote_rows, unpack_masks(patterns[pattern_ids]))
            live_tiles = jnp.arange(TILE_CAP, dtype=jnp.int32) < live_count
            placement = ((targets[:, None] == jnp.arange(BPD, dtype=jnp.int32)[None, :]) & live_tiles[:, None]).astype(jnp.float32)
            return running, jnp.einsum("tb,tnc->bnc", placement, terms, precision=lax.Precision.HIGHEST)

        _, neighbour = lax.scan(per_device, jnp.zeros((), jnp.float32), (device_ids, tile_block, tile_target, tile_pattern, tile_count))
        gradient = neighbour.reshape(NODES, C) - col_sums[None, :]
        current = jnp.maximum(current + step_size * gradient, 0.0)
    return current
```

```python
import functools

import jax
import jax.numpy as jnp
from jax import lax
from jax.experimental import pallas as pl
from jax.experimental.pallas import tpu as pltpu
from jax.sharding import Mesh
from jax.sharding import PartitionSpec as P

C = 512
BLOCK = 128
STEPS = 2
BPD = 8
SIDE = 4
CAP = 4
N_COLS = 8
NODES = 131072
UNIT = 1572864
PATTERNS = 192
TILES = 240
GROUP = 2
PHASES = 3
KEYS = PHASES * BPD
GROUPS = (TILES + KEYS * (GROUP - 1)) // GROUP + 2 * PHASES
SLOTS = GROUPS * GROUP
FLOOR = 0.001
STEP_SIZE = 0.3 / NODES

ALL = ("rows_0", "rows_1", "cols_0", "cols_1")
VMEM = pl.BlockSpec(memory_space=pltpu.VMEM)
SMEM = pl.BlockSpec(memory_space=pltpu.SMEM)
ANY = pl.BlockSpec(memory_space=pl.ANY)


def pairs(first, second):
    out = []
    for y in range(SIDE):
        for x in range(SIDE):
            for z in range(4):
                for core in range(2):
                    dx, dy = (first, second) if core == 0 else (second, first)
                    sy, sx = (y + dy) % SIDE, (x + dx) % SIDE
                    out.append((((sy * 4 + sx) * 4 + z) * 2 + core, ((y * 4 + x) * 4 + z) * 2 + core))
    return out


def fetch(value, first, second):
    return lax.ppermute(value, ALL, pairs(first, second))


def sum_over_mesh(part):
    for axis, size in (("cols_1", 2), ("cols_0", 4), ("rows_1", 4), ("rows_0", 4)):
        step = 1
        while step < size:
            part = part + lax.ppermute(part, axis, [(i, i ^ step) for i in range(size)])
            step *= 2
    return part


def plan_kernel(
    place, blocks, targets, pattern_ids, count, home,
    requests, sources, patterns, group_target, phase_start,
    rank, fill, tile_source, tile_key, per_key, cursor,
):
    first, second, core = place[0], place[1], place[2]
    live = count[0]

    def clear(ref, size, value):
        def body(i, _):
            ref[i] = value
            return 0

        lax.fori_loop(0, size, body, 0)

    clear(rank, 128, -1)
    clear(fill, 16, 0)
    clear(requests, 64, 0)
    clear(per_key, KEYS, 0)
    clear(sources, SLOTS, 0)
    clear(patterns, SLOTS, PATTERNS)
    clear(group_target, GROUPS, 0)

    def note(t, _):
        slot = home[blocks[t]]
        row = slot // (N_COLS * BPD)
        local = slot & (BPD - 1)
        y, x = row // SIDE, row & (SIDE - 1)
        owner_first = jnp.where(core == 0, x, y)
        owner_second = jnp.where(core == 0, y, x)
        k = (owner_first - first) & (SIDE - 1)
        m = (owner_second - second) & (SIDE - 1)
        pair = m * SIDE + k
        seen = rank[pair * BPD + local]
        held = fill[pair]
        mine = jnp.where(seen < 0, held, seen)
        mine = jnp.minimum(mine, CAP - 1)
        rank[pair * BPD + local] = mine
        fill[pair] = jnp.where(seen < 0, held + 1, held)
        requests[pair * CAP + mine] = local
        whole = jnp.maximum(k - 1, 0) * BPD + local
        picked = k * CAP + mine + jnp.where(m == 3, SIDE * CAP, 0)
        tile_source[t] = jnp.where(m == 0, whole, picked)
        phase = jnp.where(m == 0, 0, jnp.where(m == 2, 2, 1))
        key = phase * BPD + targets[t]
        tile_key[t] = key
        per_key[key] = per_key[key] + 1
        return 0

    lax.fori_loop(0, live, note, 0)

    base = jnp.int32(0)
    for phase in range(PHASES):
        phase_start[phase] = base
        top = base
        for target in range(BPD):
            key = phase * BPD + target
            size = (per_key[key] + GROUP - 1) // GROUP
            cursor[key] = top * GROUP
            top = top + size
        used = top - base
        base = base + jnp.maximum(2, (used + 1) // 2 * 2)
    phase_start[PHASES] = base

    def put(t, _):
        key = tile_key[t]
        at = cursor[key]
        cursor[key] = at + 1
        sources[at] = tile_source[t]
        patterns[at] = pattern_ids[t]
        group_target[at // GROUP] = targets[t]
        return 0

    lax.fori_loop(0, live, put, 0)


def make_plan(place, blocks, targets, pattern_ids, count, home):
    i32 = jnp.int32
    return pl.pallas_call(
        plan_kernel,
        out_shape=(
            jax.ShapeDtypeStruct((64,), i32),
            jax.ShapeDtypeStruct((SLOTS,), i32),
            jax.ShapeDtypeStruct((SLOTS,), i32),
            jax.ShapeDtypeStruct((GROUPS,), i32),
            jax.ShapeDtypeStruct((PHASES + 1,), i32),
        ),
        in_specs=[SMEM] * 6,
        out_specs=(SMEM,) * 5,
        scratch_shapes=[
            pltpu.SMEM((128,), i32),
            pltpu.SMEM((16,), i32),
            pltpu.SMEM((TILES,), i32),
            pltpu.SMEM((TILES,), i32),
            pltpu.SMEM((KEYS,), i32),
            pltpu.SMEM((KEYS,), i32),
        ],
        name="plan",
    )(place, blocks, targets, pattern_ids, count, home)


def pick_kernel(asked, own, far1, far2, far3, out1, out2, out3, sems):
    copies = []
    for m, out in enumerate((out1, out2, out3)):
        for k, table in enumerate((own, far1, far2, far3)):
            for r in range(CAP):
                local = asked[m, k * CAP + r]
                copies.append(
                    pltpu.make_async_copy(
                        table.at[local], out.at[k * CAP + r], sems.at[len(copies)]
                    )
                )
    for copy in copies:
        copy.start()
    for copy in copies:
        copy.wait()


def pick(asked, own, far):
    shape = jax.ShapeDtypeStruct((SIDE * CAP, BLOCK, C), jnp.bfloat16)
    return pl.pallas_call(
        pick_kernel,
        out_shape=(shape,) * 3,
        in_specs=[SMEM] + [ANY] * 4,
        out_specs=(ANY,) * 3,
        scratch_shapes=[pltpu.SemaphoreType.DMA((3 * SIDE * CAP,))],
        name="pick",
    )(asked, own, *far)


def tile_kernel(phase, parts, step_kind, *refs):
    refs = list(refs)
    sources, pattern_ids, group_target, phase_start = refs[:4]
    words, own = refs[4:6]
    tables = refs[6 : 6 + parts]
    refs = refs[6 + parts :]
    last = phase == PHASES - 1
    if phase > 0:
        earlier = refs.pop(0)
    if last:
        current, col_sums = refs.pop(0), refs.pop(0)
        fresh = refs.pop(0)
        if step_kind == "more":
            rounded, part_sums = refs.pop(0), refs.pop(0)
        total = None
    else:
        total = refs.pop(0)
    if last:
        total = refs.pop(0)
    held, score_a, score_b, bits, sems = refs

    copies = []
    at = 0
    for i, table in enumerate(tables):
        n = table.shape[0]
        copies.append(pltpu.make_async_copy(table, held.at[pl.ds(at, n)], sems.at[i]))
        at += n
    for copy in copies:
        copy.start()
    row = lax.broadcasted_iota(jnp.int32, (BLOCK, BLOCK), 0)
    bits[...] = lax.shift_left(jnp.ones_like(row), lax.rem(row, 30))
    if phase > 0:
        total[...] = earlier[...]
    else:
        total[...] = jnp.zeros_like(total)
    for copy in copies:
        copy.wait()

    sub = lax.broadcasted_iota(jnp.int32, (8, BLOCK), 0)

    def word_rows(pattern):
        rows = []
        for v in range(BLOCK // 8):
            low, high = 8 * v // 30, (8 * v + 7) // 30
            chunk = jnp.broadcast_to(words[pattern, low : low + 1, :], (8, BLOCK))
            if high != low:
                other = jnp.broadcast_to(words[pattern, high : high + 1, :], (8, BLOCK))
                chunk = jnp.where(sub + 8 * v < 30 * high, chunk, other)
            rows.append(chunk)
        return jnp.concatenate(rows, axis=0)

    def remote(group):
        return jnp.concatenate([held[sources[group * GROUP + i]] for i in range(GROUP)], axis=0)

    def score(group, out):
        mine = own[group_target[group]]
        out[...] = lax.dot_general(
            mine, remote(group), (((1,), (1,)), ((), ())), preferred_element_type=jnp.float32
        )

    def add(group, scores):
        weights = []
        for i in range(GROUP):
            packed = word_rows(pattern_ids[group * GROUP + i])
            negative = jnp.minimum(scores[:, i * BLOCK : (i + 1) * BLOCK] * (-1.0 / UNIT), -FLOOR)
            weight = 1.0 / (1.0 - jnp.exp(negative))
            linked = (packed & bits[...]) != 0
            weights.append(jnp.where(linked, weight, 0.0).astype(jnp.bfloat16))
        target = group_target[group]
        total[target] += jnp.dot(
            jnp.concatenate(weights, axis=1), remote(group), preferred_element_type=jnp.float32
        )

    start, stop = phase_start[phase], phase_start[phase + 1]
    score(start, score_a)

    def two(i, _):
        group = start + 2 * i
        score(group + 1, score_b)
        add(group, score_a)
        score(jnp.minimum(group + 2, stop - 1), score_a)
        add(group + 1, score_b)
        return 0

    lax.fori_loop(0, (stop - start) // 2, two, 0)

    if last:
        sums = jnp.sum(col_sums[...], axis=0, keepdims=True)
        parts_sum = jnp.zeros((8, C), jnp.float32)
        for j in range(BPD):
            moved = current[j] + STEP_SIZE * (total[j] - sums)
            moved = jnp.maximum(moved, 0.0)
            fresh[j] = moved
            if step_kind == "more":
                rounded[j] = moved.astype(jnp.bfloat16)
                parts_sum = parts_sum + jnp.sum(moved.reshape(BLOCK // 8, 8, C), axis=0)
        if step_kind == "more":
            part_sums[...] = parts_sum


def run_tiles(phase, lists, words, own, tables, earlier=None, current=None, col_sums=None, more=True):
    f32 = jnp.float32
    blocks = jax.ShapeDtypeStruct((BPD, BLOCK, C), f32)
    args = [*lists, words, own, *tables]
    specs = [SMEM] * 4 + [VMEM] * 2 + [ANY] * len(tables)
    scratch = []
    if phase > 0:
        args.append(earlier)
        specs.append(VMEM)
    if phase == PHASES - 1:
        args += [current, col_sums]
        specs += [VMEM, VMEM]
        out = [blocks]
        if more:
            out += [
                jax.ShapeDtypeStruct((BPD, BLOCK, C), jnp.bfloat16),
                jax.ShapeDtypeStruct((8, C), f32),
            ]
        scratch.append(pltpu.VMEM((BPD, BLOCK, C), f32))
    else:
        out = [blocks]
    rows = sum(t.shape[0] for t in tables)
    scratch += [
        pltpu.VMEM((rows, BLOCK, C), jnp.bfloat16),
        pltpu.VMEM((BLOCK, GROUP * BLOCK), f32),
        pltpu.VMEM((BLOCK, GROUP * BLOCK), f32),
        pltpu.VMEM((BLOCK, BLOCK), jnp.int32),
        pltpu.SemaphoreType.DMA((len(tables),)),
    ]
    return pl.pallas_call(
        functools.partial(tile_kernel, phase, len(tables), "more" if more else "end"),
        out_shape=tuple(out),
        in_specs=specs,
        out_specs=(VMEM,) * len(out),
        scratch_shapes=scratch,
        compiler_params=pltpu.CompilerParams(vmem_limit_bytes=48 << 20),
        name="tiles%d" % phase,
    )(*args)


def per_device(affiliations, tile_block, tile_target, tile_pattern, tile_count, block_home, patterns):
    y, x = lax.axis_index("rows_0"), lax.axis_index("rows_1")
    core = lax.axis_index("cols_1")
    first = jnp.where(core == 0, x, y)
    second = jnp.where(core == 0, y, x)
    place = jnp.stack([first, second, core]).astype(jnp.int32)
    requests, *lists = make_plan(
        place, tile_block[0], tile_target[0], tile_pattern[0], tile_count, block_home
    )
    requests = requests.reshape(SIDE, SIDE * CAP)
    asked = jnp.stack([fetch(requests[m], 0, SIDE - m) for m in (1, 2, 3)])
    words = jnp.concatenate([patterns, jnp.zeros((1, *patterns.shape[1:]), jnp.int32)], axis=0)

    current = affiliations.reshape(BPD, BLOCK, C)
    own = current.astype(jnp.bfloat16)
    part = jnp.sum(affiliations.reshape(BPD * BLOCK // 8, 8, C), axis=0)
    for step in range(STEPS):
        far1, far3, far2 = fetch(own, 1, 0), fetch(own, 3, 0), fetch(own, 2, 0)
        col_sums = sum_over_mesh(part)
        out1, out2, out3 = pick(asked, own, (far1, far2, far3))
        side1, side3, side2 = fetch(out1, 0, 1), fetch(out3, 0, 3), fetch(out2, 0, 2)
        (total,) = run_tiles(0, lists, words, own, (far1, far2, far3))
        (total,) = run_tiles(1, lists, words, own, (side1, side3), total)
        more = step < STEPS - 1
        out = run_tiles(2, lists, words, own, (side2,), total, current, col_sums, more)
        if more:
            current, own, part = out
        else:
            (current,) = out
    return current.reshape(affiliations.shape)


def solution(mesh):
    torus = Mesh(mesh.devices.reshape(4, 4, 4, 2), ALL)
    return jax.shard_map(
        per_device,
        mesh=torus,
        in_specs=(P(ALL, None), P(ALL, None), P(ALL, None), P(ALL, None), P(ALL), P(), P()),
        out_specs=P(ALL, None),
        check_vma=False,
    )
```

```python
import functools

import jax
import jax.numpy as jnp
from jax import lax
from jax.experimental import pallas as pl
from jax.experimental.pallas import tpu as pltpu
from jax.sharding import Mesh
from jax.sharding import PartitionSpec as P

C = 512
BLOCK = 128
STEPS = 2
BPD = 8
SIDE = 4
CAP = 4
N_COLS = 8
NODES = 131072
UNIT = 1572864
PATTERNS = 192
TILES = 240
GROUP = 2
PARTS = 6
KEYS = PARTS * BPD
GROUPS = (TILES + KEYS * (GROUP - 1)) // GROUP + 2 * PARTS
SLOTS = GROUPS * GROUP
FLOOR = 0.001
STEP_SIZE = 0.3 / NODES
OWN_ROWS = BPD * BLOCK
SENT_ROWS = OWN_ROWS + 16
PICKED = SIDE * CAP

ALL = ("rows_0", "rows_1", "cols_0", "cols_1")
VMEM = pl.BlockSpec(memory_space=pltpu.VMEM)
SMEM = pl.BlockSpec(memory_space=pltpu.SMEM)


def pairs(first, second):
    out = []
    for y in range(SIDE):
        for x in range(SIDE):
            for z in range(4):
                for core in range(2):
                    dx, dy = (first, second) if core == 0 else (second, first)
                    sy, sx = (y + dy) % SIDE, (x + dx) % SIDE
                    out.append((((sy * 4 + sx) * 4 + z) * 2 + core, ((y * 4 + x) * 4 + z) * 2 + core))
    return out


def fetch(value, first, second):
    return lax.ppermute(value, ALL, pairs(first, second))


def sum_over_cols(part):
    for axis, size in (("cols_1", 2), ("cols_0", 4)):
        step = 1
        while step < size:
            part = part + lax.ppermute(part, axis, [(i, i ^ step) for i in range(size)])
            step *= 2
    return part


def plan_kernel(
    place, blocks, targets, pattern_ids, count, home,
    requests, sources, patterns, group_target, part_start,
    rank, fill, tile_source, tile_key, per_key, cursor,
):
    first, second, core = place[0], place[1], place[2]
    live = count[0]

    def clear(ref, size, value):
        def body(i, _):
            ref[i] = value
            return 0

        lax.fori_loop(0, size, body, 0)

    clear(rank, 128, -1)
    clear(fill, 16, 0)
    clear(requests, 64, 0)
    clear(per_key, KEYS, 0)
    clear(sources, SLOTS, 0)
    clear(patterns, SLOTS, PATTERNS)
    clear(group_target, GROUPS, 0)

    def note(t, _):
        slot = home[blocks[t]]
        row = slot // (N_COLS * BPD)
        local = slot & (BPD - 1)
        y, x = row // SIDE, row & (SIDE - 1)
        owner_first = jnp.where(core == 0, x, y)
        owner_second = jnp.where(core == 0, y, x)
        k = (owner_first - first) & (SIDE - 1)
        m = (owner_second - second) & (SIDE - 1)
        pair = m * SIDE + k
        seen = rank[pair * BPD + local]
        held = fill[pair]
        mine = jnp.where(seen < 0, held, seen)
        mine = jnp.minimum(mine, CAP - 1)
        rank[pair * BPD + local] = mine
        fill[pair] = jnp.where(seen < 0, held + 1, held)
        requests[pair * CAP + mine] = local
        tile_source[t] = jnp.where(m == 0, local, k * CAP + mine)
        part = jnp.where(m == 0, jnp.maximum(k, 1) - 1, m + 2)
        key = part * BPD + targets[t]
        tile_key[t] = key
        per_key[key] = per_key[key] + 1
        return 0

    lax.fori_loop(0, live, note, 0)

    base = jnp.int32(0)
    for part in range(PARTS):
        part_start[part] = base
        top = base
        for target in range(BPD):
            key = part * BPD + target
            size = (per_key[key] + GROUP - 1) // GROUP
            cursor[key] = top * GROUP
            top = top + size
        used = top - base
        base = base + jnp.maximum(2, (used + 1) // 2 * 2)
    part_start[PARTS] = base

    def put(t, _):
        key = tile_key[t]
        at = cursor[key]
        cursor[key] = at + 1
        sources[at] = tile_source[t]
        patterns[at] = pattern_ids[t]
        group_target[at // GROUP] = targets[t]
        return 0

    lax.fori_loop(0, live, put, 0)


def make_plan(place, blocks, targets, pattern_ids, count, home):
    i32 = jnp.int32
    return pl.pallas_call(
        plan_kernel,
        out_shape=(
            jax.ShapeDtypeStruct((64,), i32),
            jax.ShapeDtypeStruct((SLOTS,), i32),
            jax.ShapeDtypeStruct((SLOTS,), i32),
            jax.ShapeDtypeStruct((GROUPS,), i32),
            jax.ShapeDtypeStruct((PARTS + 1,), i32),
        ),
        in_specs=[SMEM] * 6,
        out_specs=(SMEM,) * 5,
        scratch_shapes=[
            pltpu.SMEM((128,), i32),
            pltpu.SMEM((16,), i32),
            pltpu.SMEM((TILES,), i32),
            pltpu.SMEM((TILES,), i32),
            pltpu.SMEM((KEYS,), i32),
            pltpu.SMEM((KEYS,), i32),
        ],
        name="plan",
    )(place, blocks, targets, pattern_ids, count, home)


def sum_rows(total):
    high = total.astype(jnp.bfloat16).astype(jnp.float32)
    rest = total - high
    middle = rest.astype(jnp.bfloat16).astype(jnp.float32)
    low = rest - middle
    row = lax.broadcasted_iota(jnp.int32, (16, C), 0)
    out = jnp.where(row == 0, high, jnp.where(row == 1, middle, jnp.where(row == 2, low, 0.0)))
    return out.astype(jnp.bfloat16)


def first_kernel(current, sent):
    total = jnp.zeros((8, C), jnp.float32)
    for j in range(BPD):
        rows = current[pl.ds(j * BLOCK, BLOCK), :]
        sent[pl.ds(j * BLOCK, BLOCK), :] = rows.astype(jnp.bfloat16)
        total = total + jnp.sum(rows.reshape(BLOCK // 8, 8, C), axis=0)
    sent[pl.ds(OWN_ROWS, 16), :] = sum_rows(jnp.sum(total, axis=0, keepdims=True))


def first(current):
    return pl.pallas_call(
        first_kernel,
        out_shape=jax.ShapeDtypeStruct((SENT_ROWS, C), jnp.bfloat16),
        in_specs=[VMEM],
        out_specs=VMEM,
        compiler_params=pltpu.CompilerParams(vmem_limit_bytes=20 << 20),
        name="first",
    )(current)


def pick_kernel(asked, own, far1, far2, far3, out1, out2, out3, sums):
    tables = (own, far1, far2, far3)
    for m, out in enumerate((out1, out2, out3)):
        for k, table in enumerate(tables):
            for r in range(CAP):
                local = pl.multiple_of(asked[m, k * CAP + r] * BLOCK, BLOCK)
                out[pl.ds((k * CAP + r) * BLOCK, BLOCK), :] = table[pl.ds(local, BLOCK), :]
    rows = sum(t[pl.ds(OWN_ROWS, 16), :].astype(jnp.float32) for t in tables)
    sums[...] = jnp.broadcast_to(jnp.sum(rows, axis=0, keepdims=True), (8, C))


def pick(asked, own, far):
    shape = jax.ShapeDtypeStruct((PICKED * BLOCK, C), jnp.bfloat16)
    return pl.pallas_call(
        pick_kernel,
        out_shape=(shape,) * 3 + (jax.ShapeDtypeStruct((8, C), jnp.float32),),
        in_specs=[SMEM] + [VMEM] * 4,
        out_specs=(VMEM,) * 4,
        compiler_params=pltpu.CompilerParams(vmem_limit_bytes=20 << 20),
        name="pick",
    )(asked, own, *far)


def tile_kernel(parts, resume, finish, *refs):
    refs = list(refs)
    sources, pattern_ids, group_target, part_start = refs[:4]
    words, own = refs[4:6]
    tables = refs[6 : 6 + len(parts)]
    refs = refs[6 + len(parts) :]
    if resume:
        earlier = refs.pop(0)
    if finish:
        current, *sums = refs[:5]
        fresh = refs[5]
        refs = refs[6:]
        if finish == "more":
            sent = refs.pop(0)
    total, score_a, score_b, bits = refs

    row = lax.broadcasted_iota(jnp.int32, (BLOCK, BLOCK), 0)
    bits[...] = lax.shift_left(jnp.ones_like(row), lax.rem(row, 30))
    total[...] = earlier[...] if resume else jnp.zeros_like(total)
    sub = lax.broadcasted_iota(jnp.int32, (8, BLOCK), 0)

    def block(ref, index):
        return ref[pl.ds(pl.multiple_of(index * BLOCK, BLOCK), BLOCK), :]

    def word_rows(pattern):
        rows = []
        for v in range(BLOCK // 8):
            low, high = 8 * v // 30, (8 * v + 7) // 30
            chunk = jnp.broadcast_to(words[pattern, low : low + 1, :], (8, BLOCK))
            if high != low:
                other = jnp.broadcast_to(words[pattern, high : high + 1, :], (8, BLOCK))
                chunk = jnp.where(sub + 8 * v < 30 * high, chunk, other)
            rows.append(chunk)
        return jnp.concatenate(rows, axis=0)

    def remote(table, group):
        picked = [block(table, sources[group * GROUP + i]) for i in range(GROUP)]
        return jnp.concatenate(picked, axis=0)

    def score(table, group, out):
        out[...] = lax.dot_general(
            block(own, group_target[group]),
            remote(table, group),
            (((1,), (1,)), ((), ())),
            preferred_element_type=jnp.float32,
        )

    def add(table, group, scores):
        weights = []
        for i in range(GROUP):
            packed = word_rows(pattern_ids[group * GROUP + i])
            negative = jnp.minimum(scores[:, i * BLOCK : (i + 1) * BLOCK] * (-1.0 / UNIT), -FLOOR)
            weight = 1.0 / (1.0 - jnp.exp(negative))
            linked = (packed & bits[...]) != 0
            weights.append(jnp.where(linked, weight, 0.0).astype(jnp.bfloat16))
        at = pl.ds(pl.multiple_of(group_target[group] * BLOCK, BLOCK), BLOCK)
        total[at, :] += jnp.dot(
            jnp.concatenate(weights, axis=1),
            remote(table, group),
            preferred_element_type=jnp.float32,
        )

    for part, table in zip(parts, tables):
        start, stop = part_start[part], part_start[part + 1]
        score(table, start, score_a)

        def two(i, _):
            group = start + 2 * i
            score(table, group + 1, score_b)
            add(table, group, score_a)
            score(table, jnp.minimum(group + 2, stop - 1), score_a)
            add(table, group + 1, score_b)
            return 0

        lax.fori_loop(0, (stop - start) // 2, two, 0)

    if finish:
        col_sums = sum(s[0:1, :] for s in sums)
        moved_sums = jnp.zeros((8, C), jnp.float32)
        for j in range(BPD):
            at = pl.ds(j * BLOCK, BLOCK)
            moved = jnp.maximum(current[at, :] + STEP_SIZE * (total[at, :] - col_sums), 0.0)
            fresh[at, :] = moved
            if finish == "more":
                sent[at, :] = moved.astype(jnp.bfloat16)
                moved_sums = moved_sums + jnp.sum(moved.reshape(BLOCK // 8, 8, C), axis=0)
        if finish == "more":
            sent[pl.ds(OWN_ROWS, 16), :] = sum_rows(jnp.sum(moved_sums, axis=0, keepdims=True))


def run_tiles(name, parts, lists, words, own, tables, earlier=None, current=None, sums=(), finish=""):
    f32 = jnp.float32
    blocks = jax.ShapeDtypeStruct((OWN_ROWS, C), f32)
    args = [*lists, words, own, *tables]
    specs = [SMEM] * 4 + [VMEM] * (2 + len(tables))
    scratch = []
    out = [blocks]
    if earlier is not None:
        args.append(earlier)
        specs.append(VMEM)
    if finish:
        args += [current, *sums]
        specs += [VMEM] * 5
        scratch.append(pltpu.VMEM((OWN_ROWS, C), f32))
        if finish == "more":
            out.append(jax.ShapeDtypeStruct((SENT_ROWS, C), jnp.bfloat16))
    scratch += [
        pltpu.VMEM((BLOCK, GROUP * BLOCK), f32),
        pltpu.VMEM((BLOCK, GROUP * BLOCK), f32),
        pltpu.VMEM((BLOCK, BLOCK), jnp.int32),
    ]
    return pl.pallas_call(
        functools.partial(tile_kernel, parts, earlier is not None, finish),
        out_shape=tuple(out),
        in_specs=specs,
        out_specs=(VMEM,) * len(out),
        scratch_shapes=scratch,
        compiler_params=pltpu.CompilerParams(vmem_limit_bytes=20 << 20),
        name=name,
    )(*args)


def per_device(affiliations, tile_block, tile_target, tile_pattern, tile_count, block_home, patterns):
    y, x = lax.axis_index("rows_0"), lax.axis_index("rows_1")
    core = lax.axis_index("cols_1")
    place = jnp.stack([jnp.where(core == 0, x, y), jnp.where(core == 0, y, x), core])
    current = affiliations
    own = first(current)
    requests, *lists = make_plan(
        place.astype(jnp.int32), tile_block[0], tile_target[0], tile_pattern[0], tile_count, block_home
    )
    requests = requests.reshape(SIDE, PICKED)
    asked = jnp.stack([fetch(requests[m], 0, SIDE - m) for m in (1, 2, 3)])
    words = jnp.concatenate([patterns, jnp.zeros((1, *patterns.shape[1:]), jnp.int32)], axis=0)

    for step in range(STEPS):
        far = tuple(fetch(own, k, 0) for k in (1, 2, 3))
        out1, out2, out3, line_sums = pick(asked, own, far)
        side1, side3, side2 = fetch(out1, 0, 1), fetch(out3, 0, 3), fetch(out2, 0, 2)
        line_sums = sum_over_cols(line_sums)
        sums = (line_sums, *(fetch(line_sums, m, m) for m in (1, 2, 3)))
        (total,) = run_tiles("near", (0, 1, 2), lists, words, own, far)
        (total,) = run_tiles("sides", (3, 5), lists, words, own, (side1, side3), total)
        finish = "more" if step < STEPS - 1 else "end"
        current, *own_next = run_tiles(
            "across", (4,), lists, words, own, (side2,), total, current, sums, finish
        )
        if own_next:
            (own,) = own_next
    return current


def solution(mesh):
    torus = Mesh(mesh.devices.reshape(4, 4, 4, 2), ALL)
    return jax.shard_map(
        per_device,
        mesh=torus,
        in_specs=(P(ALL, None), P(ALL, None), P(ALL, None), P(ALL, None), P(ALL), P(), P()),
        out_specs=P(ALL, None),
        check_vma=False,
    )
```

```python
import functools

import jax
import jax.numpy as jnp
from jax import lax
from jax.experimental import pallas as pl
from jax.experimental.pallas import tpu as pltpu
from jax.sharding import Mesh
from jax.sharding import PartitionSpec as P

C = 512
BLOCK = 128
STEPS = 2
BPD = 8
SIDE = 4
CAP = 4
LINKS = 4
N_COLS = 8
NODES = 131072
UNIT = 1572864
PATTERNS = 192
GROUPS = 136
EMPTY = PATTERNS * BPD
FLOOR = 0.001
STEP_SIZE = 0.3 / NODES
OWN_ROWS = BPD * BLOCK
SENT_ROWS = OWN_ROWS + 16
PICKED = SIDE * CAP
PICKED_ROWS = PICKED * BLOCK

ALL = ("rows_0", "rows_1", "cols_0", "cols_1")
VMEM = pl.BlockSpec(memory_space=pltpu.VMEM)
SMEM = pl.BlockSpec(memory_space=pltpu.SMEM)


def pairs(first, second):
    out = []
    for y in range(SIDE):
        for x in range(SIDE):
            for z in range(4):
                for core in range(2):
                    dx, dy = (first, second) if core == 0 else (second, first)
                    sy, sx = (y + dy) % SIDE, (x + dx) % SIDE
                    out.append((((sy * 4 + sx) * 4 + z) * 2 + core, ((y * 4 + x) * 4 + z) * 2 + core))
    return out


def fetch(value, first, second):
    return lax.ppermute(value, ALL, pairs(first, second))


def sum_over_cols(part):
    for axis, size in (("cols_1", 2), ("cols_0", 4)):
        step = 1
        while step < size:
            part = part + lax.ppermute(part, axis, [(i, i ^ step) for i in range(size)])
            step *= 2
    return part


def plan_kernel(
    place, blocks, targets, pattern_ids, count, home,
    requests, source, left, right, part_start,
    rank, fill, used, entries,
):
    first, second, core = place[0], place[1], place[2]

    def clear(ref, size, value):
        def body(i, _):
            for j in range(8):
                ref[8 * i + j] = value
            return 0

        lax.fori_loop(0, size // 8, body, 0)

    clear(rank, 128, -1)
    clear(fill, 16, 0)
    clear(used, 64, 0)
    clear(requests, 64, 0)

    def note(t, _):
        slot = home[blocks[t]]
        row = slot // (N_COLS * BPD)
        local = slot & (BPD - 1)
        y, x = row // SIDE, row & (SIDE - 1)
        owner_first = jnp.where(core == 0, x, y)
        owner_second = jnp.where(core == 0, y, x)
        k = (owner_first - first) & (SIDE - 1)
        m = (owner_second - second) & (SIDE - 1)
        pair = m * SIDE + k
        seen = rank[pair * BPD + local]
        held = fill[pair]
        mine = jnp.minimum(jnp.where(seen < 0, held, seen), CAP - 1)
        rank[pair * BPD + local] = mine
        fill[pair] = jnp.where(seen < 0, held + 1, held)
        at = pair * CAP + mine
        requests[at] = local
        order = used[at]
        used[at] = order + 1
        entries[at * LINKS + jnp.minimum(order, LINKS - 1)] = pattern_ids[t] * BPD + targets[t]
        return 0

    lax.fori_loop(0, count[0], note, 0)

    def put(group, origin, one, two):
        source[group] = origin
        left[group] = one
        right[group] = two

    group = jnp.int32(0)
    for m in range(SIDE):
        part_start[m] = group
        start = group
        for k in range(SIDE):
            pair = m * SIDE + k
            if pair == 0:
                continue

            def spread(r, group, pair=pair):
                at = pair * CAP + r
                tiles = used[at]
                origin = at % PICKED - (CAP if pair < SIDE else 0)
                base = at * LINKS
                put(group, origin, entries[base], jnp.where(tiles > 1, entries[base + 1], EMPTY))
                put(group + 1, origin, entries[base + 2], jnp.where(tiles > 3, entries[base + 3], EMPTY))
                return group + jnp.where(tiles > 2, 2, 1)

            group = lax.fori_loop(0, jnp.minimum(fill[pair], CAP), spread, group)
        put(group, 0, EMPTY, EMPTY)
        put(group + 1, 0, EMPTY, EMPTY)
        group = start + jnp.maximum(2, (group - start + 1) // 2 * 2)
    part_start[SIDE] = group


def make_plan(place, blocks, targets, pattern_ids, count, home):
    i32 = jnp.int32
    return pl.pallas_call(
        plan_kernel,
        out_shape=(
            jax.ShapeDtypeStruct((64,), i32),
            jax.ShapeDtypeStruct((GROUPS,), i32),
            jax.ShapeDtypeStruct((GROUPS,), i32),
            jax.ShapeDtypeStruct((GROUPS,), i32),
            jax.ShapeDtypeStruct((SIDE + 1,), i32),
        ),
        in_specs=[SMEM] * 6,
        out_specs=(SMEM,) * 5,
        scratch_shapes=[
            pltpu.SMEM((128,), i32),
            pltpu.SMEM((16,), i32),
            pltpu.SMEM((64,), i32),
            pltpu.SMEM((64 * LINKS,), i32),
        ],
        name="plan",
    )(place, blocks, targets, pattern_ids, count, home)


def sum_rows(total):
    high = total.astype(jnp.bfloat16).astype(jnp.float32)
    rest = total - high
    middle = rest.astype(jnp.bfloat16).astype(jnp.float32)
    low = rest - middle
    row = lax.broadcasted_iota(jnp.int32, (16, C), 0)
    out = jnp.where(row == 0, high, jnp.where(row == 1, middle, jnp.where(row == 2, low, 0.0)))
    return out.astype(jnp.bfloat16)


def first_kernel(current, sent):
    total = jnp.zeros((8, C), jnp.float32)
    for j in range(BPD):
        rows = current[pl.ds(j * BLOCK, BLOCK), :]
        sent[pl.ds(j * BLOCK, BLOCK), :] = rows.astype(jnp.bfloat16)
        total = total + jnp.sum(rows.reshape(BLOCK // 8, 8, C), axis=0)
    sent[pl.ds(OWN_ROWS, 16), :] = sum_rows(jnp.sum(total, axis=0, keepdims=True))


def first(current):
    return pl.pallas_call(
        first_kernel,
        out_shape=jax.ShapeDtypeStruct((SENT_ROWS, C), jnp.bfloat16),
        in_specs=[VMEM],
        out_specs=VMEM,
        compiler_params=pltpu.CompilerParams(vmem_limit_bytes=20 << 20),
        name="first",
    )(current)


def pick_kernel(asked, wanted, line, own, far1, far2, far3, near, out1, out2, out3):
    tables = (own, far1, far2, far3)

    def move(table, local, out, at):
        rows = pl.ds(pl.multiple_of(local * BLOCK, BLOCK), BLOCK)
        out[pl.ds(at * BLOCK, BLOCK), :] = table[rows, :]

    for m, out in enumerate((out1, out2, out3)):
        for k, table in enumerate(tables):
            for r in range(CAP):
                move(table, asked[m, k * CAP + r], out, k * CAP + r)
    for k in (1, 2, 3):
        for r in range(CAP):
            move(tables[k], wanted[k * CAP + r], near, (k - 1) * CAP + r)
    for out in (out1, out3):
        out[pl.ds(PICKED_ROWS, 16), :] = sum_rows(line[0:1, :])


def pick(asked, wanted, line, own, far):
    b16 = jnp.bfloat16
    with_sums = jax.ShapeDtypeStruct((PICKED_ROWS + 16, C), b16)
    return pl.pallas_call(
        pick_kernel,
        out_shape=(
            jax.ShapeDtypeStruct((3 * CAP * BLOCK, C), b16),
            with_sums,
            jax.ShapeDtypeStruct((PICKED_ROWS, C), b16),
            with_sums,
        ),
        in_specs=[SMEM] * 2 + [VMEM] * 5,
        out_specs=(VMEM,) * 4,
        compiler_params=pltpu.CompilerParams(vmem_limit_bytes=20 << 20),
        name="pick",
    )(asked, wanted, line, own, *far)


def tile_kernel(parts, resume, finish, *refs):
    refs = list(refs)
    source, left, right, part_start, words, own = refs[:6]
    tables = refs[6 : 6 + len(parts)]
    refs = refs[6 + len(parts) :]
    if resume:
        earlier = refs.pop(0)
    if finish:
        current, all_sums, fresh = refs[:3]
        refs = refs[3:]
        if finish == "more":
            sent = refs.pop(0)
    total, score_a, score_b, bits = refs

    row = lax.broadcasted_iota(jnp.int32, (BLOCK, BLOCK), 0)
    bits[...] = lax.shift_left(jnp.ones_like(row), lax.rem(row, 30))
    total[...] = earlier[...] if resume else jnp.zeros_like(total)
    sub = lax.broadcasted_iota(jnp.int32, (8, BLOCK), 0)

    def rows_of(index):
        return pl.ds(pl.multiple_of(index * BLOCK, BLOCK), BLOCK)

    def target(entry):
        return rows_of(entry & (BPD - 1))

    def word_rows(pattern):
        rows = []
        for v in range(BLOCK // 8):
            low, high = 8 * v // 30, (8 * v + 7) // 30
            chunk = jnp.broadcast_to(words[pattern, low : low + 1, :], (8, BLOCK))
            if high != low:
                other = jnp.broadcast_to(words[pattern, high : high + 1, :], (8, BLOCK))
                chunk = jnp.where(sub + 8 * v < 30 * high, chunk, other)
            rows.append(chunk)
        return jnp.concatenate(rows, axis=0)

    def score(table, group, out):
        mine = jnp.concatenate([own[target(e[group]), :] for e in (left, right)], axis=0)
        out[...] = lax.dot_general(
            mine,
            table[rows_of(source[group]), :],
            (((1,), (1,)), ((), ())),
            preferred_element_type=jnp.float32,
        )

    def add(table, group, scores):
        weights = []
        for i, e in enumerate((left, right)):
            packed = word_rows(e[group] // BPD)
            negative = jnp.minimum(scores[i * BLOCK : (i + 1) * BLOCK, :] * (-1.0 / UNIT), -FLOOR)
            weight = 1.0 / (1.0 - jnp.exp(negative))
            linked = (packed & bits[...]) != 0
            weights.append(jnp.where(linked, weight, 0.0).astype(jnp.bfloat16))
        both = jnp.dot(
            jnp.concatenate(weights, axis=0),
            table[rows_of(source[group]), :],
            preferred_element_type=jnp.float32,
        )
        for i, e in enumerate((left, right)):
            total[target(e[group]), :] += both[i * BLOCK : (i + 1) * BLOCK, :]

    for part, table in zip(parts, tables):
        start, stop = part_start[part], part_start[part + 1]
        score(table, start, score_a)

        def two(i, _):
            group = start + 2 * i
            score(table, group + 1, score_b)
            add(table, group, score_a)
            score(table, jnp.minimum(group + 2, stop - 1), score_a)
            add(table, group + 1, score_b)
            return 0

        lax.fori_loop(0, (stop - start) // 2, two, 0)

    if finish:
        col_sums = all_sums[0:1, :]
        moved_sums = jnp.zeros((8, C), jnp.float32)
        for j in range(BPD):
            at = pl.ds(j * BLOCK, BLOCK)
            moved = jnp.maximum(current[at, :] + STEP_SIZE * (total[at, :] - col_sums), 0.0)
            fresh[at, :] = moved
            if finish == "more":
                sent[at, :] = moved.astype(jnp.bfloat16)
                moved_sums = moved_sums + jnp.sum(moved.reshape(BLOCK // 8, 8, C), axis=0)
        if finish == "more":
            sent[pl.ds(OWN_ROWS, 16), :] = sum_rows(jnp.sum(moved_sums, axis=0, keepdims=True))


def run_tiles(name, parts, lists, words, own, tables, earlier=None, current=None, sums=None, finish=""):
    f32 = jnp.float32
    blocks = jax.ShapeDtypeStruct((OWN_ROWS, C), f32)
    args = [*lists, words, own, *tables]
    specs = [SMEM] * 4 + [VMEM] * (2 + len(tables))
    scratch = []
    out = [blocks]
    if earlier is not None:
        args.append(earlier)
        specs.append(VMEM)
    if finish:
        args += [current, sums]
        specs += [VMEM] * 2
        scratch.append(pltpu.VMEM((OWN_ROWS, C), f32))
        if finish == "more":
            out.append(jax.ShapeDtypeStruct((SENT_ROWS, C), jnp.bfloat16))
    scratch += [
        pltpu.VMEM((2 * BLOCK, BLOCK), f32),
        pltpu.VMEM((2 * BLOCK, BLOCK), f32),
        pltpu.VMEM((BLOCK, BLOCK), jnp.int32),
    ]
    return pl.pallas_call(
        functools.partial(tile_kernel, parts, earlier is not None, finish),
        out_shape=tuple(out),
        in_specs=specs,
        out_specs=(VMEM,) * len(out),
        scratch_shapes=scratch,
        compiler_params=pltpu.CompilerParams(vmem_limit_bytes=20 << 20),
        name=name,
    )(*args)


def payload(tables, at):
    rows = sum(t[at:].astype(jnp.float32) for t in tables)
    return jnp.broadcast_to(jnp.sum(rows, axis=0, keepdims=True), (8, C))


def per_device(affiliations, tile_block, tile_target, tile_pattern, tile_count, block_home, patterns):
    y, x = lax.axis_index("rows_0"), lax.axis_index("rows_1")
    core = lax.axis_index("cols_1")
    place = jnp.stack([jnp.where(core == 0, x, y), jnp.where(core == 0, y, x), core])
    current = affiliations
    own = first(current)
    requests, *lists = make_plan(
        place.astype(jnp.int32), tile_block[0], tile_target[0], tile_pattern[0], tile_count, block_home
    )
    requests = requests.reshape(SIDE, PICKED)
    asked = jnp.stack([fetch(requests[m], 0, SIDE - m) for m in (1, 2, 3)])
    words = jnp.concatenate([patterns, jnp.zeros((1, *patterns.shape[1:]), jnp.int32)], axis=0)

    for step in range(STEPS):
        far = tuple(fetch(own, k, 0) for k in (1, 2, 3))
        line = payload((own, *far), OWN_ROWS)
        line_across = fetch(line, 0, 2)
        near, out1, out2, out3 = pick(asked, requests[0], line, own, far)
        out2, line_across = lax.optimization_barrier((out2, line_across))
        side1, side3, side2 = fetch(out1, 0, 1), fetch(out3, 0, 3), fetch(out2, 0, 2)
        (total,) = run_tiles("near", (0,), lists, words, own, (near,))
        total, side1, side3 = lax.optimization_barrier((total, side1, side3))
        plane = line + line_across + payload((side1, side3), PICKED_ROWS)
        col_sums = sum_over_cols(plane)
        (total,) = run_tiles("sides", (1, 3), lists, words, own, (side1, side3), total)
        finish = "more" if step < STEPS - 1 else "end"
        current, *own_next = run_tiles(
            "across", (2,), lists, words, own, (side2,), total, current, col_sums, finish
        )
        if own_next:
            (own,) = own_next
    return current


def solution(mesh):
    torus = Mesh(mesh.devices.reshape(4, 4, 4, 2), ALL)
    return jax.shard_map(
        per_device,
        mesh=torus,
        in_specs=(P(ALL, None), P(ALL, None), P(ALL, None), P(ALL, None), P(ALL), P(), P()),
        out_specs=P(ALL, None),
        check_vma=False,
    )
```

```python
import functools

import jax
import jax.numpy as jnp
from jax import lax
from jax.experimental import pallas as pl
from jax.experimental.pallas import tpu as pltpu
from jax.sharding import Mesh
from jax.sharding import PartitionSpec as P

C = 512
BLOCK = 128
STEPS = 2
BPD = 8
SIDE = 4
CAP = 4
LINKS = 4
N_COLS = 8
NODES = 131072
UNIT = 1572864
PATTERNS = 192
PARTS = 7
GROUPS = 144
EMPTY = PATTERNS * BPD
FLOOR = 0.001
STEP_SIZE = 0.3 / NODES
OWN_ROWS = BPD * BLOCK
SENT_ROWS = OWN_ROWS + 16
PICKED = SIDE * CAP
HALF_ROWS = OWN_ROWS // 2

ALL = ("rows_0", "rows_1", "cols_0", "cols_1")
VMEM = pl.BlockSpec(memory_space=pltpu.VMEM)
SMEM = pl.BlockSpec(memory_space=pltpu.SMEM)


def pairs(first, second):
    out = []
    for y in range(SIDE):
        for x in range(SIDE):
            for z in range(4):
                for core in range(2):
                    dx, dy = (first, second) if core == 0 else (second, first)
                    sy, sx = (y + dy) % SIDE, (x + dx) % SIDE
                    out.append((((sy * 4 + sx) * 4 + z) * 2 + core, ((y * 4 + x) * 4 + z) * 2 + core))
    return out


def fetch(value, first, second):
    return lax.ppermute(value, ALL, pairs(first, second))


def sum_over_cols(part):
    for axis, size in (("cols_1", 2), ("cols_0", 4)):
        step = 1
        while step < size:
            part = part + lax.ppermute(part, axis, [(i, i ^ step) for i in range(size)])
            step *= 2
    return part


OWNERS = (
    ((0, 1), (0, 3)),
    ((1, 0), (1, 1), (1, 3)),
    ((3, 0), (3, 1), (3, 3)),
    ((1, 2),),
    ((3, 2),),
    ((0, 2),),
    ((2, 0), (2, 1), (2, 3), (2, 2)),
)


def plan_kernel(
    place, blocks, targets, pattern_ids, count, home,
    requests, source, left, right, part_start,
    rank, fill, used, entries,
):
    first, second, core = place[0], place[1], place[2]

    def clear(ref, size, value):
        def body(i, _):
            for j in range(8):
                ref[8 * i + j] = value
            return 0

        lax.fori_loop(0, size // 8, body, 0)

    clear(rank, 128, -1)
    clear(fill, 16, 0)
    clear(used, 64, 0)
    clear(requests, 64, 0)

    def note(t, _):
        slot = home[blocks[t]]
        row = slot >> 6
        local = slot & (BPD - 1)
        y, x = row >> 2, row & (SIDE - 1)
        owner_first = jnp.where(core == 0, x, y)
        owner_second = jnp.where(core == 0, y, x)
        k = (owner_first - first) & (SIDE - 1)
        m = (owner_second - second) & (SIDE - 1)
        pair = m * SIDE + k
        seen = rank[pair * BPD + local]
        held = fill[pair]
        mine = jnp.minimum(jnp.where(seen < 0, held, seen), CAP - 1)
        rank[pair * BPD + local] = mine
        fill[pair] = jnp.where(seen < 0, held + 1, held)
        at = pair * CAP + mine
        requests[at] = local
        order = used[at]
        used[at] = order + 1
        entries[at * LINKS + jnp.minimum(order, LINKS - 1)] = pattern_ids[t] * BPD + targets[t]
        return 0

    lax.fori_loop(0, count[0], note, 0)

    def put(group, origin, one, two):
        source[group] = origin
        left[group] = one
        right[group] = two

    group = jnp.int32(0)
    for part, owners in enumerate(OWNERS):
        part_start[part] = group
        start = group
        for place_in_table, (m, k) in enumerate(owners):
            pair = m * SIDE + k

            def spread(r, group, pair=pair, origin=place_in_table * CAP):
                at = pair * CAP + r
                tiles = used[at]
                base = at * LINKS
                put(group, origin + r, entries[base], jnp.where(tiles > 1, entries[base + 1], EMPTY))
                put(
                    group + 1,
                    origin + r,
                    entries[base + 2],
                    jnp.where(tiles > 3, entries[base + 3], EMPTY),
                )
                return group + jnp.where(tiles > 2, 2, 1)

            group = lax.fori_loop(0, jnp.minimum(fill[pair], CAP), spread, group)
        put(group, 0, EMPTY, EMPTY)
        put(group + 1, 0, EMPTY, EMPTY)
        group = start + jnp.maximum(2, (group - start + 1) & -2)
    part_start[PARTS] = group


def make_plan(place, blocks, targets, pattern_ids, count, home):
    i32 = jnp.int32
    return pl.pallas_call(
        plan_kernel,
        out_shape=(
            jax.ShapeDtypeStruct((64,), i32),
            jax.ShapeDtypeStruct((GROUPS,), i32),
            jax.ShapeDtypeStruct((GROUPS,), i32),
            jax.ShapeDtypeStruct((GROUPS,), i32),
            jax.ShapeDtypeStruct((PARTS + 1,), i32),
        ),
        in_specs=[SMEM] * 6,
        out_specs=(SMEM,) * 5,
        scratch_shapes=[
            pltpu.SMEM((128,), i32),
            pltpu.SMEM((16,), i32),
            pltpu.SMEM((64,), i32),
            pltpu.SMEM((64 * LINKS,), i32),
        ],
        name="plan",
    )(place, blocks, targets, pattern_ids, count, home)


def sum_rows(total):
    high = total.astype(jnp.bfloat16).astype(jnp.float32)
    rest = total - high
    middle = rest.astype(jnp.bfloat16).astype(jnp.float32)
    low = rest - middle
    row = lax.broadcasted_iota(jnp.int32, (16, C), 0)
    out = jnp.where(row == 0, high, jnp.where(row == 1, middle, jnp.where(row == 2, low, 0.0)))
    return out.astype(jnp.bfloat16)


def first_kernel(current, sent):
    total = jnp.zeros((8, C), jnp.float32)
    for j in range(BPD):
        rows = current[pl.ds(j * BLOCK, BLOCK), :]
        sent[pl.ds(j * BLOCK, BLOCK), :] = rows.astype(jnp.bfloat16)
        total = total + jnp.sum(rows.reshape(BLOCK // 8, 8, C), axis=0)
    sent[pl.ds(OWN_ROWS, 16), :] = sum_rows(jnp.sum(total, axis=0, keepdims=True))


def first(current):
    return pl.pallas_call(
        first_kernel,
        out_shape=jax.ShapeDtypeStruct((SENT_ROWS, C), jnp.bfloat16),
        in_specs=[VMEM],
        out_specs=VMEM,
        compiler_params=pltpu.CompilerParams(vmem_limit_bytes=20 << 20),
        name="first",
    )(current)


def move(table, local, out, at):
    rows = pl.ds(pl.multiple_of(local * BLOCK, BLOCK), BLOCK)
    out[pl.ds(at * BLOCK, BLOCK), :] = table[rows, :]


def pick_early_kernel(asked, wanted, own, far1, far3, near, pass1, pass3, out1, out3):
    pass1[...] = far1[pl.ds(0, HALF_ROWS), :]
    pass3[...] = far3[pl.ds(HALF_ROWS, HALF_ROWS + 16), :]
    for m, out in ((1, out1), (3, out3)):
        for i, (k, table) in enumerate(((0, own), (1, far1), (3, far3))):
            for r in range(CAP):
                move(table, asked[m - 1, k * CAP + r], out, i * CAP + r)
    for r in range(CAP):
        move(far1, wanted[CAP + r], near, r)
        move(far3, wanted[3 * CAP + r], near, CAP + r)


def pick_early(asked, wanted, own, far1, far3):
    b16 = jnp.bfloat16
    out = jax.ShapeDtypeStruct((3 * CAP * BLOCK, C), b16)
    return pl.pallas_call(
        pick_early_kernel,
        out_shape=(
            jax.ShapeDtypeStruct((2 * CAP * BLOCK, C), b16),
            jax.ShapeDtypeStruct((HALF_ROWS, C), b16),
            jax.ShapeDtypeStruct((HALF_ROWS + 16, C), b16),
            out,
            out,
        ),
        in_specs=[SMEM] * 2 + [VMEM] * 3,
        out_specs=(VMEM,) * 5,
        compiler_params=pltpu.CompilerParams(vmem_limit_bytes=20 << 20),
        name="pick_early",
    )(asked, wanted, own, far1, far3)


def pick_late_kernel(asked, wanted, own, far1, far3, low2, high2, near, out1, out3, out2, line, far2):
    far2[pl.ds(0, HALF_ROWS), :] = low2[...]
    far2[pl.ds(HALF_ROWS, HALF_ROWS + 16), :] = high2[...]
    tables = ((0, own), (1, far1), (3, far3), (2, far2))
    for r in range(CAP):
        move(far2, asked[0, 2 * CAP + r], out1, r)
        move(far2, asked[2, 2 * CAP + r], out3, r)
        move(far2, wanted[2 * CAP + r], near, r)
    for i, (k, table) in enumerate(tables):
        for r in range(CAP):
            move(table, asked[1, k * CAP + r], out2, i * CAP + r)
    rows = sum(t[pl.ds(OWN_ROWS, 16), :].astype(jnp.float32) for _, t in tables)
    sums = jnp.sum(rows, axis=0, keepdims=True)
    line[...] = jnp.broadcast_to(sums, (8, C))


def pick_late(asked, wanted, own, far1, far3, low2, high2):
    b16 = jnp.bfloat16
    piece = jax.ShapeDtypeStruct((CAP * BLOCK, C), b16)
    return pl.pallas_call(
        pick_late_kernel,
        out_shape=(
            piece,
            piece,
            piece,
            jax.ShapeDtypeStruct((PICKED * BLOCK, C), b16),
            jax.ShapeDtypeStruct((8, C), jnp.float32),
        ),
        in_specs=[SMEM] * 2 + [VMEM] * 5,
        out_specs=(VMEM,) * 5,
        scratch_shapes=[pltpu.VMEM((SENT_ROWS, C), b16)],
        compiler_params=pltpu.CompilerParams(vmem_limit_bytes=20 << 20),
        name="pick_late",
    )(asked, wanted, own, far1, far3, low2, high2)


def tile_kernel(parts, resume, finish, *refs):
    refs = list(refs)
    source, left, right, part_start, words, own = refs[:6]
    tables = refs[6 : 6 + len(parts)]
    refs = refs[6 + len(parts) :]
    if resume:
        earlier = refs.pop(0)
    if finish:
        current, all_sums, fresh = refs[:3]
        refs = refs[3:]
        if finish == "more":
            sent = refs.pop(0)
    total, score_a, score_b, bits = refs

    row = lax.broadcasted_iota(jnp.int32, (BLOCK, BLOCK), 0)
    bits[...] = lax.shift_left(jnp.ones_like(row), lax.rem(row, 30))
    total[...] = earlier[...] if resume else jnp.zeros_like(total)
    sub = lax.broadcasted_iota(jnp.int32, (8, BLOCK), 0)

    def rows_of(index):
        return pl.ds(pl.multiple_of(index * BLOCK, BLOCK), BLOCK)

    def target(entry):
        return rows_of(entry & (BPD - 1))

    def word_rows(pattern):
        rows = []
        for v in range(BLOCK // 8):
            low, high = 8 * v // 30, (8 * v + 7) // 30
            chunk = jnp.broadcast_to(words[pattern, low : low + 1, :], (8, BLOCK))
            if high != low:
                other = jnp.broadcast_to(words[pattern, high : high + 1, :], (8, BLOCK))
                chunk = jnp.where(sub + 8 * v < 30 * high, chunk, other)
            rows.append(chunk)
        return jnp.concatenate(rows, axis=0)

    def score(table, group, out):
        mine = jnp.concatenate([own[target(e[group]), :] for e in (left, right)], axis=0)
        out[...] = lax.dot_general(
            mine,
            table[rows_of(source[group]), :],
            (((1,), (1,)), ((), ())),
            preferred_element_type=jnp.float32,
        )

    def add(table, group, scores):
        weights = []
        for i, e in enumerate((left, right)):
            packed = word_rows(e[group] >> 3)
            negative = jnp.minimum(scores[i * BLOCK : (i + 1) * BLOCK, :] * (-1.0 / UNIT), -FLOOR)
            weight = 1.0 / (1.0 - jnp.exp(negative))
            linked = (packed & bits[...]) != 0
            weights.append(jnp.where(linked, weight, 0.0).astype(jnp.bfloat16))
        both = jnp.dot(
            jnp.concatenate(weights, axis=0),
            table[rows_of(source[group]), :],
            preferred_element_type=jnp.float32,
        )
        for i, e in enumerate((left, right)):
            total[target(e[group]), :] += both[i * BLOCK : (i + 1) * BLOCK, :]

    for part, table in zip(parts, tables):
        start, stop = part_start[part], part_start[part + 1]
        score(table, start, score_a)

        def two(i, _):
            group = start + 2 * i
            score(table, group + 1, score_b)
            add(table, group, score_a)
            score(table, jnp.minimum(group + 2, stop - 1), score_a)
            add(table, group + 1, score_b)
            return 0

        lax.fori_loop(0, (stop - start) >> 1, two, 0)

    if finish:
        col_sums = all_sums[0:1, :]
        moved_sums = jnp.zeros((8, C), jnp.float32)
        for j in range(BPD):
            at = pl.ds(j * BLOCK, BLOCK)
            moved = jnp.maximum(current[at, :] + STEP_SIZE * (total[at, :] - col_sums), 0.0)
            fresh[at, :] = moved
            if finish == "more":
                sent[at, :] = moved.astype(jnp.bfloat16)
                moved_sums = moved_sums + jnp.sum(moved.reshape(BLOCK // 8, 8, C), axis=0)
        if finish == "more":
            sent[pl.ds(OWN_ROWS, 16), :] = sum_rows(jnp.sum(moved_sums, axis=0, keepdims=True))


def run_tiles(name, parts, lists, words, own, tables, earlier=None, current=None, sums=None, finish=""):
    f32 = jnp.float32
    blocks = jax.ShapeDtypeStruct((OWN_ROWS, C), f32)
    args = [*lists, words, own, *tables]
    specs = [SMEM] * 4 + [VMEM] * (2 + len(tables))
    scratch = []
    out = [blocks]
    if earlier is not None:
        args.append(earlier)
        specs.append(VMEM)
    if finish:
        args += [current, sums]
        specs += [VMEM] * 2
        scratch.append(pltpu.VMEM((OWN_ROWS, C), f32))
        if finish == "more":
            out.append(jax.ShapeDtypeStruct((SENT_ROWS, C), jnp.bfloat16))
    scratch += [
        pltpu.VMEM((2 * BLOCK, BLOCK), f32),
        pltpu.VMEM((2 * BLOCK, BLOCK), f32),
        pltpu.VMEM((BLOCK, BLOCK), jnp.int32),
    ]
    return pl.pallas_call(
        functools.partial(tile_kernel, parts, earlier is not None, finish),
        out_shape=tuple(out),
        in_specs=specs,
        out_specs=(VMEM,) * len(out),
        scratch_shapes=scratch,
        compiler_params=pltpu.CompilerParams(vmem_limit_bytes=20 << 20),
        name=name,
    )(*args)


def per_device(affiliations, tile_block, tile_target, tile_pattern, tile_count, block_home, patterns):
    y, x = lax.axis_index("rows_0"), lax.axis_index("rows_1")
    core = lax.axis_index("cols_1")
    place = jnp.stack([jnp.where(core == 0, x, y), jnp.where(core == 0, y, x), core])
    current = affiliations
    own = first(current)
    requests, *lists = make_plan(
        place.astype(jnp.int32), tile_block[0], tile_target[0], tile_pattern[0], tile_count, block_home
    )
    requests = requests.reshape(SIDE, PICKED)
    asked = jnp.stack([fetch(requests[m], 0, SIDE - m) for m in (1, 2, 3)])
    words = jnp.concatenate([patterns, jnp.zeros((1, *patterns.shape[1:]), jnp.int32)], axis=0)

    for step in range(STEPS):
        far1, far3 = fetch(own, 1, 0), fetch(own, 3, 0)
        near, pass1, pass3, out1, out3 = pick_early(asked, requests[0], own, far1, far3)
        low2, high2 = fetch(pass1, 1, 0), fetch(pass3, 3, 0)
        side1, side3 = fetch(out1, 0, 1), fetch(out3, 0, 3)
        (total,) = run_tiles("near", (0,), lists, words, own, (near,))
        total, low2, high2 = lax.optimization_barrier((total, low2, high2))
        near, out1, out3, out2, line = pick_late(asked, requests[0], own, far1, far3, low2, high2)
        lines = tuple(fetch(line, 0, m) for m in (1, 3, 2))
        lines, out2, side1, side3 = lax.optimization_barrier((lines, out2, side1, side3))
        side2 = fetch(out2, 0, 2)
        late1, late3 = fetch(out1, 0, 1), fetch(out3, 0, 3)
        col_sums = sum_over_cols(line + lines[0] + lines[1] + lines[2])
        tables = (side1, side3, near)
        (total,) = run_tiles("sides", (1, 2, 5), lists, words, own, tables, total)
        (total,) = run_tiles("across", (6,), lists, words, own, (side2,), total)
        total, late1, late3 = lax.optimization_barrier((total, late1, late3))
        finish = "more" if step < STEPS - 1 else "end"
        current, *own_next = run_tiles(
            "late", (3, 4), lists, words, own, (late1, late3), total, current, col_sums, finish
        )
        if own_next:
            (own,) = own_next
    return current


def solution(mesh):
    torus = Mesh(mesh.devices.reshape(4, 4, 4, 2), ALL)
    return jax.shard_map(
        per_device,
        mesh=torus,
        in_specs=(P(ALL, None), P(ALL, None), P(ALL, None), P(ALL, None), P(ALL), P(), P()),
        out_specs=P(ALL, None),
        check_vma=False,
    )
```

```python
import functools

import jax
import jax.numpy as jnp
from jax import lax
from jax.experimental import pallas as pl
from jax.experimental.pallas import tpu as pltpu
from jax.sharding import Mesh
from jax.sharding import PartitionSpec as P

C = 512
BLOCK = 128
STEPS = 2
BPD = 8
SIDE = 4
CAP = 4
N_COLS = 8
NODES = 131072
UNIT = 1572864
PATTERNS = 192
TILES = 240
GROUP = 4
PARTS = 3
KEYS = PARTS * BPD
GROUPS = (TILES + KEYS * (GROUP - 1)) // GROUP + 2 * PARTS + 2
SLOTS = GROUPS * GROUP
EMPTY = PATTERNS * 64
FLOOR = 0.001
STEP_SIZE = 0.3 / NODES
OWN_ROWS = BPD * BLOCK
SENT_ROWS = OWN_ROWS + 16
PICKED = SIDE * CAP
HALF_ROWS = OWN_ROWS // 2

ALL = ("rows_0", "rows_1", "cols_0", "cols_1")
VMEM = pl.BlockSpec(memory_space=pltpu.VMEM)
SMEM = pl.BlockSpec(memory_space=pltpu.SMEM)


def pairs(first, second):
    out = []
    for y in range(SIDE):
        for x in range(SIDE):
            for z in range(4):
                for core in range(2):
                    dx, dy = (first, second) if core == 0 else (second, first)
                    sy, sx = (y + dy) % SIDE, (x + dx) % SIDE
                    out.append((((sy * 4 + sx) * 4 + z) * 2 + core, ((y * 4 + x) * 4 + z) * 2 + core))
    return out


def fetch(value, first, second):
    return lax.ppermute(value, ALL, pairs(first, second))


def sum_over_cols(part):
    for axis, size in (("cols_1", 2), ("cols_0", 4)):
        step = 1
        while step < size:
            part = part + lax.ppermute(part, axis, [(i, i ^ step) for i in range(size)])
            step *= 2
    return part


OWNERS = (
    ((1, 0), (1, 1), (1, 3), (3, 0), (3, 1), (3, 3), (0, 1), (0, 3), (0, 2)),
    ((2, 0), (2, 1), (2, 3), (2, 2)),
    ((1, 2), (3, 2)),
)


def clear(ref, size, value):
    def body(i, _):
        for j in range(8):
            ref[8 * i + j] = value
        return 0

    lax.fori_loop(0, size // 8, body, 0)


def ask_kernel(place, blocks, targets, count, home, requests, codes, rank, fill, base):
    first, second, core = place[0], place[1], place[2]
    clear(rank, 128, -1)
    clear(fill, 16, 0)
    clear(requests, 64, 0)
    base[0] = 0
    for part, owners in enumerate(OWNERS):
        for i, (m, k) in enumerate(owners):
            base[m * SIDE + k] = part * 512 + i * CAP

    def note(t, _):
        slot = home[blocks[t]]
        row = slot >> 6
        local = slot & (BPD - 1)
        y, x = row >> 2, row & (SIDE - 1)
        owner_first = jnp.where(core == 0, x, y)
        owner_second = jnp.where(core == 0, y, x)
        k = (owner_first - first) & (SIDE - 1)
        m = (owner_second - second) & (SIDE - 1)
        pair = m * SIDE + k
        seen = rank[pair * BPD + local]
        held = fill[pair]
        mine = jnp.minimum(jnp.where(seen < 0, held, seen), CAP - 1)
        rank[pair * BPD + local] = mine
        fill[pair] = jnp.where(seen < 0, held + 1, held)
        requests[pair * CAP + mine] = local
        codes[t] = base[pair] + mine + targets[t] * 64
        return 0

    lax.fori_loop(0, count[0], note, 0)


def ask(place, blocks, targets, count, home):
    i32 = jnp.int32
    return pl.pallas_call(
        ask_kernel,
        out_shape=(jax.ShapeDtypeStruct((64,), i32), jax.ShapeDtypeStruct((TILES,), i32)),
        in_specs=[SMEM] * 5,
        out_specs=(SMEM,) * 2,
        scratch_shapes=[pltpu.SMEM((128,), i32), pltpu.SMEM((16,), i32), pltpu.SMEM((16,), i32)],
        compiler_params=pltpu.CompilerParams(vmem_limit_bytes=2 << 20),
        name="ask",
    )(place, blocks, targets, count, home)


def sort_kernel(codes, pattern_ids, count, slots, group_target, part_start, per_key):
    clear(per_key, KEYS, 0)
    clear(slots, SLOTS, EMPTY)
    clear(group_target, GROUPS, 0)

    def tally(t, _):
        key = codes[t] >> 6
        per_key[key] = per_key[key] + 1
        return 0

    lax.fori_loop(0, count[0], tally, 0)
    group = jnp.int32(0)
    for part in range(PARTS):
        part_start[part] = group
        start = group
        for target in range(BPD):
            key = part * BPD + target
            size = (per_key[key] + GROUP - 1) >> 2
            per_key[key] = group * GROUP
            group = group + size
        group = start + jnp.maximum(2, (group - start + 1) & -2)
    part_start[PARTS] = group

    def put(t, _):
        code = codes[t]
        key = code >> 6
        at = per_key[key]
        per_key[key] = at + 1
        slots[at] = pattern_ids[t] * 64 + (code & 63)
        group_target[at >> 2] = key & (BPD - 1)
        return 0

    lax.fori_loop(0, count[0], put, 0)


def sort_tiles(codes, pattern_ids, count):
    i32 = jnp.int32
    return pl.pallas_call(
        sort_kernel,
        out_shape=(
            jax.ShapeDtypeStruct((SLOTS,), i32),
            jax.ShapeDtypeStruct((GROUPS,), i32),
            jax.ShapeDtypeStruct((PARTS + 1,), i32),
        ),
        in_specs=[SMEM] * 3,
        out_specs=(SMEM,) * 3,
        scratch_shapes=[pltpu.SMEM((KEYS,), i32)],
        compiler_params=pltpu.CompilerParams(vmem_limit_bytes=2 << 20),
        name="sort_tiles",
    )(codes, pattern_ids, count)


def sum_rows(total):
    high = total.astype(jnp.bfloat16).astype(jnp.float32)
    rest = total - high
    middle = rest.astype(jnp.bfloat16).astype(jnp.float32)
    low = rest - middle
    row = lax.broadcasted_iota(jnp.int32, (16, C), 0)
    out = jnp.where(row == 0, high, jnp.where(row == 1, middle, jnp.where(row == 2, low, 0.0)))
    return out.astype(jnp.bfloat16)


def first_kernel(current, sent):
    total = jnp.zeros((8, C), jnp.float32)
    for j in range(BPD):
        rows = current[pl.ds(j * BLOCK, BLOCK), :]
        sent[pl.ds(j * BLOCK, BLOCK), :] = rows.astype(jnp.bfloat16)
        total = total + jnp.sum(rows.reshape(BLOCK // 8, 8, C), axis=0)
    sent[pl.ds(OWN_ROWS, 16), :] = sum_rows(jnp.sum(total, axis=0, keepdims=True))


def first(current):
    return pl.pallas_call(
        first_kernel,
        out_shape=jax.ShapeDtypeStruct((SENT_ROWS, C), jnp.bfloat16),
        in_specs=[VMEM],
        out_specs=VMEM,
        compiler_params=pltpu.CompilerParams(vmem_limit_bytes=20 << 20),
        name="first",
    )(current)


def move(table, local, out, at):
    rows = pl.ds(pl.multiple_of(local * BLOCK, BLOCK), BLOCK)
    out[pl.ds(at * BLOCK, BLOCK), :] = table[rows, :]


def pick_early_kernel(asked, wanted, own, far1, far3, near, pass1, pass3, out1, out3):
    pass1[...] = far1[pl.ds(0, HALF_ROWS), :]
    pass3[...] = far3[pl.ds(HALF_ROWS, HALF_ROWS + 16), :]
    for m, out in ((1, out1), (3, out3)):
        for i, (k, table) in enumerate(((0, own), (1, far1), (3, far3))):
            for r in range(CAP):
                move(table, asked[m - 1, k * CAP + r], out, i * CAP + r)
    for r in range(CAP):
        move(far1, wanted[CAP + r], near, r)
        move(far3, wanted[3 * CAP + r], near, CAP + r)


def pick_early(asked, wanted, own, far1, far3):
    b16 = jnp.bfloat16
    out = jax.ShapeDtypeStruct((3 * CAP * BLOCK, C), b16)
    return pl.pallas_call(
        pick_early_kernel,
        out_shape=(
            jax.ShapeDtypeStruct((2 * CAP * BLOCK, C), b16),
            jax.ShapeDtypeStruct((HALF_ROWS, C), b16),
            jax.ShapeDtypeStruct((HALF_ROWS + 16, C), b16),
            out,
            out,
        ),
        in_specs=[SMEM] * 2 + [VMEM] * 3,
        out_specs=(VMEM,) * 5,
        compiler_params=pltpu.CompilerParams(vmem_limit_bytes=20 << 20),
        name="pick_early",
    )(asked, wanted, own, far1, far3)


def pick_late_kernel(asked, wanted, own, far1, far3, low2, high2, near, out1, out3, out2, line, far2):
    far2[pl.ds(0, HALF_ROWS), :] = low2[...]
    far2[pl.ds(HALF_ROWS, HALF_ROWS + 16), :] = high2[...]
    tables = ((0, own), (1, far1), (3, far3), (2, far2))
    for r in range(CAP):
        move(far2, asked[0, 2 * CAP + r], out1, r)
        move(far2, asked[2, 2 * CAP + r], out3, r)
        move(far2, wanted[2 * CAP + r], near, r)
    for i, (k, table) in enumerate(tables):
        for r in range(CAP):
            move(table, asked[1, k * CAP + r], out2, i * CAP + r)
    rows = sum(t[pl.ds(OWN_ROWS, 16), :].astype(jnp.float32) for _, t in tables)
    sums = jnp.sum(rows, axis=0, keepdims=True)
    line[...] = jnp.broadcast_to(sums, (8, C))


def pick_late(asked, wanted, own, far1, far3, low2, high2):
    b16 = jnp.bfloat16
    piece = jax.ShapeDtypeStruct((CAP * BLOCK, C), b16)
    return pl.pallas_call(
        pick_late_kernel,
        out_shape=(
            piece,
            piece,
            piece,
            jax.ShapeDtypeStruct((PICKED * BLOCK, C), b16),
            jax.ShapeDtypeStruct((8, C), jnp.float32),
        ),
        in_specs=[SMEM] * 2 + [VMEM] * 5,
        out_specs=(VMEM,) * 5,
        scratch_shapes=[pltpu.VMEM((SENT_ROWS, C), b16)],
        compiler_params=pltpu.CompilerParams(vmem_limit_bytes=20 << 20),
        name="pick_late",
    )(asked, wanted, own, far1, far3, low2, high2)


def tile_kernel(part, table_count, resume, finish, *refs):
    refs = list(refs)
    slots, group_target, part_start, words, own = refs[:5]
    tables = refs[5 : 5 + table_count]
    refs = refs[5 + table_count :]
    if resume:
        earlier = refs.pop(0)
    if finish:
        current, all_sums, fresh = refs[:3]
        refs = refs[3:]
        if finish == "more":
            sent = refs.pop(0)
    total, score_a, score_b, bits = refs[:4]

    row = lax.broadcasted_iota(jnp.int32, (BLOCK, BLOCK), 0)
    bits[...] = lax.shift_left(jnp.ones_like(row), lax.rem(row, 30))
    total[...] = earlier[...] if resume else jnp.zeros_like(total)
    sub = lax.broadcasted_iota(jnp.int32, (8, BLOCK), 0)
    if table_count == 1:
        held = tables[0]
    else:
        held = refs[4]
        at = 0
        for table in tables:
            held[pl.ds(at, table.shape[0]), :] = table[...]
            at += table.shape[0]

    def rows_of(index):
        return pl.ds(pl.multiple_of(index * BLOCK, BLOCK), BLOCK)

    def word_rows(pattern):
        rows = []
        for v in range(BLOCK // 8):
            low, high = 8 * v // 30, (8 * v + 7) // 30
            chunk = jnp.broadcast_to(words[pattern, low : low + 1, :], (8, BLOCK))
            if high != low:
                other = jnp.broadcast_to(words[pattern, high : high + 1, :], (8, BLOCK))
                chunk = jnp.where(sub + 8 * v < 30 * high, chunk, other)
            rows.append(chunk)
        return jnp.concatenate(rows, axis=0)

    def remote(group, i):
        return held[rows_of(slots[group * GROUP + i] & 63), :]

    def score(group, out):
        mine = own[rows_of(group_target[group]), :]
        for i in range(GROUP):
            out[:, i * BLOCK : (i + 1) * BLOCK] = lax.dot_general(
                mine,
                remote(group, i),
                (((1,), (1,)), ((), ())),
                preferred_element_type=jnp.float32,
            )

    def add(group, scores):
        weights = []
        for i in range(GROUP):
            packed = word_rows(slots[group * GROUP + i] >> 6)
            negative = jnp.minimum(scores[:, i * BLOCK : (i + 1) * BLOCK] * (-1.0 / UNIT), -FLOOR)
            weight = 1.0 / (1.0 - jnp.exp(negative))
            linked = (packed & bits[...]) != 0
            weights.append(jnp.where(linked, weight, 0.0).astype(jnp.bfloat16))
        total[rows_of(group_target[group]), :] += jnp.dot(
            jnp.concatenate(weights, axis=1),
            jnp.concatenate([remote(group, i) for i in range(GROUP)], axis=0),
            preferred_element_type=jnp.float32,
        )

    start, stop = part_start[part], part_start[part + 1]
    score(start, score_a)

    def two(i, _):
        group = start + 2 * i
        score(group + 1, score_b)
        add(group, score_a)
        score(jnp.minimum(group + 2, stop - 1), score_a)
        add(group + 1, score_b)
        return 0

    lax.fori_loop(0, (stop - start) >> 1, two, 0)

    if finish:
        col_sums = all_sums[0:1, :]
        moved_sums = jnp.zeros((8, C), jnp.float32)
        for j in range(BPD):
            at = pl.ds(j * BLOCK, BLOCK)
            moved = jnp.maximum(current[at, :] + STEP_SIZE * (total[at, :] - col_sums), 0.0)
            fresh[at, :] = moved
            if finish == "more":
                sent[at, :] = moved.astype(jnp.bfloat16)
                moved_sums = moved_sums + jnp.sum(moved.reshape(BLOCK // 8, 8, C), axis=0)
        if finish == "more":
            sent[pl.ds(OWN_ROWS, 16), :] = sum_rows(jnp.sum(moved_sums, axis=0, keepdims=True))


def run_tiles(name, part, lists, words, own, tables, earlier=None, current=None, sums=None, finish=""):
    f32 = jnp.float32
    blocks = jax.ShapeDtypeStruct((OWN_ROWS, C), f32)
    args = [*lists, words, own, *tables]
    specs = [SMEM] * 3 + [VMEM] * (2 + len(tables))
    scratch = []
    out = [blocks]
    if earlier is not None:
        args.append(earlier)
        specs.append(VMEM)
    if finish:
        args += [current, sums]
        specs += [VMEM] * 2
        scratch.append(pltpu.VMEM((OWN_ROWS, C), f32))
        if finish == "more":
            out.append(jax.ShapeDtypeStruct((SENT_ROWS, C), jnp.bfloat16))
    scratch += [
        pltpu.VMEM((BLOCK, GROUP * BLOCK), f32),
        pltpu.VMEM((BLOCK, GROUP * BLOCK), f32),
        pltpu.VMEM((BLOCK, BLOCK), jnp.int32),
    ]
    if len(tables) > 1:
        scratch.append(pltpu.VMEM((sum(t.shape[0] for t in tables), C), jnp.bfloat16))
    return pl.pallas_call(
        functools.partial(tile_kernel, part, len(tables), earlier is not None, finish),
        out_shape=tuple(out),
        in_specs=specs,
        out_specs=(VMEM,) * len(out),
        scratch_shapes=scratch,
        compiler_params=pltpu.CompilerParams(vmem_limit_bytes=24 << 20),
        name=name,
    )(*args)


def per_device(affiliations, tile_block, tile_target, tile_pattern, tile_count, block_home, patterns):
    y, x = lax.axis_index("rows_0"), lax.axis_index("rows_1")
    core = lax.axis_index("cols_1")
    place = jnp.stack([jnp.where(core == 0, x, y), jnp.where(core == 0, y, x), core])
    current = affiliations
    own = first(current)
    requests, codes = ask(
        place.astype(jnp.int32), tile_block[0], tile_target[0], tile_count, block_home
    )
    requests = requests.reshape(SIDE, PICKED)
    asked = jnp.stack([fetch(requests[m], 0, SIDE - m) for m in (1, 2, 3)])
    words = jnp.concatenate([patterns, jnp.zeros((1, *patterns.shape[1:]), jnp.int32)], axis=0)

    lists = sort_tiles(codes, tile_pattern[0], tile_count)
    for step in range(STEPS):
        far1, far3 = fetch(own, 1, 0), fetch(own, 3, 0)
        near1, pass1, pass3, out1, out3 = pick_early(asked, requests[0], own, far1, far3)
        low2, high2 = fetch(pass1, 1, 0), fetch(pass3, 3, 0)
        side1, side3 = fetch(out1, 0, 1), fetch(out3, 0, 3)
        lists, low2, high2 = lax.optimization_barrier((lists, low2, high2))
        near2, out1, out3, out2, line = pick_late(asked, requests[0], own, far1, far3, low2, high2)
        lines = tuple(fetch(line, 0, m) for m in (1, 3, 2))
        lines, out2, side1, side3 = lax.optimization_barrier((lines, out2, side1, side3))
        side2 = fetch(out2, 0, 2)
        late1, late3 = fetch(out1, 0, 1), fetch(out3, 0, 3)
        col_sums = sum_over_cols(line + lines[0] + lines[1] + lines[2])
        tables = (side1, side3, near1, near2)
        (total,) = run_tiles("sides", 0, lists, words, own, tables)
        (total,) = run_tiles("across", 1, lists, words, own, (side2,), total)
        total, late1, late3 = lax.optimization_barrier((total, late1, late3))
        finish = "more" if step < STEPS - 1 else "end"
        current, *own_next = run_tiles(
            "late", 2, lists, words, own, (late1, late3), total, current, col_sums, finish
        )
        if own_next:
            (own,) = own_next
    return current


def solution(mesh):
    torus = Mesh(mesh.devices.reshape(4, 4, 4, 2), ALL)
    return jax.shard_map(
        per_device,
        mesh=torus,
        in_specs=(P(ALL, None), P(ALL, None), P(ALL, None), P(ALL, None), P(ALL), P(), P()),
        out_specs=P(ALL, None),
        check_vma=False,
    )
```

```python
import functools

import jax
import jax.numpy as jnp
from jax import lax
from jax.experimental import pallas as pl
from jax.experimental.pallas import tpu as pltpu
from jax.sharding import Mesh
from jax.sharding import PartitionSpec as P

C = 512
BLOCK = 128
STEPS = 2
BPD = 8
SIDE = 4
CAP = 4
N_COLS = 8
NODES = 131072
UNIT = 1572864
PATTERNS = 192
TILES = 240
GROUP = 4
PARTS = 4
KEYS = PARTS * BPD
GROUPS = (TILES + KEYS * (GROUP - 1)) // GROUP + 2 * PARTS + 2
SLOTS = GROUPS * GROUP
LIST = SLOTS + GROUPS + 8
EMPTY = PATTERNS * 64
FLOOR = 0.001
STEP_SIZE = 0.3 / NODES
OWN_ROWS = BPD * BLOCK
SENT_ROWS = OWN_ROWS + 16
PICKED = SIDE * CAP
HALF_ROWS = OWN_ROWS // 2

ALL = ("rows_0", "rows_1", "cols_0", "cols_1")
VMEM = pl.BlockSpec(memory_space=pltpu.VMEM)
SMEM = pl.BlockSpec(memory_space=pltpu.SMEM)


def pairs(first, second):
    out = []
    for y in range(SIDE):
        for x in range(SIDE):
            for z in range(4):
                for core in range(2):
                    dx, dy = (first, second) if core == 0 else (second, first)
                    sy, sx = (y + dy) % SIDE, (x + dx) % SIDE
                    out.append((((sy * 4 + sx) * 4 + z) * 2 + core, ((y * 4 + x) * 4 + z) * 2 + core))
    return out


def fetch(value, first, second):
    return lax.ppermute(value, ALL, pairs(first, second))


def sum_over_cols(part):
    for axis, size in (("cols_1", 2), ("cols_0", 4)):
        step = 1
        while step < size:
            part = part + lax.ppermute(part, axis, [(i, i ^ step) for i in range(size)])
            step *= 2
    return part


OWNERS = (
    ((0, 1), (0, 2), (0, 3)),
    ((1, 0), (1, 1), (1, 2), (1, 3), (3, 0), (3, 1), (3, 2), (3, 3)),
    ((2, 0), (2, 1)),
    ((2, 2), (2, 3)),
)


def clear(ref, start, size, value):
    def body(i, _):
        for j in range(8):
            ref[start + 8 * i + j] = value
        return 0

    lax.fori_loop(0, size // 8, body, 0)


def ask_kernel(place, blocks, targets, count, home, requests, codes, rank, fill, base):
    first, second, core = place[0], place[1], place[2]
    clear(rank, 0, 128, -1)
    clear(fill, 0, 16, 0)
    clear(requests, 0, 64, 0)
    base[0] = 0
    for part, owners in enumerate(OWNERS):
        for i, (m, k) in enumerate(owners):
            base[m * SIDE + k] = part * 512 + i * CAP

    def note(t, _):
        slot = home[blocks[t]]
        row = slot >> 6
        local = slot & (BPD - 1)
        y, x = row >> 2, row & (SIDE - 1)
        owner_first = jnp.where(core == 0, x, y)
        owner_second = jnp.where(core == 0, y, x)
        k = (owner_first - first) & (SIDE - 1)
        m = (owner_second - second) & (SIDE - 1)
        pair = m * SIDE + k
        seen = rank[pair * BPD + local]
        held = fill[pair]
        mine = jnp.minimum(jnp.where(seen < 0, held, seen), CAP - 1)
        rank[pair * BPD + local] = mine
        fill[pair] = jnp.where(seen < 0, held + 1, held)
        requests[pair * CAP + mine] = local
        codes[t] = base[pair] + mine + targets[t] * 64
        return 0

    lax.fori_loop(0, count[0], note, 0)


def ask(place, blocks, targets, count, home):
    i32 = jnp.int32
    return pl.pallas_call(
        ask_kernel,
        out_shape=(jax.ShapeDtypeStruct((64,), i32), jax.ShapeDtypeStruct((TILES,), i32)),
        in_specs=[SMEM] * 5,
        out_specs=(SMEM,) * 2,
        scratch_shapes=[pltpu.SMEM((128,), i32), pltpu.SMEM((16,), i32), pltpu.SMEM((16,), i32)],
        compiler_params=pltpu.CompilerParams(vmem_limit_bytes=2 << 20),
        name="ask",
    )(place, blocks, targets, count, home)


def sort_kernel(codes, pattern_ids, count, lists, per_key):
    clear(per_key, 0, KEYS, 0)
    clear(lists, 0, SLOTS, EMPTY)
    clear(lists, SLOTS, GROUPS, 0)

    def tally(t, _):
        key = codes[t] >> 6
        per_key[key] = per_key[key] + 1
        return 0

    lax.fori_loop(0, count[0], tally, 0)
    group = jnp.int32(0)
    for part in range(PARTS):
        lists[SLOTS + GROUPS + part] = group
        start = group
        for target in range(BPD):
            key = part * BPD + target
            size = (per_key[key] + GROUP - 1) >> 2
            per_key[key] = group * GROUP
            group = group + size
        group = start + jnp.maximum(2, (group - start + 1) & -2)
    lists[SLOTS + GROUPS + PARTS] = group

    def put(t, _):
        code = codes[t]
        key = code >> 6
        at = per_key[key]
        per_key[key] = at + 1
        lists[at] = pattern_ids[t] * 64 + (code & 63)
        lists[SLOTS + (at >> 2)] = key & (BPD - 1)
        return 0

    lax.fori_loop(0, count[0], put, 0)


def sort_tiles(codes, pattern_ids, count):
    i32 = jnp.int32
    return pl.pallas_call(
        sort_kernel,
        out_shape=jax.ShapeDtypeStruct((LIST,), i32),
        in_specs=[SMEM] * 3,
        out_specs=SMEM,
        scratch_shapes=[pltpu.SMEM((KEYS,), i32)],
        compiler_params=pltpu.CompilerParams(vmem_limit_bytes=2 << 20),
        name="sort_tiles",
    )(codes, pattern_ids, count)


def sum_rows(total):
    high = total.astype(jnp.bfloat16).astype(jnp.float32)
    rest = total - high
    middle = rest.astype(jnp.bfloat16).astype(jnp.float32)
    low = rest - middle
    row = lax.broadcasted_iota(jnp.int32, (16, C), 0)
    out = jnp.where(row == 0, high, jnp.where(row == 1, middle, jnp.where(row == 2, low, 0.0)))
    return out.astype(jnp.bfloat16)


SENT = tuple(
    jax.ShapeDtypeStruct((rows, C), jnp.bfloat16) for rows in (SENT_ROWS, HALF_ROWS + 16, HALF_ROWS + 16)
)


def put_block(j, rows, sent, low, high):
    sent[pl.ds(j * BLOCK, BLOCK), :] = rows
    half, at = (low, j) if j < BPD // 2 else (high, j - BPD // 2)
    half[pl.ds(at * BLOCK, BLOCK), :] = rows


def put_sums(total, sent, low, high):
    rows = sum_rows(total)
    sent[pl.ds(OWN_ROWS, 16), :] = rows
    for half in (low, high):
        half[pl.ds(HALF_ROWS, 16), :] = rows


def first_kernel(current, sent, low, high):
    total = jnp.zeros((8, C), jnp.float32)
    for j in range(BPD):
        rows = current[pl.ds(j * BLOCK, BLOCK), :]
        put_block(j, rows.astype(jnp.bfloat16), sent, low, high)
        total = total + jnp.sum(rows.reshape(BLOCK // 8, 8, C), axis=0)
    put_sums(jnp.sum(total, axis=0, keepdims=True), sent, low, high)


def first(current):
    return pl.pallas_call(
        first_kernel,
        out_shape=SENT,
        in_specs=[VMEM],
        out_specs=(VMEM,) * 3,
        compiler_params=pltpu.CompilerParams(vmem_limit_bytes=20 << 20),
        name="first",
    )(current)


def move(table, local, out, at):
    rows = pl.ds(pl.multiple_of(local * BLOCK, BLOCK), BLOCK)
    out[pl.ds(at * BLOCK, BLOCK), :] = table[rows, :]


def pick_kernel(
    asked, wanted, own, low1, high1, low2, high2, low3, high3,
    near, out1, out3, out2a, out2b, line, far1, far2, far3,
):
    for low, high, far in ((low1, high1, far1), (low2, high2, far2), (low3, high3, far3)):
        far[pl.ds(0, HALF_ROWS), :] = low[pl.ds(0, HALF_ROWS), :]
        far[pl.ds(HALF_ROWS, HALF_ROWS + 16), :] = high[...]
    tables = (own, far1, far2, far3)
    for m, out in ((1, out1), (3, out3)):
        for k, table in enumerate(tables):
            for r in range(CAP):
                move(table, asked[m - 1, k * CAP + r], out, k * CAP + r)
    for k, table in enumerate(tables):
        out, at = (out2a, k) if k < 2 else (out2b, k - 2)
        for r in range(CAP):
            move(table, asked[1, k * CAP + r], out, at * CAP + r)
            if k > 0:
                move(table, wanted[k * CAP + r], near, (k - 1) * CAP + r)
    rows = sum(t[pl.ds(OWN_ROWS, 16), :].astype(jnp.float32) for t in tables)
    sums = jnp.sum(rows, axis=0, keepdims=True)
    line[...] = jnp.broadcast_to(sums, (8, C))
    for out in (out1, out3):
        out[pl.ds(PICKED * BLOCK, 16), :] = sum_rows(sums)


def pick(asked, wanted, own, *far):
    b16 = jnp.bfloat16
    shape = lambda rows: jax.ShapeDtypeStruct((rows, C), b16)
    return pl.pallas_call(
        pick_kernel,
        out_shape=(
            shape(3 * CAP * BLOCK),
            shape(PICKED * BLOCK + 16),
            shape(PICKED * BLOCK + 16),
            shape(2 * CAP * BLOCK),
            shape(2 * CAP * BLOCK),
            jax.ShapeDtypeStruct((8, C), jnp.float32),
        ),
        in_specs=[SMEM] * 2 + [VMEM] * 7,
        out_specs=(VMEM,) * 6,
        scratch_shapes=[pltpu.VMEM((SENT_ROWS, C), b16)] * 3,
        compiler_params=pltpu.CompilerParams(vmem_limit_bytes=20 << 20),
        name="pick",
    )(asked, wanted, own, *far)


def tile_kernel(part, table_count, resume, finish, *refs):
    refs = list(refs)
    lists, words, own = refs[:3]
    tables = refs[3 : 3 + table_count]
    refs = refs[3 + table_count :]
    if resume:
        earlier = refs.pop(0)
    if finish:
        current, chain, cross, fresh = refs[:4]
        refs = refs[4:]
        if finish == "more":
            sent = refs[:3]
            refs = refs[3:]
    total, score_a, score_b, bits = refs[:4]

    row = lax.broadcasted_iota(jnp.int32, (BLOCK, BLOCK), 0)
    bits[...] = lax.shift_left(jnp.ones_like(row), lax.rem(row, 30))
    total[...] = earlier[...] if resume else jnp.zeros_like(total)
    sub = lax.broadcasted_iota(jnp.int32, (8, BLOCK), 0)
    if table_count == 1:
        held = tables[0]
    else:
        held = refs[4]
        at = 0
        for table in tables:
            held[pl.ds(at, PICKED * BLOCK), :] = table[pl.ds(0, PICKED * BLOCK), :]
            at += PICKED * BLOCK

    def rows_of(index):
        return pl.ds(pl.multiple_of(index * BLOCK, BLOCK), BLOCK)

    def word_rows(pattern):
        rows = []
        for v in range(BLOCK // 8):
            low, high = 8 * v // 30, (8 * v + 7) // 30
            chunk = jnp.broadcast_to(words[pattern, low : low + 1, :], (8, BLOCK))
            if high != low:
                other = jnp.broadcast_to(words[pattern, high : high + 1, :], (8, BLOCK))
                chunk = jnp.where(sub + 8 * v < 30 * high, chunk, other)
            rows.append(chunk)
        return jnp.concatenate(rows, axis=0)

    def remote(group, i):
        return held[rows_of(lists[group * GROUP + i] & 63), :]

    def score(group, out):
        mine = own[rows_of(lists[SLOTS + group]), :]
        for i in range(GROUP):
            out[:, i * BLOCK : (i + 1) * BLOCK] = lax.dot_general(
                mine,
                remote(group, i),
                (((1,), (1,)), ((), ())),
                preferred_element_type=jnp.float32,
            )

    def add(group, scores):
        weights = []
        for i in range(GROUP):
            packed = word_rows(lists[group * GROUP + i] >> 6)
            negative = jnp.minimum(scores[:, i * BLOCK : (i + 1) * BLOCK] * (-1.0 / UNIT), -FLOOR)
            weight = 1.0 / (1.0 - jnp.exp(negative))
            linked = (packed & bits[...]) != 0
            weights.append(jnp.where(linked, weight, 0.0).astype(jnp.bfloat16))
        total[rows_of(lists[SLOTS + group]), :] += jnp.dot(
            jnp.concatenate(weights, axis=1),
            jnp.concatenate([remote(group, i) for i in range(GROUP)], axis=0),
            preferred_element_type=jnp.float32,
        )

    start, stop = lists[SLOTS + GROUPS + part], lists[SLOTS + GROUPS + part + 1]
    score(start, score_a)

    def two(i, _):
        group = start + 2 * i
        score(group + 1, score_b)
        add(group, score_a)
        score(jnp.minimum(group + 2, stop - 1), score_a)
        add(group + 1, score_b)
        return 0

    lax.fori_loop(0, (stop - start) >> 1, two, 0)

    if finish:
        col_sums = chain[0:1, :] + cross[4:5, :]
        moved_sums = jnp.zeros((8, C), jnp.float32)
        for j in range(BPD):
            at = pl.ds(j * BLOCK, BLOCK)
            moved = jnp.maximum(current[at, :] + STEP_SIZE * (total[at, :] - col_sums), 0.0)
            fresh[at, :] = moved
            if finish == "more":
                put_block(j, moved.astype(jnp.bfloat16), *sent)
                moved_sums = moved_sums + jnp.sum(moved.reshape(BLOCK // 8, 8, C), axis=0)
        if finish == "more":
            put_sums(jnp.sum(moved_sums, axis=0, keepdims=True), *sent)


def run_tiles(name, part, lists, words, own, tables, earlier=None, current=None, sums=(), finish=""):
    f32 = jnp.float32
    blocks = jax.ShapeDtypeStruct((OWN_ROWS, C), f32)
    args = [lists, words, own, *tables]
    specs = [SMEM] + [VMEM] * (2 + len(tables))
    scratch = []
    out = [blocks]
    if earlier is not None:
        args.append(earlier)
        specs.append(VMEM)
    if finish:
        args += [current, *sums]
        specs += [VMEM] * 3
        scratch.append(pltpu.VMEM((OWN_ROWS, C), f32))
        if finish == "more":
            out += SENT
    scratch += [
        pltpu.VMEM((BLOCK, GROUP * BLOCK), f32),
        pltpu.VMEM((BLOCK, GROUP * BLOCK), f32),
        pltpu.VMEM((BLOCK, BLOCK), jnp.int32),
    ]
    if len(tables) > 1:
        scratch.append(pltpu.VMEM((len(tables) * PICKED * BLOCK, C), jnp.bfloat16))
    return pl.pallas_call(
        functools.partial(tile_kernel, part, len(tables), earlier is not None, finish),
        out_shape=tuple(out),
        in_specs=specs,
        out_specs=(VMEM,) * len(out),
        scratch_shapes=scratch,
        compiler_params=pltpu.CompilerParams(vmem_limit_bytes=24 << 20),
        name=name,
    )(*args)


def line_sums(line, side1, side3):
    rows = sum(t[PICKED * BLOCK :].astype(jnp.float32) for t in (side1, side3))
    beside = jnp.sum(rows, axis=0, keepdims=True)
    return line + jnp.where(jnp.arange(8)[:, None] < 4, beside, 0.0)


def per_device(affiliations, tile_block, tile_target, tile_pattern, tile_count, block_home, patterns):
    y, x = lax.axis_index("rows_0"), lax.axis_index("rows_1")
    core = lax.axis_index("cols_1")
    place = jnp.stack([jnp.where(core == 0, x, y), jnp.where(core == 0, y, x), core])
    current = affiliations
    own, low, high = first(current)
    requests, codes = ask(
        place.astype(jnp.int32), tile_block[0], tile_target[0], tile_count, block_home
    )
    requests = requests.reshape(SIDE, PICKED)
    asked = jnp.stack([fetch(requests[m], 0, SIDE - m) for m in (1, 2, 3)])
    words = jnp.concatenate([patterns, jnp.zeros((1, *patterns.shape[1:]), jnp.int32)], axis=0)

    lists = sort_tiles(codes, tile_pattern[0], tile_count)
    for step in range(STEPS):
        low1, high3 = fetch(low, 1, 0), fetch(high, 3, 0)
        high1, low3 = fetch(high, 1, 0), fetch(low, 3, 0)
        low2, high2 = fetch(low1, 1, 0), fetch(high3, 3, 0)
        lists, low2, high2 = lax.optimization_barrier((lists, low2, high2))
        near, out1, out3, out2a, out2b, line = pick(
            asked, requests[0], own, low1, high1, low2, high2, low3, high3
        )
        side1, side3 = fetch(out1, 0, 1), fetch(out3, 0, 3)
        far_a, far_b = fetch(out2a, 0, 2), fetch(out2b, 0, 2)
        (total,) = run_tiles("near", 0, lists, words, own, (near,))
        total, side1, side3 = lax.optimization_barrier((total, side1, side3))
        chain = sum_over_cols(line_sums(line, side1, side3))
        cross = fetch(chain, 2, 2)
        (total,) = run_tiles("sides", 1, lists, words, own, (side1, side3), total)
        (total,) = run_tiles("across", 2, lists, words, own, (far_a,), total)
        total, far_b = lax.optimization_barrier((total, far_b))
        finish = "more" if step < STEPS - 1 else "end"
        current, *own_next = run_tiles(
            "late", 3, lists, words, own, (far_b,), total, current, (chain, cross), finish
        )
        if own_next:
            own, low, high = own_next
    return current


def solution(mesh):
    torus = Mesh(mesh.devices.reshape(4, 4, 4, 2), ALL)
    return jax.shard_map(
        per_device,
        mesh=torus,
        in_specs=(P(ALL, None), P(ALL, None), P(ALL, None), P(ALL, None), P(ALL), P(), P()),
        out_specs=P(ALL, None),
        check_vma=False,
    )
```

```python
import functools

import jax
import jax.numpy as jnp
from jax import lax
from jax.experimental import pallas as pl
from jax.experimental.pallas import tpu as pltpu
from jax.sharding import Mesh
from jax.sharding import PartitionSpec as P

C = 512
BLOCK = 128
STEPS = 2
BPD = 8
SIDE = 4
CAP = 4
N_COLS = 8
NODES = 131072
UNIT = 1572864
PATTERNS = 192
TILES = 240
GROUP = 4
PARTS = 3
KEYS = PARTS * BPD
GROUPS = -(-((TILES + KEYS * (GROUP - 1)) // GROUP + 2 * PARTS) // 8) * 8
SLOTS = GROUPS * GROUP
LIST = SLOTS + GROUPS + 8
EMPTY = PATTERNS * 64
FLOOR = 0.001
STEP_SIZE = 0.3 / NODES
OWN_ROWS = BPD * BLOCK
SENT_ROWS = OWN_ROWS + 16
PICKED = SIDE * CAP
HALF_ROWS = OWN_ROWS // 2

ALL = ("rows_0", "rows_1", "cols_0", "cols_1")
VMEM = pl.BlockSpec(memory_space=pltpu.VMEM)
SMEM = pl.BlockSpec(memory_space=pltpu.SMEM)
HBM = pl.BlockSpec(memory_space=pltpu.HBM)


def pairs(first, second):
    out = []
    for y in range(SIDE):
        for x in range(SIDE):
            for z in range(4):
                for core in range(2):
                    dx, dy = (first, second) if core == 0 else (second, first)
                    sy, sx = (y + dy) % SIDE, (x + dx) % SIDE
                    out.append((((sy * 4 + sx) * 4 + z) * 2 + core, ((y * 4 + x) * 4 + z) * 2 + core))
    return out


def fetch(value, first, second):
    return lax.ppermute(value, ALL, pairs(first, second))


def sum_over_cols(part):
    for axis, size in (("cols_1", 2), ("cols_0", 4)):
        step = 1
        while step < size:
            part = part + lax.ppermute(part, axis, [(i, i ^ step) for i in range(size)])
            step *= 2
    return part


OWNERS = (
    ((1, 0), (1, 1), (1, 3), (3, 0), (3, 1), (3, 3), (0, 1), (0, 3), (0, 2)),
    ((2, 0), (2, 1), (2, 3), (2, 2)),
    ((1, 2), (3, 2)),
)


def clear(ref, start, size, value):
    def body(i, _):
        for j in range(8):
            ref[start + 8 * i + j] = value
        return 0

    lax.fori_loop(0, size // 8, body, 0)


def ask_kernel(place, blocks, targets, count, home, requests, codes, rank, fill, base):
    first, second, core = place[0], place[1], place[2]
    clear(rank, 0, 128, -1)
    clear(fill, 0, 16, 0)
    clear(requests, 0, 64, 0)
    base[0] = 0
    for part, owners in enumerate(OWNERS):
        for i, (m, k) in enumerate(owners):
            base[m * SIDE + k] = part * 512 + i * CAP

    def note(t, _):
        slot = home[blocks[t]]
        row = slot >> 6
        local = slot & (BPD - 1)
        y, x = row >> 2, row & (SIDE - 1)
        owner_first = jnp.where(core == 0, x, y)
        owner_second = jnp.where(core == 0, y, x)
        k = (owner_first - first) & (SIDE - 1)
        m = (owner_second - second) & (SIDE - 1)
        pair = m * SIDE + k
        seen = rank[pair * BPD + local]
        held = fill[pair]
        mine = jnp.minimum(jnp.where(seen < 0, held, seen), CAP - 1)
        rank[pair * BPD + local] = mine
        fill[pair] = jnp.where(seen < 0, held + 1, held)
        requests[pair * CAP + mine] = local
        codes[t] = base[pair] + mine + targets[t] * 64
        return 0

    lax.fori_loop(0, count[0], note, 0)


def ask(place, blocks, targets, count, home):
    i32 = jnp.int32
    return pl.pallas_call(
        ask_kernel,
        out_shape=(jax.ShapeDtypeStruct((64,), i32), jax.ShapeDtypeStruct((TILES,), i32)),
        in_specs=[SMEM] * 5,
        out_specs=(SMEM,) * 2,
        scratch_shapes=[pltpu.SMEM((128,), i32), pltpu.SMEM((16,), i32), pltpu.SMEM((16,), i32)],
        compiler_params=pltpu.CompilerParams(vmem_limit_bytes=2 << 20),
        name="ask",
    )(place, blocks, targets, count, home)


def sort_kernel(codes, pattern_ids, count, lists, per_key):
    clear(per_key, 0, KEYS, 0)
    clear(lists, 0, SLOTS, EMPTY)
    clear(lists, SLOTS, GROUPS, 0)

    def tally(t, _):
        key = codes[t] >> 6
        per_key[key] = per_key[key] + 1
        return 0

    lax.fori_loop(0, count[0], tally, 0)
    group = jnp.int32(0)
    for part in range(PARTS):
        lists[SLOTS + GROUPS + part] = group
        start = group
        for target in range(BPD):
            key = part * BPD + target
            size = (per_key[key] + GROUP - 1) >> 2
            per_key[key] = group * GROUP
            group = group + size
        group = start + jnp.maximum(2, (group - start + 1) & -2)
    lists[SLOTS + GROUPS + PARTS] = group

    def put(t, _):
        code = codes[t]
        key = code >> 6
        at = per_key[key]
        per_key[key] = at + 1
        lists[at] = pattern_ids[t] * 64 + (code & 63)
        lists[SLOTS + (at >> 2)] = key & (BPD - 1)
        return 0

    lax.fori_loop(0, count[0], put, 0)


def sort_tiles(codes, pattern_ids, count):
    i32 = jnp.int32
    return pl.pallas_call(
        sort_kernel,
        out_shape=jax.ShapeDtypeStruct((LIST,), i32),
        in_specs=[SMEM] * 3,
        out_specs=SMEM,
        scratch_shapes=[pltpu.SMEM((KEYS,), i32)],
        compiler_params=pltpu.CompilerParams(vmem_limit_bytes=2 << 20),
        name="sort_tiles",
    )(codes, pattern_ids, count)


def sum_rows(total):
    high = total.astype(jnp.bfloat16).astype(jnp.float32)
    rest = total - high
    middle = rest.astype(jnp.bfloat16).astype(jnp.float32)
    low = rest - middle
    row = lax.broadcasted_iota(jnp.int32, (16, C), 0)
    out = jnp.where(row == 0, high, jnp.where(row == 1, middle, jnp.where(row == 2, low, 0.0)))
    return out.astype(jnp.bfloat16)


def first_kernel(current, sent):
    total = jnp.zeros((8, C), jnp.float32)
    for j in range(BPD):
        rows = current[pl.ds(j * BLOCK, BLOCK), :]
        sent[pl.ds(j * BLOCK, BLOCK), :] = rows.astype(jnp.bfloat16)
        total = total + jnp.sum(rows.reshape(BLOCK // 8, 8, C), axis=0)
    sent[pl.ds(OWN_ROWS, 16), :] = sum_rows(jnp.sum(total, axis=0, keepdims=True))


def first(current):
    return pl.pallas_call(
        first_kernel,
        out_shape=jax.ShapeDtypeStruct((SENT_ROWS, C), jnp.bfloat16),
        in_specs=[VMEM],
        out_specs=VMEM,
        compiler_params=pltpu.CompilerParams(vmem_limit_bytes=20 << 20),
        name="first",
    )(current)


def move(table, local, out, at):
    rows = pl.ds(pl.multiple_of(local * BLOCK, BLOCK), BLOCK)
    out[pl.ds(at * BLOCK, BLOCK), :] = table[rows, :]


def pick_early_kernel(asked, wanted, own, far1, far3, near, pass1, pass3, out1, out3):
    pass1[...] = far1[pl.ds(0, HALF_ROWS), :]
    pass3[...] = far3[pl.ds(HALF_ROWS, HALF_ROWS + 16), :]
    for m, out in ((1, out1), (3, out3)):
        for i, (k, table) in enumerate(((0, own), (1, far1), (3, far3))):
            for r in range(CAP):
                move(table, asked[m - 1, k * CAP + r], out, i * CAP + r)
    for r in range(CAP):
        move(far1, wanted[CAP + r], near, r)
        move(far3, wanted[3 * CAP + r], near, CAP + r)


def pick_early(asked, wanted, own, far1, far3):
    b16 = jnp.bfloat16
    out = jax.ShapeDtypeStruct((3 * CAP * BLOCK, C), b16)
    return pl.pallas_call(
        pick_early_kernel,
        out_shape=(
            jax.ShapeDtypeStruct((2 * CAP * BLOCK, C), b16),
            jax.ShapeDtypeStruct((HALF_ROWS, C), b16),
            jax.ShapeDtypeStruct((HALF_ROWS + 16, C), b16),
            out,
            out,
        ),
        in_specs=[SMEM] * 2 + [VMEM] * 3,
        out_specs=(VMEM,) * 5,
        compiler_params=pltpu.CompilerParams(vmem_limit_bytes=20 << 20),
        name="pick_early",
    )(asked, wanted, own, far1, far3)


def pick_late_kernel(asked, wanted, own, far1, far3, low2, high2, near, out1, out3, out2, line, far2):
    far2[pl.ds(0, HALF_ROWS), :] = low2[...]
    far2[pl.ds(HALF_ROWS, HALF_ROWS + 16), :] = high2[...]
    tables = ((0, own), (1, far1), (3, far3), (2, far2))
    for r in range(CAP):
        move(far2, asked[0, 2 * CAP + r], out1, r)
        move(far2, asked[2, 2 * CAP + r], out3, r)
        move(far2, wanted[2 * CAP + r], near, r)
    for i, (k, table) in enumerate(tables):
        for r in range(CAP):
            move(table, asked[1, k * CAP + r], out2, i * CAP + r)
    rows = sum(t[pl.ds(OWN_ROWS, 16), :].astype(jnp.float32) for _, t in tables)
    sums = jnp.sum(rows, axis=0, keepdims=True)
    line[...] = jnp.broadcast_to(sums, (8, C))


def pick_late(asked, wanted, own, far1, far3, low2, high2):
    b16 = jnp.bfloat16
    piece = jax.ShapeDtypeStruct((CAP * BLOCK, C), b16)
    return pl.pallas_call(
        pick_late_kernel,
        out_shape=(
            piece,
            piece,
            piece,
            jax.ShapeDtypeStruct((PICKED * BLOCK, C), b16),
            jax.ShapeDtypeStruct((8, C), jnp.float32),
        ),
        in_specs=[SMEM] * 2 + [VMEM] * 5,
        out_specs=(VMEM,) * 5,
        scratch_shapes=[pltpu.VMEM((SENT_ROWS, C), b16)],
        compiler_params=pltpu.CompilerParams(vmem_limit_bytes=20 << 20),
        name="pick_late",
    )(asked, wanted, own, far1, far3, low2, high2)


def tile_kernel(part, table_count, resume, finish, *refs):
    refs = list(refs)
    lists, words, own = refs[:3]
    tables = refs[3 : 3 + table_count]
    refs = refs[3 + table_count :]
    if resume:
        earlier = refs.pop(0)
    if finish:
        current, all_sums, fresh = refs[:3]
        refs = refs[3:]
        if finish == "more":
            sent = refs.pop(0)
    if finish == "end":
        ready, sems = refs[:2]
        refs = refs[2:]
    total, score_a, score_b, bits = refs[:4]

    row = lax.broadcasted_iota(jnp.int32, (BLOCK, BLOCK), 0)
    bits[...] = lax.shift_left(jnp.ones_like(row), lax.rem(row, 30))
    total[...] = earlier[...] if resume else jnp.zeros_like(total)
    sub = lax.broadcasted_iota(jnp.int32, (8, BLOCK), 0)
    if table_count == 1:
        held = tables[0]
    else:
        held = refs[4]
        at = 0
        for table in tables:
            held[pl.ds(at, table.shape[0]), :] = table[...]
            at += table.shape[0]

    def rows_of(index):
        return pl.ds(pl.multiple_of(index * BLOCK, BLOCK), BLOCK)

    def word_rows(pattern):
        rows = []
        for v in range(BLOCK // 8):
            low, high = 8 * v // 30, (8 * v + 7) // 30
            chunk = jnp.broadcast_to(words[pattern, low : low + 1, :], (8, BLOCK))
            if high != low:
                other = jnp.broadcast_to(words[pattern, high : high + 1, :], (8, BLOCK))
                chunk = jnp.where(sub + 8 * v < 30 * high, chunk, other)
            rows.append(chunk)
        return jnp.concatenate(rows, axis=0)

    def remote(group, i):
        return held[rows_of(lists[group * GROUP + i] & 63), :]

    def score(group, out):
        mine = own[rows_of(lists[SLOTS + group]), :]
        for i in range(GROUP):
            out[:, i * BLOCK : (i + 1) * BLOCK] = lax.dot_general(
                mine,
                remote(group, i),
                (((1,), (1,)), ((), ())),
                preferred_element_type=jnp.float32,
            )

    def add(group, scores):
        weights = []
        for i in range(GROUP):
            packed = word_rows(lists[group * GROUP + i] >> 6)
            negative = jnp.minimum(scores[:, i * BLOCK : (i + 1) * BLOCK] * (-1.0 / UNIT), -FLOOR)
            weight = 1.0 / (1.0 - jnp.exp(negative))
            linked = (packed & bits[...]) != 0
            weights.append(jnp.where(linked, weight, 0.0).astype(jnp.bfloat16))
        total[rows_of(lists[SLOTS + group]), :] += jnp.dot(
            jnp.concatenate(weights, axis=1),
            jnp.concatenate([remote(group, i) for i in range(GROUP)], axis=0),
            preferred_element_type=jnp.float32,
        )

    start, stop = lists[SLOTS + GROUPS + part], lists[SLOTS + GROUPS + part + 1]
    score(start, score_a)

    def two(i, _):
        group = start + 2 * i
        score(group + 1, score_b)
        add(group, score_a)
        score(jnp.minimum(group + 2, stop - 1), score_a)
        add(group + 1, score_b)
        return 0

    lax.fori_loop(0, (stop - start) >> 1, two, 0)

    if not finish:
        return
    col_sums = all_sums[0:1, :]
    moved_sums = jnp.zeros((8, C), jnp.float32)
    copies = []
    for j in range(BPD):
        at = pl.ds(j * BLOCK, BLOCK)
        moved = jnp.maximum(current[at, :] + STEP_SIZE * (total[at, :] - col_sums), 0.0)
        if finish == "more":
            fresh[at, :] = moved
            sent[at, :] = moved.astype(jnp.bfloat16)
            moved_sums = moved_sums + jnp.sum(moved.reshape(BLOCK // 8, 8, C), axis=0)
        else:
            ready[at, :] = moved
            copies.append(pltpu.make_async_copy(ready.at[at, :], fresh.at[at, :], sems.at[j]))
            copies[j].start()
    if finish == "more":
        sent[pl.ds(OWN_ROWS, 16), :] = sum_rows(jnp.sum(moved_sums, axis=0, keepdims=True))
    for copy in copies:
        copy.wait()


def run_tiles(name, part, lists, words, own, tables, earlier=None, current=None, sums=None, finish=""):
    f32 = jnp.float32
    blocks = jax.ShapeDtypeStruct((OWN_ROWS, C), f32)
    args = [lists, words, own, *tables]
    specs = [SMEM] + [VMEM] * (2 + len(tables))
    scratch = []
    out = [blocks]
    if earlier is not None:
        args.append(earlier)
        specs.append(VMEM)
    if finish:
        args += [current, sums]
        specs += [VMEM] * 2
        if finish == "end":
            scratch += [pltpu.VMEM((OWN_ROWS, C), f32), pltpu.SemaphoreType.DMA((BPD,))]
        scratch.append(pltpu.VMEM((OWN_ROWS, C), f32))
        if finish == "more":
            out.append(jax.ShapeDtypeStruct((SENT_ROWS, C), jnp.bfloat16))
    scratch += [
        pltpu.VMEM((BLOCK, GROUP * BLOCK), f32),
        pltpu.VMEM((BLOCK, GROUP * BLOCK), f32),
        pltpu.VMEM((BLOCK, BLOCK), jnp.int32),
    ]
    if len(tables) > 1:
        scratch.append(pltpu.VMEM((sum(t.shape[0] for t in tables), C), jnp.bfloat16))
    return pl.pallas_call(
        functools.partial(tile_kernel, part, len(tables), earlier is not None, finish),
        out_shape=tuple(out),
        in_specs=specs,
        out_specs=(HBM,) if finish == "end" else (VMEM,) * len(out),
        scratch_shapes=scratch,
        compiler_params=pltpu.CompilerParams(vmem_limit_bytes=24 << 20),
        name=name,
    )(*args)


def per_device(affiliations, tile_block, tile_target, tile_pattern, tile_count, block_home, patterns):
    y, x = lax.axis_index("rows_0"), lax.axis_index("rows_1")
    core = lax.axis_index("cols_1")
    place = jnp.stack([jnp.where(core == 0, x, y), jnp.where(core == 0, y, x), core])
    current = affiliations
    own = first(current)
    requests, codes = ask(
        place.astype(jnp.int32), tile_block[0], tile_target[0], tile_count, block_home
    )
    requests = requests.reshape(SIDE, PICKED)
    asked = jnp.stack([fetch(requests[m], 0, SIDE - m) for m in (1, 2, 3)])
    words = jnp.concatenate([patterns, jnp.zeros((1, *patterns.shape[1:]), jnp.int32)], axis=0)

    lists = sort_tiles(codes, tile_pattern[0], tile_count)
    for step in range(STEPS):
        far1, far3 = fetch(own, 1, 0), fetch(own, 3, 0)
        near1, pass1, pass3, out1, out3 = pick_early(asked, requests[0], own, far1, far3)
        low2, high2 = fetch(pass1, 1, 0), fetch(pass3, 3, 0)
        side1, side3 = fetch(out1, 0, 1), fetch(out3, 0, 3)
        lists, low2, high2 = lax.optimization_barrier((lists, low2, high2))
        near2, out1, out3, out2, line = pick_late(asked, requests[0], own, far1, far3, low2, high2)
        lines = tuple(fetch(line, 0, m) for m in (1, 3, 2))
        lines, out2, side1, side3 = lax.optimization_barrier((lines, out2, side1, side3))
        side2 = fetch(out2, 0, 2)
        late1, late3 = fetch(out1, 0, 1), fetch(out3, 0, 3)
        col_sums = sum_over_cols(line + lines[0] + lines[1] + lines[2])
        tables = (side1, side3, near1, near2)
        (total,) = run_tiles("sides", 0, lists, words, own, tables)
        (total,) = run_tiles("across", 1, lists, words, own, (side2,), total)
        total, late1, late3 = lax.optimization_barrier((total, late1, late3))
        finish = "more" if step < STEPS - 1 else "end"
        current, *own_next = run_tiles(
            "late", 2, lists, words, own, (late1, late3), total, current, col_sums, finish
        )
        if own_next:
            (own,) = own_next
    return current


def solution(mesh):
    torus = Mesh(mesh.devices.reshape(4, 4, 4, 2), ALL)
    return jax.shard_map(
        per_device,
        mesh=torus,
        in_specs=(P(ALL, None), P(ALL, None), P(ALL, None), P(ALL, None), P(ALL), P(), P()),
        out_specs=P(ALL, None),
        check_vma=False,
    )
```

```python
import functools

import jax
import jax.numpy as jnp
from jax import lax
from jax.experimental import pallas as pl
from jax.experimental.pallas import tpu as pltpu
from jax.sharding import Mesh
from jax.sharding import PartitionSpec as P

C = 512
BLOCK = 128
STEPS = 2
BPD = 8
SIDE = 4
CAP = 4
N_COLS = 8
NODES = 131072
UNIT = 1572864
PATTERNS = 192
TILES = 240
PARTS = 3
GROUP = (4, 4, 2)
KEYS = PARTS * BPD
SLOTS = TILES + sum(BPD * (g - 1) + 2 * g for g in GROUP) // 8 * 8 + 8
STARTS = SLOTS + SLOTS // 2
LIST = STARTS + 8
EMPTY = PATTERNS * 64
FLOOR = 0.001
STEP_SIZE = 0.3 / NODES
OWN_ROWS = BPD * BLOCK
SENT_ROWS = OWN_ROWS + 16
PICKED = SIDE * CAP
HALF_ROWS = OWN_ROWS // 2

ALL = ("rows_0", "rows_1", "cols_0", "cols_1")
VMEM = pl.BlockSpec(memory_space=pltpu.VMEM)
SMEM = pl.BlockSpec(memory_space=pltpu.SMEM)
HBM = pl.BlockSpec(memory_space=pltpu.HBM)


def pairs(first, second):
    out = []
    for y in range(SIDE):
        for x in range(SIDE):
            for z in range(4):
                for core in range(2):
                    dx, dy = (first, second) if core == 0 else (second, first)
                    sy, sx = (y + dy) % SIDE, (x + dx) % SIDE
                    out.append((((sy * 4 + sx) * 4 + z) * 2 + core, ((y * 4 + x) * 4 + z) * 2 + core))
    return out


def fetch(value, first, second):
    return lax.ppermute(value, ALL, pairs(first, second))


def sum_over_cols(part):
    for axis, size in (("cols_1", 2), ("cols_0", 4)):
        step = 1
        while step < size:
            part = part + lax.ppermute(part, axis, [(i, i ^ step) for i in range(size)])
            step *= 2
    return part


OWNERS = (
    ((1, 0), (1, 1), (1, 3), (3, 0), (3, 1), (3, 3), (0, 1), (0, 2), (0, 3)),
    ((2, 0), (2, 1), (2, 3), (2, 2)),
    ((1, 2), (3, 2)),
)


def clear(ref, start, size, value):
    def body(i, _):
        for j in range(8):
            ref[start + 8 * i + j] = value
        return 0

    lax.fori_loop(0, size // 8, body, 0)


def ask_kernel(place, blocks, targets, count, home, requests, codes, rank, fill, base):
    first, second, core = place[0], place[1], place[2]
    clear(rank, 0, 128, -1)
    clear(fill, 0, 16, 0)
    clear(requests, 0, 64, 0)
    base[0] = 0
    for part, owners in enumerate(OWNERS):
        for i, (m, k) in enumerate(owners):
            base[m * SIDE + k] = part * 512 + i * CAP

    def note(t, _):
        slot = home[blocks[t]]
        row = slot >> 6
        local = slot & (BPD - 1)
        y, x = row >> 2, row & (SIDE - 1)
        owner_first = jnp.where(core == 0, x, y)
        owner_second = jnp.where(core == 0, y, x)
        k = (owner_first - first) & (SIDE - 1)
        m = (owner_second - second) & (SIDE - 1)
        pair = m * SIDE + k
        seen = rank[pair * BPD + local]
        held = fill[pair]
        mine = jnp.minimum(jnp.where(seen < 0, held, seen), CAP - 1)
        rank[pair * BPD + local] = mine
        fill[pair] = jnp.where(seen < 0, held + 1, held)
        requests[pair * CAP + mine] = local
        codes[t] = base[pair] + mine + targets[t] * 64
        return 0

    lax.fori_loop(0, count[0], note, 0)


def ask(place, blocks, targets, count, home):
    i32 = jnp.int32
    return pl.pallas_call(
        ask_kernel,
        out_shape=(jax.ShapeDtypeStruct((64,), i32), jax.ShapeDtypeStruct((TILES,), i32)),
        in_specs=[SMEM] * 5,
        out_specs=(SMEM,) * 2,
        scratch_shapes=[pltpu.SMEM((128,), i32), pltpu.SMEM((16,), i32), pltpu.SMEM((16,), i32)],
        compiler_params=pltpu.CompilerParams(vmem_limit_bytes=2 << 20),
        name="ask",
    )(place, blocks, targets, count, home)


def sort_kernel(codes, pattern_ids, count, lists, per_key):
    clear(per_key, 0, KEYS, 0)
    clear(lists, 0, SLOTS, EMPTY)
    clear(lists, SLOTS, SLOTS // 2, 0)

    def tally(t, _):
        key = codes[t] >> 6
        per_key[key] = per_key[key] + 1
        return 0

    lax.fori_loop(0, count[0], tally, 0)
    slot = jnp.int32(0)
    for part, size in enumerate(GROUP):
        lists[STARTS + part] = slot
        start = slot
        for target in range(BPD):
            key = part * BPD + target
            tiles = per_key[key]
            per_key[key] = slot
            slot = slot + ((tiles + size - 1) & -size)
        slot = start + jnp.maximum(2 * size, (slot - start + 2 * size - 1) & -(2 * size))
    lists[STARTS + PARTS] = slot

    def put(t, _):
        code = codes[t]
        key = code >> 6
        at = per_key[key]
        per_key[key] = at + 1
        lists[at] = pattern_ids[t] * 64 + (code & 63)
        lists[SLOTS + (at >> 1)] = key & (BPD - 1)
        return 0

    lax.fori_loop(0, count[0], put, 0)


def sort_tiles(codes, pattern_ids, count):
    i32 = jnp.int32
    return pl.pallas_call(
        sort_kernel,
        out_shape=jax.ShapeDtypeStruct((LIST,), i32),
        in_specs=[SMEM] * 3,
        out_specs=SMEM,
        scratch_shapes=[pltpu.SMEM((KEYS,), i32)],
        compiler_params=pltpu.CompilerParams(vmem_limit_bytes=2 << 20),
        name="sort_tiles",
    )(codes, pattern_ids, count)


def sum_rows(total):
    high = total.astype(jnp.bfloat16).astype(jnp.float32)
    rest = total - high
    middle = rest.astype(jnp.bfloat16).astype(jnp.float32)
    low = rest - middle
    row = lax.broadcasted_iota(jnp.int32, (16, C), 0)
    out = jnp.where(row == 0, high, jnp.where(row == 1, middle, jnp.where(row == 2, low, 0.0)))
    return out.astype(jnp.bfloat16)


def first_kernel(current, sent):
    total = jnp.zeros((8, C), jnp.float32)
    for j in range(BPD):
        rows = current[pl.ds(j * BLOCK, BLOCK), :]
        sent[pl.ds(j * BLOCK, BLOCK), :] = rows.astype(jnp.bfloat16)
        total = total + jnp.sum(rows.reshape(BLOCK // 8, 8, C), axis=0)
    sent[pl.ds(OWN_ROWS, 16), :] = sum_rows(jnp.sum(total, axis=0, keepdims=True))


def first(current):
    return pl.pallas_call(
        first_kernel,
        out_shape=jax.ShapeDtypeStruct((SENT_ROWS, C), jnp.bfloat16),
        in_specs=[VMEM],
        out_specs=VMEM,
        compiler_params=pltpu.CompilerParams(vmem_limit_bytes=20 << 20),
        name="first",
    )(current)


def move(table, local, out, at):
    rows = pl.ds(pl.multiple_of(local * BLOCK, BLOCK), BLOCK)
    out[pl.ds(at * BLOCK, BLOCK), :] = table[rows, :]


def pick_early_kernel(asked, own, far1, far3, pass1, pass3, out1, out3):
    pass1[...] = far1[pl.ds(0, HALF_ROWS), :]
    pass3[...] = far3[pl.ds(HALF_ROWS, HALF_ROWS + 16), :]
    for m, out in ((1, out1), (3, out3)):
        for i, (k, table) in enumerate(((0, own), (1, far1), (3, far3))):
            for r in range(CAP):
                move(table, asked[m - 1, k * CAP + r], out, i * CAP + r)


def pick_early(asked, own, far1, far3):
    b16 = jnp.bfloat16
    out = jax.ShapeDtypeStruct((3 * CAP * BLOCK, C), b16)
    return pl.pallas_call(
        pick_early_kernel,
        out_shape=(
            jax.ShapeDtypeStruct((HALF_ROWS, C), b16),
            jax.ShapeDtypeStruct((HALF_ROWS + 16, C), b16),
            out,
            out,
        ),
        in_specs=[SMEM] + [VMEM] * 3,
        out_specs=(VMEM,) * 4,
        compiler_params=pltpu.CompilerParams(vmem_limit_bytes=20 << 20),
        name="pick_early",
    )(asked, own, far1, far3)


def pick_late_kernel(asked, wanted, own, far1, far3, low2, high2, near, out1, out3, out2, line, far2):
    far2[pl.ds(0, HALF_ROWS), :] = low2[...]
    far2[pl.ds(HALF_ROWS, HALF_ROWS + 16), :] = high2[...]
    tables = ((0, own), (1, far1), (3, far3), (2, far2))
    for r in range(CAP):
        move(far2, asked[0, 2 * CAP + r], out1, r)
        move(far2, asked[2, 2 * CAP + r], out3, r)
    for i, (k, table) in enumerate(tables):
        for r in range(CAP):
            move(table, asked[1, k * CAP + r], out2, i * CAP + r)
            if k > 0:
                move(table, wanted[k * CAP + r], near, (k - 1) * CAP + r)
    rows = sum(t[pl.ds(OWN_ROWS, 16), :].astype(jnp.float32) for _, t in tables)
    sums = jnp.sum(rows, axis=0, keepdims=True)
    line[...] = jnp.broadcast_to(sums, (8, C))


def pick_late(asked, wanted, own, far1, far3, low2, high2):
    b16 = jnp.bfloat16
    piece = jax.ShapeDtypeStruct((CAP * BLOCK, C), b16)
    return pl.pallas_call(
        pick_late_kernel,
        out_shape=(
            jax.ShapeDtypeStruct((3 * CAP * BLOCK, C), b16),
            piece,
            piece,
            jax.ShapeDtypeStruct((PICKED * BLOCK, C), b16),
            jax.ShapeDtypeStruct((8, C), jnp.float32),
        ),
        in_specs=[SMEM] * 2 + [VMEM] * 5,
        out_specs=(VMEM,) * 5,
        scratch_shapes=[pltpu.VMEM((SENT_ROWS, C), b16)],
        compiler_params=pltpu.CompilerParams(vmem_limit_bytes=20 << 20),
        name="pick_late",
    )(asked, wanted, own, far1, far3, low2, high2)


def tile_kernel(part, table_count, resume, finish, *refs):
    refs = list(refs)
    lists, words, own = refs[:3]
    tables = refs[3 : 3 + table_count]
    refs = refs[3 + table_count :]
    if resume:
        earlier = refs.pop(0)
    if finish:
        current, all_sums, fresh = refs[:3]
        refs = refs[3:]
        if finish == "more":
            sent = refs.pop(0)
    if finish == "end":
        ready, sems = refs[:2]
        refs = refs[2:]
    total, score_a, score_b, bits = refs[:4]

    row = lax.broadcasted_iota(jnp.int32, (BLOCK, BLOCK), 0)
    bits[...] = lax.shift_left(jnp.ones_like(row), lax.rem(row, 30))
    total[...] = earlier[...] if resume else jnp.zeros_like(total)
    sub = lax.broadcasted_iota(jnp.int32, (8, BLOCK), 0)
    if table_count == 1:
        held = tables[0]
    else:
        held = refs[4]
        at = 0
        for table in tables:
            held[pl.ds(at, table.shape[0]), :] = table[...]
            at += table.shape[0]

    def rows_of(index):
        return pl.ds(pl.multiple_of(index * BLOCK, BLOCK), BLOCK)

    def word_rows(pattern):
        rows = []
        for v in range(BLOCK // 8):
            low, high = 8 * v // 30, (8 * v + 7) // 30
            chunk = jnp.broadcast_to(words[pattern, low : low + 1, :], (8, BLOCK))
            if high != low:
                other = jnp.broadcast_to(words[pattern, high : high + 1, :], (8, BLOCK))
                chunk = jnp.where(sub + 8 * v < 30 * high, chunk, other)
            rows.append(chunk)
        return jnp.concatenate(rows, axis=0)

    size = GROUP[part]

    def target(slot):
        return rows_of(lists[SLOTS + (slot >> 1)])

    def remote(slot, i):
        return held[rows_of(lists[slot + i] & 63), :]

    def score(slot, out):
        mine = own[target(slot), :]
        for i in range(size):
            out[:, i * BLOCK : (i + 1) * BLOCK] = lax.dot_general(
                mine,
                remote(slot, i),
                (((1,), (1,)), ((), ())),
                preferred_element_type=jnp.float32,
            )

    def add(slot, scores):
        weights = []
        for i in range(size):
            packed = word_rows(lists[slot + i] >> 6)
            negative = jnp.minimum(scores[:, i * BLOCK : (i + 1) * BLOCK] * (-1.0 / UNIT), -FLOOR)
            weight = 1.0 / (1.0 - jnp.exp(negative))
            linked = (packed & bits[...]) != 0
            weights.append(jnp.where(linked, weight, 0.0).astype(jnp.bfloat16))
        total[target(slot), :] += jnp.dot(
            jnp.concatenate(weights, axis=1),
            jnp.concatenate([remote(slot, i) for i in range(size)], axis=0),
            preferred_element_type=jnp.float32,
        )

    start, stop = lists[STARTS + part], lists[STARTS + part + 1]
    score(start, score_a)

    def two(i, _):
        slot = pl.multiple_of(start + 2 * size * i, size)
        score(slot + size, score_b)
        add(slot, score_a)
        score(jnp.minimum(slot + 2 * size, stop - size), score_a)
        add(slot + size, score_b)
        return 0

    lax.fori_loop(0, lax.shift_right_logical(stop - start, size.bit_length()), two, 0)

    if not finish:
        return
    col_sums = all_sums[0:1, :]
    moved_sums = jnp.zeros((8, C), jnp.float32)
    copies = []
    for j in range(BPD):
        at = pl.ds(j * BLOCK, BLOCK)
        moved = jnp.maximum(current[at, :] + STEP_SIZE * (total[at, :] - col_sums), 0.0)
        if finish == "more":
            fresh[at, :] = moved
            sent[at, :] = moved.astype(jnp.bfloat16)
            moved_sums = moved_sums + jnp.sum(moved.reshape(BLOCK // 8, 8, C), axis=0)
        else:
            ready[at, :] = moved
            copies.append(pltpu.make_async_copy(ready.at[at, :], fresh.at[at, :], sems.at[j]))
            copies[j].start()
    if finish == "more":
        sent[pl.ds(OWN_ROWS, 16), :] = sum_rows(jnp.sum(moved_sums, axis=0, keepdims=True))
    for copy in copies:
        copy.wait()


def run_tiles(name, part, lists, words, own, tables, earlier=None, current=None, sums=None, finish=""):
    f32 = jnp.float32
    blocks = jax.ShapeDtypeStruct((OWN_ROWS, C), f32)
    args = [lists, words, own, *tables]
    specs = [SMEM] + [VMEM] * (2 + len(tables))
    scratch = []
    out = [blocks]
    if earlier is not None:
        args.append(earlier)
        specs.append(VMEM)
    if finish:
        args += [current, sums]
        specs += [VMEM] * 2
        if finish == "end":
            scratch += [pltpu.VMEM((OWN_ROWS, C), f32), pltpu.SemaphoreType.DMA((BPD,))]
        scratch.append(pltpu.VMEM((OWN_ROWS, C), f32))
        if finish == "more":
            out.append(jax.ShapeDtypeStruct((SENT_ROWS, C), jnp.bfloat16))
    scratch += [
        pltpu.VMEM((BLOCK, GROUP[part] * BLOCK), f32),
        pltpu.VMEM((BLOCK, GROUP[part] * BLOCK), f32),
        pltpu.VMEM((BLOCK, BLOCK), jnp.int32),
    ]
    if len(tables) > 1:
        scratch.append(pltpu.VMEM((sum(t.shape[0] for t in tables), C), jnp.bfloat16))
    return pl.pallas_call(
        functools.partial(tile_kernel, part, len(tables), earlier is not None, finish),
        out_shape=tuple(out),
        in_specs=specs,
        out_specs=(HBM,) if finish == "end" else (VMEM,) * len(out),
        scratch_shapes=scratch,
        compiler_params=pltpu.CompilerParams(vmem_limit_bytes=24 << 20),
        name=name,
    )(*args)


def per_device(affiliations, tile_block, tile_target, tile_pattern, tile_count, block_home, patterns):
    y, x = lax.axis_index("rows_0"), lax.axis_index("rows_1")
    core = lax.axis_index("cols_1")
    place = jnp.stack([jnp.where(core == 0, x, y), jnp.where(core == 0, y, x), core])
    current = affiliations
    own = first(current)
    requests, codes = ask(
        place.astype(jnp.int32), tile_block[0], tile_target[0], tile_count, block_home
    )
    requests = requests.reshape(SIDE, PICKED)
    asked = jnp.stack([fetch(requests[m], 0, SIDE - m) for m in (1, 2, 3)])
    words = jnp.concatenate([patterns, jnp.zeros((1, *patterns.shape[1:]), jnp.int32)], axis=0)

    lists = sort_tiles(codes, tile_pattern[0], tile_count)
    for step in range(STEPS):
        far1, far3 = fetch(own, 1, 0), fetch(own, 3, 0)
        pass1, pass3, out1, out3 = pick_early(asked, own, far1, far3)
        low2, high2 = fetch(pass1, 1, 0), fetch(pass3, 3, 0)
        side1, side3 = fetch(out1, 0, 1), fetch(out3, 0, 3)
        lists, low2, high2 = lax.optimization_barrier((lists, low2, high2))
        near, out1, out3, out2, line = pick_late(asked, requests[0], own, far1, far3, low2, high2)
        lines = tuple(fetch(line, 0, m) for m in (1, 3, 2))
        lines, out2, side1, side3 = lax.optimization_barrier((lines, out2, side1, side3))
        side2 = fetch(out2, 0, 2)
        late1, late3 = fetch(out1, 0, 1), fetch(out3, 0, 3)
        col_sums = sum_over_cols(line + lines[0] + lines[1] + lines[2])
        tables = (side1, side3, near)
        (total,) = run_tiles("sides", 0, lists, words, own, tables)
        (total,) = run_tiles("across", 1, lists, words, own, (side2,), total)
        total, late1, late3 = lax.optimization_barrier((total, late1, late3))
        finish = "more" if step < STEPS - 1 else "end"
        current, *own_next = run_tiles(
            "late", 2, lists, words, own, (late1, late3), total, current, col_sums, finish
        )
        if own_next:
            (own,) = own_next
    return current


def solution(mesh):
    torus = Mesh(mesh.devices.reshape(4, 4, 4, 2), ALL)
    return jax.shard_map(
        per_device,
        mesh=torus,
        in_specs=(P(ALL, None), P(ALL, None), P(ALL, None), P(ALL, None), P(ALL), P(), P()),
        out_specs=P(ALL, None),
        check_vma=False,
    )
```

```python
import functools

import jax
import jax.numpy as jnp
from jax import lax
from jax.experimental import pallas as pl
from jax.experimental.pallas import tpu as pltpu
from jax.sharding import Mesh
from jax.sharding import PartitionSpec as P

C = 512
BLOCK = 128
STEPS = 2
BPD = 8
SIDE = 4
CAP = 4
N_COLS = 8
NODES = 131072
UNIT = 1572864
PATTERNS = 192
TILES = 240
PARTS = 4
GROUP = (4, 4, 4, 4)
KEYS = PARTS * BPD
SLOTS = TILES + sum(BPD * (g - 1) + 2 * g for g in GROUP) // 16 * 16 + 16
STARTS = SLOTS + SLOTS // 2
LIST = STARTS + 8
EMPTY = PATTERNS * 64
FLOOR = 0.001
STEP_SIZE = 0.3 / NODES
OWN_ROWS = BPD * BLOCK
SENT_ROWS = OWN_ROWS + 16
PICKED = SIDE * CAP
HALF_ROWS = OWN_ROWS // 2

ALL = ("rows_0", "rows_1", "cols_0", "cols_1")
VMEM = pl.BlockSpec(memory_space=pltpu.VMEM)
SMEM = pl.BlockSpec(memory_space=pltpu.SMEM)
HBM = pl.BlockSpec(memory_space=pltpu.HBM)


def pairs(first, second):
    out = []
    for y in range(SIDE):
        for x in range(SIDE):
            for z in range(4):
                for core in range(2):
                    dx, dy = (first, second) if core == 0 else (second, first)
                    sy, sx = (y + dy) % SIDE, (x + dx) % SIDE
                    out.append((((sy * 4 + sx) * 4 + z) * 2 + core, ((y * 4 + x) * 4 + z) * 2 + core))
    return out


def fetch(value, first, second):
    return lax.ppermute(value, ALL, pairs(first, second))


def sum_over_cols(part):
    for axis, size in (("cols_1", 2), ("cols_0", 4)):
        step = 1
        while step < size:
            part = part + lax.ppermute(part, axis, [(i, i ^ step) for i in range(size)])
            step *= 2
    return part


OWNERS = (
    ((1, 0), (1, 1), (1, 3), (3, 0), (3, 1), (3, 3), (0, 1), (0, 2), (0, 3)),
    ((2, 0), (2, 1)),
    ((2, 3), (2, 2)),
    ((1, 2), (3, 2)),
)


def clear(ref, start, size, value):
    def body(i, _):
        for j in range(8):
            ref[start + 8 * i + j] = value
        return 0

    lax.fori_loop(0, size // 8, body, 0)


def ask_kernel(place, blocks, targets, count, home, requests, codes, rank, fill, base):
    first, second, core = place[0], place[1], place[2]
    clear(rank, 0, 128, -1)
    clear(fill, 0, 16, 0)
    clear(requests, 0, 64, 0)
    base[0] = 0
    for part, owners in enumerate(OWNERS):
        for i, (m, k) in enumerate(owners):
            base[m * SIDE + k] = part * 512 + i * CAP

    def note(t, _):
        slot = home[blocks[t]]
        row = slot >> 6
        local = slot & (BPD - 1)
        y, x = row >> 2, row & (SIDE - 1)
        owner_first = jnp.where(core == 0, x, y)
        owner_second = jnp.where(core == 0, y, x)
        k = (owner_first - first) & (SIDE - 1)
        m = (owner_second - second) & (SIDE - 1)
        pair = m * SIDE + k
        seen = rank[pair * BPD + local]
        held = fill[pair]
        mine = jnp.minimum(jnp.where(seen < 0, held, seen), CAP - 1)
        rank[pair * BPD + local] = mine
        fill[pair] = jnp.where(seen < 0, held + 1, held)
        requests[pair * CAP + mine] = local
        codes[t] = base[pair] + mine + targets[t] * 64
        return 0

    lax.fori_loop(0, count[0], note, 0)


def ask(place, blocks, targets, count, home):
    i32 = jnp.int32
    return pl.pallas_call(
        ask_kernel,
        out_shape=(jax.ShapeDtypeStruct((64,), i32), jax.ShapeDtypeStruct((TILES,), i32)),
        in_specs=[SMEM] * 5,
        out_specs=(SMEM,) * 2,
        scratch_shapes=[pltpu.SMEM((128,), i32), pltpu.SMEM((16,), i32), pltpu.SMEM((16,), i32)],
        compiler_params=pltpu.CompilerParams(vmem_limit_bytes=2 << 20),
        name="ask",
    )(place, blocks, targets, count, home)


def sort_kernel(codes, pattern_ids, count, lists, per_key):
    clear(per_key, 0, KEYS, 0)
    clear(lists, 0, SLOTS, EMPTY)
    clear(lists, SLOTS, SLOTS // 2, 0)

    def tally(t, _):
        key = codes[t] >> 6
        per_key[key] = per_key[key] + 1
        return 0

    lax.fori_loop(0, count[0], tally, 0)
    slot = jnp.int32(0)
    for part, size in enumerate(GROUP):
        lists[STARTS + part] = slot
        start = slot
        for target in range(BPD):
            key = part * BPD + target
            tiles = per_key[key]
            per_key[key] = slot
            slot = slot + ((tiles + size - 1) & -size)
        slot = start + jnp.maximum(2 * size, (slot - start + 2 * size - 1) & -(2 * size))
    lists[STARTS + PARTS] = slot

    def put(t, _):
        code = codes[t]
        key = code >> 6
        at = per_key[key]
        per_key[key] = at + 1
        lists[at] = pattern_ids[t] * 64 + (code & 63)
        lists[SLOTS + (at >> 1)] = key & (BPD - 1)
        return 0

    lax.fori_loop(0, count[0], put, 0)


def sort_tiles(codes, pattern_ids, count):
    i32 = jnp.int32
    return pl.pallas_call(
        sort_kernel,
        out_shape=jax.ShapeDtypeStruct((LIST,), i32),
        in_specs=[SMEM] * 3,
        out_specs=SMEM,
        scratch_shapes=[pltpu.SMEM((KEYS,), i32)],
        compiler_params=pltpu.CompilerParams(vmem_limit_bytes=2 << 20),
        name="sort_tiles",
    )(codes, pattern_ids, count)


def sum_rows(total):
    high = total.astype(jnp.bfloat16).astype(jnp.float32)
    rest = total - high
    middle = rest.astype(jnp.bfloat16).astype(jnp.float32)
    low = rest - middle
    row = lax.broadcasted_iota(jnp.int32, (16, C), 0)
    out = jnp.where(row == 0, high, jnp.where(row == 1, middle, jnp.where(row == 2, low, 0.0)))
    return out.astype(jnp.bfloat16)


def first_kernel(current, sent):
    total = jnp.zeros((8, C), jnp.float32)
    for j in range(BPD):
        rows = current[pl.ds(j * BLOCK, BLOCK), :]
        sent[pl.ds(j * BLOCK, BLOCK), :] = rows.astype(jnp.bfloat16)
        total = total + jnp.sum(rows.reshape(BLOCK // 8, 8, C), axis=0)
    sent[pl.ds(OWN_ROWS, 16), :] = sum_rows(jnp.sum(total, axis=0, keepdims=True))


def first(current):
    return pl.pallas_call(
        first_kernel,
        out_shape=jax.ShapeDtypeStruct((SENT_ROWS, C), jnp.bfloat16),
        in_specs=[VMEM],
        out_specs=VMEM,
        compiler_params=pltpu.CompilerParams(vmem_limit_bytes=20 << 20),
        name="first",
    )(current)


def move(table, local, out, at):
    rows = pl.ds(pl.multiple_of(local * BLOCK, BLOCK), BLOCK)
    out[pl.ds(at * BLOCK, BLOCK), :] = table[rows, :]


def pick_early_kernel(asked, own, far1, far3, pass1, pass3, out1, out3):
    pass1[...] = far1[pl.ds(0, HALF_ROWS), :]
    pass3[...] = far3[pl.ds(HALF_ROWS, HALF_ROWS + 16), :]
    for m, out in ((1, out1), (3, out3)):
        for i, (k, table) in enumerate(((0, own), (1, far1), (3, far3))):
            for r in range(CAP):
                move(table, asked[m - 1, k * CAP + r], out, i * CAP + r)


def pick_early(asked, own, far1, far3):
    b16 = jnp.bfloat16
    out = jax.ShapeDtypeStruct((3 * CAP * BLOCK, C), b16)
    return pl.pallas_call(
        pick_early_kernel,
        out_shape=(
            jax.ShapeDtypeStruct((HALF_ROWS, C), b16),
            jax.ShapeDtypeStruct((HALF_ROWS + 16, C), b16),
            out,
            out,
        ),
        in_specs=[SMEM] + [VMEM] * 3,
        out_specs=(VMEM,) * 4,
        compiler_params=pltpu.CompilerParams(vmem_limit_bytes=20 << 20),
        name="pick_early",
    )(asked, own, far1, far3)


def pick_late_kernel(asked, wanted, own, far1, far3, low2, high2, near, out1, out3, out2a, out2b, line, far2):
    far2[pl.ds(0, HALF_ROWS), :] = low2[...]
    far2[pl.ds(HALF_ROWS, HALF_ROWS + 16), :] = high2[...]
    tables = ((0, own), (1, far1), (3, far3), (2, far2))
    for r in range(CAP):
        move(far2, asked[0, 2 * CAP + r], out1, r)
        move(far2, asked[2, 2 * CAP + r], out3, r)
    for i, (k, table) in enumerate(tables):
        for r in range(CAP):
            out, at = (out2a, i) if i < 2 else (out2b, i - 2)
            move(table, asked[1, k * CAP + r], out, at * CAP + r)
            if k > 0:
                move(table, wanted[k * CAP + r], near, (k - 1) * CAP + r)
    rows = sum(t[pl.ds(OWN_ROWS, 16), :].astype(jnp.float32) for _, t in tables)
    sums = jnp.sum(rows, axis=0, keepdims=True)
    line[...] = jnp.broadcast_to(sums, (8, C))


def pick_late(asked, wanted, own, far1, far3, low2, high2):
    b16 = jnp.bfloat16
    piece = jax.ShapeDtypeStruct((CAP * BLOCK, C), b16)
    return pl.pallas_call(
        pick_late_kernel,
        out_shape=(
            jax.ShapeDtypeStruct((3 * CAP * BLOCK, C), b16),
            piece,
            piece,
            jax.ShapeDtypeStruct((2 * CAP * BLOCK, C), b16),
            jax.ShapeDtypeStruct((2 * CAP * BLOCK, C), b16),
            jax.ShapeDtypeStruct((8, C), jnp.float32),
        ),
        in_specs=[SMEM] * 2 + [VMEM] * 5,
        out_specs=(VMEM,) * 6,
        scratch_shapes=[pltpu.VMEM((SENT_ROWS, C), b16)],
        compiler_params=pltpu.CompilerParams(vmem_limit_bytes=20 << 20),
        name="pick_late",
    )(asked, wanted, own, far1, far3, low2, high2)


def tile_kernel(part, table_count, resume, finish, *refs):
    refs = list(refs)
    lists, words, own = refs[:3]
    tables = refs[3 : 3 + table_count]
    refs = refs[3 + table_count :]
    if resume:
        earlier = refs.pop(0)
    if finish:
        current, all_sums, fresh = refs[:3]
        refs = refs[3:]
        if finish == "more":
            sent = refs.pop(0)
    if finish == "end":
        ready, sems = refs[:2]
        refs = refs[2:]
    total, score_a, score_b, bits = refs[:4]

    row = lax.broadcasted_iota(jnp.int32, (BLOCK, BLOCK), 0)
    bits[...] = lax.shift_left(jnp.ones_like(row), lax.rem(row, 30))
    total[...] = earlier[...] if resume else jnp.zeros_like(total)
    sub = lax.broadcasted_iota(jnp.int32, (8, BLOCK), 0)
    if table_count == 1:
        held = tables[0]
    else:
        held = refs[4]
        at = 0
        for table in tables:
            held[pl.ds(at, table.shape[0]), :] = table[...]
            at += table.shape[0]

    def rows_of(index):
        return pl.ds(pl.multiple_of(index * BLOCK, BLOCK), BLOCK)

    def word_rows(pattern):
        rows = []
        for v in range(BLOCK // 8):
            low, high = 8 * v // 30, (8 * v + 7) // 30
            chunk = jnp.broadcast_to(words[pattern, low : low + 1, :], (8, BLOCK))
            if high != low:
                other = jnp.broadcast_to(words[pattern, high : high + 1, :], (8, BLOCK))
                chunk = jnp.where(sub + 8 * v < 30 * high, chunk, other)
            rows.append(chunk)
        return jnp.concatenate(rows, axis=0)

    size = GROUP[part]

    def target(slot):
        return rows_of(lists[SLOTS + (slot >> 1)])

    def remote(slot, i):
        return held[rows_of(lists[slot + i] & 63), :]

    def score(slot, out):
        mine = own[target(slot), :]
        for i in range(size):
            out[:, i * BLOCK : (i + 1) * BLOCK] = lax.dot_general(
                mine,
                remote(slot, i),
                (((1,), (1,)), ((), ())),
                preferred_element_type=jnp.float32,
            )

    def add(slot, scores):
        weights = []
        for i in range(size):
            packed = word_rows(lists[slot + i] >> 6)
            negative = jnp.minimum(scores[:, i * BLOCK : (i + 1) * BLOCK] * (-1.0 / UNIT), -FLOOR)
            weight = 1.0 / (1.0 - jnp.exp(negative))
            linked = (packed & bits[...]) != 0
            weights.append(jnp.where(linked, weight, 0.0).astype(jnp.bfloat16))
        total[target(slot), :] += jnp.dot(
            jnp.concatenate(weights, axis=1),
            jnp.concatenate([remote(slot, i) for i in range(size)], axis=0),
            preferred_element_type=jnp.float32,
        )

    start, stop = lists[STARTS + part], lists[STARTS + part + 1]
    score(start, score_a)

    def two(i, _):
        slot = pl.multiple_of(start + 2 * size * i, size)
        score(slot + size, score_b)
        add(slot, score_a)
        score(jnp.minimum(slot + 2 * size, stop - size), score_a)
        add(slot + size, score_b)
        return 0

    lax.fori_loop(0, lax.shift_right_logical(stop - start, size.bit_length()), two, 0)

    if not finish:
        return
    col_sums = all_sums[0:1, :]
    moved_sums = jnp.zeros((8, C), jnp.float32)
    copies = []
    for j in range(BPD):
        at = pl.ds(j * BLOCK, BLOCK)
        moved = jnp.maximum(current[at, :] + STEP_SIZE * (total[at, :] - col_sums), 0.0)
        if finish == "more":
            fresh[at, :] = moved
            sent[at, :] = moved.astype(jnp.bfloat16)
            moved_sums = moved_sums + jnp.sum(moved.reshape(BLOCK // 8, 8, C), axis=0)
        else:
            ready[at, :] = moved
            copies.append(pltpu.make_async_copy(ready.at[at, :], fresh.at[at, :], sems.at[j]))
            copies[j].start()
    if finish == "more":
        sent[pl.ds(OWN_ROWS, 16), :] = sum_rows(jnp.sum(moved_sums, axis=0, keepdims=True))
    for copy in copies:
        copy.wait()


def run_tiles(name, part, lists, words, own, tables, earlier=None, current=None, sums=None, finish=""):
    f32 = jnp.float32
    blocks = jax.ShapeDtypeStruct((OWN_ROWS, C), f32)
    args = [lists, words, own, *tables]
    specs = [SMEM] + [VMEM] * (2 + len(tables))
    scratch = []
    out = [blocks]
    if earlier is not None:
        args.append(earlier)
        specs.append(VMEM)
    if finish:
        args += [current, sums]
        specs += [VMEM] * 2
        if finish == "end":
            scratch += [pltpu.VMEM((OWN_ROWS, C), f32), pltpu.SemaphoreType.DMA((BPD,))]
        scratch.append(pltpu.VMEM((OWN_ROWS, C), f32))
        if finish == "more":
            out.append(jax.ShapeDtypeStruct((SENT_ROWS, C), jnp.bfloat16))
    scratch += [
        pltpu.VMEM((BLOCK, GROUP[part] * BLOCK), f32),
        pltpu.VMEM((BLOCK, GROUP[part] * BLOCK), f32),
        pltpu.VMEM((BLOCK, BLOCK), jnp.int32),
    ]
    if len(tables) > 1:
        scratch.append(pltpu.VMEM((sum(t.shape[0] for t in tables), C), jnp.bfloat16))
    return pl.pallas_call(
        functools.partial(tile_kernel, part, len(tables), earlier is not None, finish),
        out_shape=tuple(out),
        in_specs=specs,
        out_specs=(HBM,) if finish == "end" else (VMEM,) * len(out),
        scratch_shapes=scratch,
        compiler_params=pltpu.CompilerParams(vmem_limit_bytes=24 << 20),
        name=name,
    )(*args)


def per_device(affiliations, tile_block, tile_target, tile_pattern, tile_count, block_home, patterns):
    y, x = lax.axis_index("rows_0"), lax.axis_index("rows_1")
    core = lax.axis_index("cols_1")
    place = jnp.stack([jnp.where(core == 0, x, y), jnp.where(core == 0, y, x), core])
    current = affiliations
    own = first(current)
    requests, codes = ask(
        place.astype(jnp.int32), tile_block[0], tile_target[0], tile_count, block_home
    )
    requests = requests.reshape(SIDE, PICKED)
    asked = jnp.stack([fetch(requests[m], 0, SIDE - m) for m in (1, 2, 3)])
    words = jnp.concatenate([patterns, jnp.zeros((1, *patterns.shape[1:]), jnp.int32)], axis=0)

    lists = sort_tiles(codes, tile_pattern[0], tile_count)
    for step in range(STEPS):
        far1, far3 = fetch(own, 1, 0), fetch(own, 3, 0)
        pass1, pass3, out1, out3 = pick_early(asked, own, far1, far3)
        low2, high2 = fetch(pass1, 1, 0), fetch(pass3, 3, 0)
        side1, side3 = fetch(out1, 0, 1), fetch(out3, 0, 3)
        lists, low2, high2 = lax.optimization_barrier((lists, low2, high2))
        near, out1, out3, out2a, out2b, line = pick_late(asked, requests[0], own, far1, far3, low2, high2)
        lines = tuple(fetch(line, 0, m) for m in (1, 3, 2))
        lines, out2a, out2b, side1, side3 = lax.optimization_barrier(
            (lines, out2a, out2b, side1, side3)
        )
        side2a, side2b = fetch(out2a, 0, 2), fetch(out2b, 0, 2)
        late1, late3 = fetch(out1, 0, 1), fetch(out3, 0, 3)
        col_sums = sum_over_cols(line + lines[0] + lines[1] + lines[2])
        tables = (side1, side3, near)
        (total,) = run_tiles("sides", 0, lists, words, own, tables)
        (total,) = run_tiles("across", 1, lists, words, own, (side2a,), total)
        total, side2b = lax.optimization_barrier((total, side2b))
        (total,) = run_tiles("across_more", 2, lists, words, own, (side2b,), total)
        total, late1, late3 = lax.optimization_barrier((total, late1, late3))
        finish = "more" if step < STEPS - 1 else "end"
        current, *own_next = run_tiles(
            "late", 3, lists, words, own, (late1, late3), total, current, col_sums, finish
        )
        if own_next:
            (own,) = own_next
    return current


def solution(mesh):
    torus = Mesh(mesh.devices.reshape(4, 4, 4, 2), ALL)
    return jax.shard_map(
        per_device,
        mesh=torus,
        in_specs=(P(ALL, None), P(ALL, None), P(ALL, None), P(ALL, None), P(ALL), P(), P()),
        out_specs=P(ALL, None),
        check_vma=False,
    )
```

```python
import functools

import jax
import jax.numpy as jnp
from jax import lax
from jax.experimental import pallas as pl
from jax.experimental.pallas import tpu as pltpu
from jax.sharding import Mesh
from jax.sharding import PartitionSpec as P

C = 512
BLOCK = 128
STEPS = 2
BPD = 8
SIDE = 4
CAP = 4
N_COLS = 8
NODES = 131072
UNIT = 1572864
PATTERNS = 192
TILES = 240
PARTS = 6
GROUP = (4, 4, 4, 4, 4, 4)
KEYS = PARTS * BPD
SLOTS = TILES + sum(BPD * (g - 1) + 2 * g for g in GROUP) // 16 * 16 + 16
STARTS = SLOTS + SLOTS // 2
LIST = STARTS + 8
EMPTY = PATTERNS * 64
FLOOR = 0.001
STEP_SIZE = 0.3 / NODES
OWN_ROWS = BPD * BLOCK
SENT_ROWS = OWN_ROWS + 16
PICKED = SIDE * CAP
HALF_ROWS = OWN_ROWS // 2

ALL = ("rows_0", "rows_1", "cols_0", "cols_1")
VMEM = pl.BlockSpec(memory_space=pltpu.VMEM)
SMEM = pl.BlockSpec(memory_space=pltpu.SMEM)
HBM = pl.BlockSpec(memory_space=pltpu.HBM)


def pairs(first, second):
    out = []
    for y in range(SIDE):
        for x in range(SIDE):
            for z in range(4):
                for core in range(2):
                    dx, dy = (first, second) if core == 0 else (second, first)
                    sy, sx = (y + dy) % SIDE, (x + dx) % SIDE
                    out.append((((sy * 4 + sx) * 4 + z) * 2 + core, ((y * 4 + x) * 4 + z) * 2 + core))
    return out


def fetch(value, first, second):
    return lax.ppermute(value, ALL, pairs(first, second))


def swap(value, axis, step):
    return lax.ppermute(value, axis, [(i, i ^ step) for i in range(lax.axis_size(axis))])


OWNERS = (
    ((0, 1), (0, 3)),
    ((1, 0), (1, 1), (1, 3), (0, 2)),
    ((3, 0), (3, 1), (3, 3)),
    ((2, 0), (2, 1)),
    ((2, 3), (2, 2)),
    ((1, 2), (3, 2)),
)


def clear(ref, start, size, value):
    def body(i, _):
        for j in range(8):
            ref[start + 8 * i + j] = value
        return 0

    lax.fori_loop(0, size // 8, body, 0)


def ask_kernel(place, blocks, targets, count, home, requests, codes, rank, fill, base):
    first, second, core = place[0], place[1], place[2]
    clear(rank, 0, 128, -1)
    clear(fill, 0, 16, 0)
    clear(requests, 0, 64, 0)
    base[0] = 0
    for part, owners in enumerate(OWNERS):
        for i, (m, k) in enumerate(owners):
            base[m * SIDE + k] = part * 512 + i * CAP

    def note(t, _):
        slot = home[blocks[t]]
        row = slot >> 6
        local = slot & (BPD - 1)
        y, x = row >> 2, row & (SIDE - 1)
        owner_first = jnp.where(core == 0, x, y)
        owner_second = jnp.where(core == 0, y, x)
        k = (owner_first - first) & (SIDE - 1)
        m = (owner_second - second) & (SIDE - 1)
        pair = m * SIDE + k
        seen = rank[pair * BPD + local]
        held = fill[pair]
        mine = jnp.minimum(jnp.where(seen < 0, held, seen), CAP - 1)
        rank[pair * BPD + local] = mine
        fill[pair] = jnp.where(seen < 0, held + 1, held)
        requests[pair * CAP + mine] = local
        codes[t] = base[pair] + mine + targets[t] * 64
        return 0

    lax.fori_loop(0, count[0], note, 0)


def ask(place, blocks, targets, count, home):
    i32 = jnp.int32
    return pl.pallas_call(
        ask_kernel,
        out_shape=(jax.ShapeDtypeStruct((64,), i32), jax.ShapeDtypeStruct((TILES,), i32)),
        in_specs=[SMEM] * 5,
        out_specs=(SMEM,) * 2,
        scratch_shapes=[pltpu.SMEM((128,), i32), pltpu.SMEM((16,), i32), pltpu.SMEM((16,), i32)],
        compiler_params=pltpu.CompilerParams(vmem_limit_bytes=2 << 20),
        name="ask",
    )(place, blocks, targets, count, home)


def sort_kernel(codes, pattern_ids, count, lists, per_key):
    clear(per_key, 0, KEYS, 0)
    clear(lists, 0, SLOTS, EMPTY)
    clear(lists, SLOTS, SLOTS // 2, 0)

    def tally(t, _):
        key = codes[t] >> 6
        per_key[key] = per_key[key] + 1
        return 0

    lax.fori_loop(0, count[0], tally, 0)
    slot = jnp.int32(0)
    for part, size in enumerate(GROUP):
        lists[STARTS + part] = slot
        start = slot
        for target in range(BPD):
            key = part * BPD + target
            tiles = per_key[key]
            per_key[key] = slot
            slot = slot + ((tiles + size - 1) & -size)
        slot = start + jnp.maximum(2 * size, (slot - start + 2 * size - 1) & -(2 * size))
    lists[STARTS + PARTS] = slot

    def put(t, _):
        code = codes[t]
        key = code >> 6
        at = per_key[key]
        per_key[key] = at + 1
        lists[at] = pattern_ids[t] * 64 + (code & 63)
        lists[SLOTS + (at >> 1)] = key & (BPD - 1)
        return 0

    lax.fori_loop(0, count[0], put, 0)


def sort_tiles(codes, pattern_ids, count):
    i32 = jnp.int32
    return pl.pallas_call(
        sort_kernel,
        out_shape=jax.ShapeDtypeStruct((LIST,), i32),
        in_specs=[SMEM] * 3,
        out_specs=SMEM,
        scratch_shapes=[pltpu.SMEM((KEYS,), i32)],
        compiler_params=pltpu.CompilerParams(vmem_limit_bytes=2 << 20),
        name="sort_tiles",
    )(codes, pattern_ids, count)


def sum_rows(total):
    high = total.astype(jnp.bfloat16).astype(jnp.float32)
    rest = total - high
    middle = rest.astype(jnp.bfloat16).astype(jnp.float32)
    low = rest - middle
    row = lax.broadcasted_iota(jnp.int32, (16, C), 0)
    out = jnp.where(row == 0, high, jnp.where(row == 1, middle, jnp.where(row == 2, low, 0.0)))
    return out.astype(jnp.bfloat16)


def first_kernel(current, sent):
    total = jnp.zeros((8, C), jnp.float32)
    for j in range(BPD):
        rows = current[pl.ds(j * BLOCK, BLOCK), :]
        sent[pl.ds(j * BLOCK, BLOCK), :] = rows.astype(jnp.bfloat16)
        total = total + jnp.sum(rows.reshape(BLOCK // 8, 8, C), axis=0)
    sent[pl.ds(OWN_ROWS, 16), :] = sum_rows(jnp.sum(total, axis=0, keepdims=True))


def first(current):
    return pl.pallas_call(
        first_kernel,
        out_shape=jax.ShapeDtypeStruct((SENT_ROWS, C), jnp.bfloat16),
        in_specs=[VMEM],
        out_specs=VMEM,
        compiler_params=pltpu.CompilerParams(vmem_limit_bytes=20 << 20),
        name="first",
    )(current)


def move(table, local, out, at):
    rows = pl.ds(pl.multiple_of(local * BLOCK, BLOCK), BLOCK)
    out[pl.ds(at * BLOCK, BLOCK), :] = table[rows, :]


def pick_early_kernel(asked, wanted, own, far1, far3, near, pass1, pass3, out1, out3):
    pass1[...] = far1[pl.ds(0, HALF_ROWS), :]
    pass3[...] = far3[pl.ds(HALF_ROWS, HALF_ROWS + 16), :]
    for m, out in ((1, out1), (3, out3)):
        for i, (k, table) in enumerate(((0, own), (1, far1), (3, far3))):
            for r in range(CAP):
                move(table, asked[m - 1, k * CAP + r], out, i * CAP + r)
    for r in range(CAP):
        move(far1, wanted[CAP + r], near, r)
        move(far3, wanted[3 * CAP + r], near, CAP + r)


def pick_early(asked, wanted, own, far1, far3):
    b16 = jnp.bfloat16
    out = jax.ShapeDtypeStruct((3 * CAP * BLOCK, C), b16)
    return pl.pallas_call(
        pick_early_kernel,
        out_shape=(
            jax.ShapeDtypeStruct((2 * CAP * BLOCK, C), b16),
            jax.ShapeDtypeStruct((HALF_ROWS, C), b16),
            jax.ShapeDtypeStruct((HALF_ROWS + 16, C), b16),
            out,
            out,
        ),
        in_specs=[SMEM] * 2 + [VMEM] * 3,
        out_specs=(VMEM,) * 5,
        compiler_params=pltpu.CompilerParams(vmem_limit_bytes=20 << 20),
        name="pick_early",
    )(asked, wanted, own, far1, far3)


def pick_late_kernel(asked, wanted, own, far1, far3, low2, high2, near, out1, out3, out2a, out2b, line, far2):
    far2[pl.ds(0, HALF_ROWS), :] = low2[...]
    far2[pl.ds(HALF_ROWS, HALF_ROWS + 16), :] = high2[...]
    tables = ((0, own), (1, far1), (3, far3), (2, far2))
    for r in range(CAP):
        move(far2, asked[0, 2 * CAP + r], out1, r)
        move(far2, asked[2, 2 * CAP + r], out3, r)
        move(far2, wanted[2 * CAP + r], near, r)
    for i, (k, table) in enumerate(tables):
        for r in range(CAP):
            out, at = (out2a, i) if i < 2 else (out2b, i - 2)
            move(table, asked[1, k * CAP + r], out, at * CAP + r)
    rows = sum(t[pl.ds(OWN_ROWS, 16), :].astype(jnp.float32) for _, t in tables)
    sums = jnp.sum(rows, axis=0, keepdims=True)
    line[...] = jnp.broadcast_to(sums, (8, C))


def pick_late(asked, wanted, own, far1, far3, low2, high2):
    b16 = jnp.bfloat16
    piece = jax.ShapeDtypeStruct((CAP * BLOCK, C), b16)
    return pl.pallas_call(
        pick_late_kernel,
        out_shape=(
            piece,
            piece,
            piece,
            jax.ShapeDtypeStruct((2 * CAP * BLOCK, C), b16),
            jax.ShapeDtypeStruct((2 * CAP * BLOCK, C), b16),
            jax.ShapeDtypeStruct((8, C), jnp.float32),
        ),
        in_specs=[SMEM] * 2 + [VMEM] * 5,
        out_specs=(VMEM,) * 6,
        scratch_shapes=[pltpu.VMEM((SENT_ROWS, C), b16)],
        compiler_params=pltpu.CompilerParams(vmem_limit_bytes=20 << 20),
        name="pick_late",
    )(asked, wanted, own, far1, far3, low2, high2)


def tile_kernel(part, table_count, resume, finish, *refs):
    refs = list(refs)
    lists, words, own = refs[:3]
    tables = refs[3 : 3 + table_count]
    refs = refs[3 + table_count :]
    if resume:
        earlier = refs.pop(0)
    if finish:
        current, all_sums, fresh = refs[:3]
        refs = refs[3:]
        if finish == "more":
            sent = refs.pop(0)
    if finish == "end":
        ready, sems = refs[:2]
        refs = refs[2:]
    total, score_a, score_b, bits = refs[:4]

    row = lax.broadcasted_iota(jnp.int32, (BLOCK, BLOCK), 0)
    bits[...] = lax.shift_left(jnp.ones_like(row), lax.rem(row, 30))
    total[...] = earlier[...] if resume else jnp.zeros_like(total)
    sub = lax.broadcasted_iota(jnp.int32, (8, BLOCK), 0)
    if table_count == 1:
        held = tables[0]
    else:
        held = refs[4]
        at = 0
        for table in tables:
            held[pl.ds(at, table.shape[0]), :] = table[...]
            at += table.shape[0]

    def rows_of(index):
        return pl.ds(pl.multiple_of(index * BLOCK, BLOCK), BLOCK)

    def word_rows(pattern):
        rows = []
        for v in range(BLOCK // 8):
            low, high = 8 * v // 30, (8 * v + 7) // 30
            chunk = jnp.broadcast_to(words[pattern, low : low + 1, :], (8, BLOCK))
            if high != low:
                other = jnp.broadcast_to(words[pattern, high : high + 1, :], (8, BLOCK))
                chunk = jnp.where(sub + 8 * v < 30 * high, chunk, other)
            rows.append(chunk)
        return jnp.concatenate(rows, axis=0)

    size = GROUP[part]

    def target(slot):
        return rows_of(lists[SLOTS + (slot >> 1)])

    def remote(slot, i):
        return held[rows_of(lists[slot + i] & 63), :]

    def score(slot, out):
        mine = own[target(slot), :]
        for i in range(size):
            out[:, i * BLOCK : (i + 1) * BLOCK] = lax.dot_general(
                mine,
                remote(slot, i),
                (((1,), (1,)), ((), ())),
                preferred_element_type=jnp.float32,
            )

    def add(slot, scores):
        weights = []
        for i in range(size):
            packed = word_rows(lists[slot + i] >> 6)
            negative = jnp.minimum(scores[:, i * BLOCK : (i + 1) * BLOCK] * (-1.0 / UNIT), -FLOOR)
            weight = 1.0 / (1.0 - jnp.exp(negative))
            linked = (packed & bits[...]) != 0
            weights.append(jnp.where(linked, weight, 0.0).astype(jnp.bfloat16))
        total[target(slot), :] += jnp.dot(
            jnp.concatenate(weights, axis=1),
            jnp.concatenate([remote(slot, i) for i in range(size)], axis=0),
            preferred_element_type=jnp.float32,
        )

    start, stop = lists[STARTS + part], lists[STARTS + part + 1]
    score(start, score_a)

    def two(i, _):
        slot = pl.multiple_of(start + 2 * size * i, size)
        score(slot + size, score_b)
        add(slot, score_a)
        score(jnp.minimum(slot + 2 * size, stop - size), score_a)
        add(slot + size, score_b)
        return 0

    lax.fori_loop(0, lax.shift_right_logical(stop - start, size.bit_length()), two, 0)

    if not finish:
        return
    col_sums = all_sums[0:1, :]
    moved_sums = jnp.zeros((8, C), jnp.float32)
    copies = []
    for j in range(BPD):
        at = pl.ds(j * BLOCK, BLOCK)
        moved = jnp.maximum(current[at, :] + STEP_SIZE * (total[at, :] - col_sums), 0.0)
        if finish == "more":
            fresh[at, :] = moved
            sent[at, :] = moved.astype(jnp.bfloat16)
            moved_sums = moved_sums + jnp.sum(moved.reshape(BLOCK // 8, 8, C), axis=0)
        else:
            ready[at, :] = moved
            copies.append(pltpu.make_async_copy(ready.at[at, :], fresh.at[at, :], sems.at[j]))
            copies[j].start()
    if finish == "more":
        sent[pl.ds(OWN_ROWS, 16), :] = sum_rows(jnp.sum(moved_sums, axis=0, keepdims=True))
    for copy in copies:
        copy.wait()


def run_tiles(name, part, lists, words, own, tables, earlier=None, current=None, sums=None, finish=""):
    f32 = jnp.float32
    blocks = jax.ShapeDtypeStruct((OWN_ROWS, C), f32)
    args = [lists, words, own, *tables]
    specs = [SMEM] + [VMEM] * (2 + len(tables))
    scratch = []
    out = [blocks]
    if earlier is not None:
        args.append(earlier)
        specs.append(VMEM)
    if finish:
        args += [current, sums]
        specs += [VMEM] * 2
        if finish == "end":
            scratch += [pltpu.VMEM((OWN_ROWS, C), f32), pltpu.SemaphoreType.DMA((BPD,))]
        scratch.append(pltpu.VMEM((OWN_ROWS, C), f32))
        if finish == "more":
            out.append(jax.ShapeDtypeStruct((SENT_ROWS, C), jnp.bfloat16))
    scratch += [
        pltpu.VMEM((BLOCK, GROUP[part] * BLOCK), f32),
        pltpu.VMEM((BLOCK, GROUP[part] * BLOCK), f32),
        pltpu.VMEM((BLOCK, BLOCK), jnp.int32),
    ]
    if len(tables) > 1:
        scratch.append(pltpu.VMEM((sum(t.shape[0] for t in tables), C), jnp.bfloat16))
    return pl.pallas_call(
        functools.partial(tile_kernel, part, len(tables), earlier is not None, finish),
        out_shape=tuple(out),
        in_specs=specs,
        out_specs=(HBM,) if finish == "end" else (VMEM,) * len(out),
        scratch_shapes=scratch,
        compiler_params=pltpu.CompilerParams(vmem_limit_bytes=24 << 20),
        name=name,
    )(*args)


def per_device(affiliations, tile_block, tile_target, tile_pattern, tile_count, block_home, patterns):
    y, x = lax.axis_index("rows_0"), lax.axis_index("rows_1")
    core = lax.axis_index("cols_1")
    place = jnp.stack([jnp.where(core == 0, x, y), jnp.where(core == 0, y, x), core])
    current = affiliations
    own = first(current)
    requests, codes = ask(
        place.astype(jnp.int32), tile_block[0], tile_target[0], tile_count, block_home
    )
    requests = requests.reshape(SIDE, PICKED)
    asked = jnp.stack([fetch(requests[m], 0, SIDE - m) for m in (1, 2, 3)])
    words = jnp.concatenate([patterns, jnp.zeros((1, *patterns.shape[1:]), jnp.int32)], axis=0)

    lists = sort_tiles(codes, tile_pattern[0], tile_count)
    for step in range(STEPS):
        far1, far3 = fetch(own, 1, 0), fetch(own, 3, 0)
        near, pass1, pass3, out1, out3 = pick_early(asked, requests[0], own, far1, far3)
        low2, high2 = fetch(pass1, 1, 0), fetch(pass3, 3, 0)
        side1, side3 = fetch(out1, 0, 1), fetch(out3, 0, 3)
        (total,) = run_tiles("near", 0, lists, words, own, (near,))
        total, low2, high2 = lax.optimization_barrier((total, low2, high2))
        near, out1, out3, out2a, out2b, line = pick_late(asked, requests[0], own, far1, far3, low2, high2)
        lines = tuple(fetch(line, 0, m) for m in (1, 3, 2))
        lines, out2a, out2b, side1, side3 = lax.optimization_barrier(
            (lines, out2a, out2b, side1, side3)
        )
        side2a, side2b = fetch(out2a, 0, 2), fetch(out2b, 0, 2)
        late1, late3 = fetch(out1, 0, 1), fetch(out3, 0, 3)
        sums = line + lines[0] + lines[1] + lines[2]
        other = swap(sums, "cols_1", 1)
        (total,) = run_tiles("sides_1", 1, lists, words, own, (side1, near), total)
        total, other = lax.optimization_barrier((total, other))
        sums = sums + other
        other = swap(sums, "cols_0", 1)
        (total,) = run_tiles("sides_3", 2, lists, words, own, (side3,), total)
        total, other = lax.optimization_barrier((total, other))
        sums = sums + other
        col_sums = sums + swap(sums, "cols_0", 2)
        (total,) = run_tiles("across", 3, lists, words, own, (side2a,), total)
        total, side2b = lax.optimization_barrier((total, side2b))
        (total,) = run_tiles("across_more", 4, lists, words, own, (side2b,), total)
        total, late1, late3 = lax.optimization_barrier((total, late1, late3))
        finish = "more" if step < STEPS - 1 else "end"
        current, *own_next = run_tiles(
            "late", 5, lists, words, own, (late1, late3), total, current, col_sums, finish
        )
        if own_next:
            (own,) = own_next
    return current


def solution(mesh):
    torus = Mesh(mesh.devices.reshape(4, 4, 4, 2), ALL)
    return jax.shard_map(
        per_device,
        mesh=torus,
        in_specs=(P(ALL, None), P(ALL, None), P(ALL, None), P(ALL, None), P(ALL), P(), P()),
        out_specs=P(ALL, None),
        check_vma=False,
    )
```

```python
import functools

import jax
import jax.numpy as jnp
from jax import lax
from jax.experimental import pallas as pl
from jax.experimental.pallas import tpu as pltpu
from jax.sharding import Mesh
from jax.sharding import PartitionSpec as P

C = 512
BLOCK = 128
STEPS = 2
BPD = 8
SIDE = 4
CAP = 4
N_COLS = 8
NODES = 131072
UNIT = 1572864
PATTERNS = 192
TILES = 240
PARTS = 5
GROUP = (4, 4, 4, 4, 4)
KEYS = PARTS * BPD
SLOTS = TILES + sum(BPD * (g - 1) + 2 * g for g in GROUP) // 16 * 16 + 16
STARTS = SLOTS + SLOTS // 2
LIST = STARTS + 8
EMPTY = PATTERNS * 64
FLOOR = 0.001
STEP_SIZE = 0.3 / NODES
OWN_ROWS = BPD * BLOCK
SENT_ROWS = OWN_ROWS + 16
PICKED = SIDE * CAP
HALF_ROWS = OWN_ROWS // 2

ALL = ("rows_0", "rows_1", "cols_0", "cols_1")
VMEM = pl.BlockSpec(memory_space=pltpu.VMEM)
SMEM = pl.BlockSpec(memory_space=pltpu.SMEM)
HBM = pl.BlockSpec(memory_space=pltpu.HBM)


def pairs(first, second):
    out = []
    for y in range(SIDE):
        for x in range(SIDE):
            for z in range(4):
                for core in range(2):
                    dx, dy = (first, second) if core == 0 else (second, first)
                    sy, sx = (y + dy) % SIDE, (x + dx) % SIDE
                    out.append((((sy * 4 + sx) * 4 + z) * 2 + core, ((y * 4 + x) * 4 + z) * 2 + core))
    return out


def fetch(value, first, second):
    return lax.ppermute(value, ALL, pairs(first, second))


def swap(value, axis, step):
    return lax.ppermute(value, axis, [(i, i ^ step) for i in range(lax.axis_size(axis))])


OWNERS = (
    ((0, 1), (0, 3)),
    ((1, 0), (1, 1), (1, 3), (0, 2)),
    ((3, 0), (3, 1), (3, 3), (1, 2), (3, 2)),
    ((2, 0), (2, 1)),
    ((2, 3), (2, 2)),
)


def clear(ref, start, size, value):
    def body(i, _):
        for j in range(8):
            ref[start + 8 * i + j] = value
        return 0

    lax.fori_loop(0, size // 8, body, 0)


def ask_kernel(place, blocks, targets, count, home, requests, codes, rank, fill, base):
    first, second, core = place[0], place[1], place[2]
    clear(rank, 0, 128, -1)
    clear(fill, 0, 16, 0)
    clear(requests, 0, 64, 0)
    base[0] = 0
    for part, owners in enumerate(OWNERS):
        for i, (m, k) in enumerate(owners):
            base[m * SIDE + k] = part * 512 + i * CAP

    def note(t, _):
        slot = home[blocks[t]]
        row = slot >> 6
        local = slot & (BPD - 1)
        y, x = row >> 2, row & (SIDE - 1)
        owner_first = jnp.where(core == 0, x, y)
        owner_second = jnp.where(core == 0, y, x)
        k = (owner_first - first) & (SIDE - 1)
        m = (owner_second - second) & (SIDE - 1)
        pair = m * SIDE + k
        seen = rank[pair * BPD + local]
        held = fill[pair]
        mine = jnp.minimum(jnp.where(seen < 0, held, seen), CAP - 1)
        rank[pair * BPD + local] = mine
        fill[pair] = jnp.where(seen < 0, held + 1, held)
        requests[pair * CAP + mine] = local
        codes[t] = base[pair] + mine + targets[t] * 64
        return 0

    lax.fori_loop(0, count[0], note, 0)


def ask(place, blocks, targets, count, home):
    i32 = jnp.int32
    return pl.pallas_call(
        ask_kernel,
        out_shape=(jax.ShapeDtypeStruct((64,), i32), jax.ShapeDtypeStruct((TILES,), i32)),
        in_specs=[SMEM] * 5,
        out_specs=(SMEM,) * 2,
        scratch_shapes=[pltpu.SMEM((128,), i32), pltpu.SMEM((16,), i32), pltpu.SMEM((16,), i32)],
        compiler_params=pltpu.CompilerParams(vmem_limit_bytes=2 << 20),
        name="ask",
    )(place, blocks, targets, count, home)


def sort_kernel(codes, pattern_ids, count, lists, per_key):
    clear(per_key, 0, KEYS, 0)
    clear(lists, 0, SLOTS, EMPTY)
    clear(lists, SLOTS, SLOTS // 2, 0)

    def tally(t, _):
        key = codes[t] >> 6
        per_key[key] = per_key[key] + 1
        return 0

    lax.fori_loop(0, count[0], tally, 0)
    slot = jnp.int32(0)
    for part, size in enumerate(GROUP):
        lists[STARTS + part] = slot
        start = slot
        for target in range(BPD):
            key = part * BPD + target
            tiles = per_key[key]
            per_key[key] = slot
            slot = slot + ((tiles + size - 1) & -size)
        slot = start + jnp.maximum(2 * size, (slot - start + 2 * size - 1) & -(2 * size))
    lists[STARTS + PARTS] = slot

    def put(t, _):
        code = codes[t]
        key = code >> 6
        at = per_key[key]
        per_key[key] = at + 1
        lists[at] = pattern_ids[t] * 64 + (code & 63)
        lists[SLOTS + (at >> 1)] = key & (BPD - 1)
        return 0

    lax.fori_loop(0, count[0], put, 0)


def sort_tiles(codes, pattern_ids, count):
    i32 = jnp.int32
    return pl.pallas_call(
        sort_kernel,
        out_shape=jax.ShapeDtypeStruct((LIST,), i32),
        in_specs=[SMEM] * 3,
        out_specs=SMEM,
        scratch_shapes=[pltpu.SMEM((KEYS,), i32)],
        compiler_params=pltpu.CompilerParams(vmem_limit_bytes=2 << 20),
        name="sort_tiles",
    )(codes, pattern_ids, count)


def sum_rows(total):
    high = total.astype(jnp.bfloat16).astype(jnp.float32)
    rest = total - high
    middle = rest.astype(jnp.bfloat16).astype(jnp.float32)
    low = rest - middle
    row = lax.broadcasted_iota(jnp.int32, (16, C), 0)
    out = jnp.where(row == 0, high, jnp.where(row == 1, middle, jnp.where(row == 2, low, 0.0)))
    return out.astype(jnp.bfloat16)


def first_kernel(current, sent):
    total = jnp.zeros((8, C), jnp.float32)
    for j in range(BPD):
        rows = current[pl.ds(j * BLOCK, BLOCK), :]
        sent[pl.ds(j * BLOCK, BLOCK), :] = rows.astype(jnp.bfloat16)
        total = total + jnp.sum(rows.reshape(BLOCK // 8, 8, C), axis=0)
    sent[pl.ds(OWN_ROWS, 16), :] = sum_rows(jnp.sum(total, axis=0, keepdims=True))


def first(current):
    return pl.pallas_call(
        first_kernel,
        out_shape=jax.ShapeDtypeStruct((SENT_ROWS, C), jnp.bfloat16),
        in_specs=[VMEM],
        out_specs=VMEM,
        compiler_params=pltpu.CompilerParams(vmem_limit_bytes=20 << 20),
        name="first",
    )(current)


def move(table, local, out, at):
    rows = pl.ds(pl.multiple_of(local * BLOCK, BLOCK), BLOCK)
    out[pl.ds(at * BLOCK, BLOCK), :] = table[rows, :]


def pick_early_kernel(asked, wanted, own, far1, far3, near, pass1, pass3, out1, out3):
    pass1[...] = far1[pl.ds(0, HALF_ROWS), :]
    pass3[...] = far3[pl.ds(HALF_ROWS, HALF_ROWS + 16), :]
    for m, out in ((1, out1), (3, out3)):
        for i, (k, table) in enumerate(((0, own), (1, far1), (3, far3))):
            for r in range(CAP):
                move(table, asked[m - 1, k * CAP + r], out, i * CAP + r)
    for r in range(CAP):
        move(far1, wanted[CAP + r], near, r)
        move(far3, wanted[3 * CAP + r], near, CAP + r)


def pick_early(asked, wanted, own, far1, far3):
    b16 = jnp.bfloat16
    out = jax.ShapeDtypeStruct((3 * CAP * BLOCK, C), b16)
    return pl.pallas_call(
        pick_early_kernel,
        out_shape=(
            jax.ShapeDtypeStruct((2 * CAP * BLOCK, C), b16),
            jax.ShapeDtypeStruct((HALF_ROWS, C), b16),
            jax.ShapeDtypeStruct((HALF_ROWS + 16, C), b16),
            out,
            out,
        ),
        in_specs=[SMEM] * 2 + [VMEM] * 3,
        out_specs=(VMEM,) * 5,
        compiler_params=pltpu.CompilerParams(vmem_limit_bytes=20 << 20),
        name="pick_early",
    )(asked, wanted, own, far1, far3)


def pick_late_kernel(asked, wanted, own, far1, far3, low2, high2, near, out1, out3, out2a, out2b, line, far2):
    far2[pl.ds(0, HALF_ROWS), :] = low2[...]
    far2[pl.ds(HALF_ROWS, HALF_ROWS + 16), :] = high2[...]
    tables = ((0, own), (1, far1), (3, far3), (2, far2))
    for r in range(CAP):
        move(far2, asked[0, 2 * CAP + r], out1, r)
        move(far2, asked[2, 2 * CAP + r], out3, r)
        move(far2, wanted[2 * CAP + r], near, r)
    for i, (k, table) in enumerate(tables):
        for r in range(CAP):
            out, at = (out2a, i) if i < 2 else (out2b, i - 2)
            move(table, asked[1, k * CAP + r], out, at * CAP + r)
    rows = sum(t[pl.ds(OWN_ROWS, 16), :].astype(jnp.float32) for _, t in tables)
    sums = jnp.sum(rows, axis=0, keepdims=True)
    line[...] = jnp.broadcast_to(sums, (8, C))
    for out in (out1, out3):
        out[pl.ds(CAP * BLOCK, 16), :] = sum_rows(sums)


def pick_late(asked, wanted, own, far1, far3, low2, high2):
    b16 = jnp.bfloat16
    piece = jax.ShapeDtypeStruct((CAP * BLOCK, C), b16)
    with_sums = jax.ShapeDtypeStruct((CAP * BLOCK + 16, C), b16)
    double = jax.ShapeDtypeStruct((2 * CAP * BLOCK, C), b16)
    return pl.pallas_call(
        pick_late_kernel,
        out_shape=(piece, with_sums, with_sums, double, double, jax.ShapeDtypeStruct((8, C), jnp.float32)),
        in_specs=[SMEM] * 2 + [VMEM] * 5,
        out_specs=(VMEM,) * 6,
        scratch_shapes=[pltpu.VMEM((SENT_ROWS, C), b16)],
        compiler_params=pltpu.CompilerParams(vmem_limit_bytes=20 << 20),
        name="pick_late",
    )(asked, wanted, own, far1, far3, low2, high2)


def tile_kernel(part, table_count, resume, finish, *refs):
    refs = list(refs)
    lists, words, own = refs[:3]
    tables = refs[3 : 3 + table_count]
    refs = refs[3 + table_count :]
    if resume:
        earlier = refs.pop(0)
    if finish:
        current, chain, cross, fresh = refs[:4]
        refs = refs[4:]
        if finish == "more":
            sent = refs.pop(0)
    if finish == "end":
        ready, sems = refs[:2]
        refs = refs[2:]
    total, score_a, score_b, bits = refs[:4]

    row = lax.broadcasted_iota(jnp.int32, (BLOCK, BLOCK), 0)
    bits[...] = lax.shift_left(jnp.ones_like(row), lax.rem(row, 30))
    total[...] = earlier[...] if resume else jnp.zeros_like(total)
    sub = lax.broadcasted_iota(jnp.int32, (8, BLOCK), 0)
    if table_count == 1:
        held = tables[0]
    else:
        held = refs[4]
        at = 0
        for table in tables:
            rows = table.shape[0] // BLOCK * BLOCK
            held[pl.ds(at, rows), :] = table[pl.ds(0, rows), :]
            at += rows

    def rows_of(index):
        return pl.ds(pl.multiple_of(index * BLOCK, BLOCK), BLOCK)

    def word_rows(pattern):
        rows = []
        for v in range(BLOCK // 8):
            low, high = 8 * v // 30, (8 * v + 7) // 30
            chunk = jnp.broadcast_to(words[pattern, low : low + 1, :], (8, BLOCK))
            if high != low:
                other = jnp.broadcast_to(words[pattern, high : high + 1, :], (8, BLOCK))
                chunk = jnp.where(sub + 8 * v < 30 * high, chunk, other)
            rows.append(chunk)
        return jnp.concatenate(rows, axis=0)

    size = GROUP[part]

    def target(slot):
        return rows_of(lists[SLOTS + (slot >> 1)])

    def remote(slot, i):
        return held[rows_of(lists[slot + i] & 63), :]

    def score(slot, out):
        mine = own[target(slot), :]
        for i in range(size):
            out[:, i * BLOCK : (i + 1) * BLOCK] = lax.dot_general(
                mine,
                remote(slot, i),
                (((1,), (1,)), ((), ())),
                preferred_element_type=jnp.float32,
            )

    def add(slot, scores):
        weights = []
        for i in range(size):
            packed = word_rows(lists[slot + i] >> 6)
            negative = jnp.minimum(scores[:, i * BLOCK : (i + 1) * BLOCK] * (-1.0 / UNIT), -FLOOR)
            weight = 1.0 / (1.0 - jnp.exp(negative))
            linked = (packed & bits[...]) != 0
            weights.append(jnp.where(linked, weight, 0.0).astype(jnp.bfloat16))
        total[target(slot), :] += jnp.dot(
            jnp.concatenate(weights, axis=1),
            jnp.concatenate([remote(slot, i) for i in range(size)], axis=0),
            preferred_element_type=jnp.float32,
        )

    start, stop = lists[STARTS + part], lists[STARTS + part + 1]
    score(start, score_a)

    def two(i, _):
        slot = pl.multiple_of(start + 2 * size * i, size)
        score(slot + size, score_b)
        add(slot, score_a)
        score(jnp.minimum(slot + 2 * size, stop - size), score_a)
        add(slot + size, score_b)
        return 0

    lax.fori_loop(0, lax.shift_right_logical(stop - start, size.bit_length()), two, 0)

    if not finish:
        return
    col_sums = chain[0:1, :] + cross[4:5, :]
    moved_sums = jnp.zeros((8, C), jnp.float32)
    copies = []
    for j in range(BPD):
        at = pl.ds(j * BLOCK, BLOCK)
        moved = jnp.maximum(current[at, :] + STEP_SIZE * (total[at, :] - col_sums), 0.0)
        if finish == "more":
            fresh[at, :] = moved
            sent[at, :] = moved.astype(jnp.bfloat16)
            moved_sums = moved_sums + jnp.sum(moved.reshape(BLOCK // 8, 8, C), axis=0)
        else:
            ready[at, :] = moved
            copies.append(pltpu.make_async_copy(ready.at[at, :], fresh.at[at, :], sems.at[j]))
            copies[j].start()
    if finish == "more":
        sent[pl.ds(OWN_ROWS, 16), :] = sum_rows(jnp.sum(moved_sums, axis=0, keepdims=True))
    for copy in copies:
        copy.wait()


def run_tiles(name, part, lists, words, own, tables, earlier=None, current=None, sums=(), finish=""):
    f32 = jnp.float32
    blocks = jax.ShapeDtypeStruct((OWN_ROWS, C), f32)
    args = [lists, words, own, *tables]
    specs = [SMEM] + [VMEM] * (2 + len(tables))
    scratch = []
    out = [blocks]
    if earlier is not None:
        args.append(earlier)
        specs.append(VMEM)
    if finish:
        args += [current, *sums]
        specs += [VMEM] * 3
        if finish == "end":
            scratch += [pltpu.VMEM((OWN_ROWS, C), f32), pltpu.SemaphoreType.DMA((BPD,))]
        scratch.append(pltpu.VMEM((OWN_ROWS, C), f32))
        if finish == "more":
            out.append(jax.ShapeDtypeStruct((SENT_ROWS, C), jnp.bfloat16))
    scratch += [
        pltpu.VMEM((BLOCK, GROUP[part] * BLOCK), f32),
        pltpu.VMEM((BLOCK, GROUP[part] * BLOCK), f32),
        pltpu.VMEM((BLOCK, BLOCK), jnp.int32),
    ]
    if len(tables) > 1:
        scratch.append(pltpu.VMEM((sum(t.shape[0] for t in tables), C), jnp.bfloat16))
    return pl.pallas_call(
        functools.partial(tile_kernel, part, len(tables), earlier is not None, finish),
        out_shape=tuple(out),
        in_specs=specs,
        out_specs=(HBM,) if finish == "end" else (VMEM,) * len(out),
        scratch_shapes=scratch,
        compiler_params=pltpu.CompilerParams(vmem_limit_bytes=24 << 20),
        name=name,
    )(*args)


def line_sums(line, side1, side3):
    rows = sum(t[CAP * BLOCK :].astype(jnp.float32) for t in (side1, side3))
    beside = jnp.sum(rows, axis=0, keepdims=True)
    return line + jnp.where(jnp.arange(8)[:, None] < 4, beside, 0.0)


def per_device(affiliations, tile_block, tile_target, tile_pattern, tile_count, block_home, patterns):
    y, x = lax.axis_index("rows_0"), lax.axis_index("rows_1")
    core = lax.axis_index("cols_1")
    place = jnp.stack([jnp.where(core == 0, x, y), jnp.where(core == 0, y, x), core])
    current = affiliations
    own = first(current)
    requests, codes = ask(
        place.astype(jnp.int32), tile_block[0], tile_target[0], tile_count, block_home
    )
    requests = requests.reshape(SIDE, PICKED)
    asked = jnp.stack([fetch(requests[m], 0, SIDE - m) for m in (1, 2, 3)])
    words = jnp.concatenate([patterns, jnp.zeros((1, *patterns.shape[1:]), jnp.int32)], axis=0)

    lists = sort_tiles(codes, tile_pattern[0], tile_count)
    for step in range(STEPS):
        far1, far3 = fetch(own, 1, 0), fetch(own, 3, 0)
        near, pass1, pass3, out1, out3 = pick_early(asked, requests[0], own, far1, far3)
        low2, high2 = fetch(pass1, 1, 0), fetch(pass3, 3, 0)
        side1, side3 = fetch(out1, 0, 1), fetch(out3, 0, 3)
        (total,) = run_tiles("near", 0, lists, words, own, (near,))
        total, low2, high2 = lax.optimization_barrier((total, low2, high2))
        near, out1, out3, *out2, line = pick_late(
            asked, requests[0], own, far1, far3, low2, high2
        )
        late1, late3 = fetch(out1, 0, 1), fetch(out3, 0, 3)
        out2, side1, side3 = lax.optimization_barrier((out2, side1, side3))
        side2 = [fetch(piece, 0, 2) for piece in out2]
        (total,) = run_tiles("sides_1", 1, lists, words, own, (side1, near), total)
        total, late1, late3 = lax.optimization_barrier((total, late1, late3))
        sums = line_sums(line, late1, late3)
        other = swap(sums, "cols_1", 1)
        (total,) = run_tiles("sides_3", 2, lists, words, own, (side3, late1, late3), total)
        total, other = lax.optimization_barrier((total, other))
        sums = sums + other
        sums = sums + swap(sums, "cols_0", 1)
        sums = sums + swap(sums, "cols_0", 2)
        cross = fetch(sums, 2, 2)
        (total,) = run_tiles("across", 3, lists, words, own, side2[:1], total)
        total, last = lax.optimization_barrier((total, side2[1:]))
        finish = "more" if step < STEPS - 1 else "end"
        current, *own_next = run_tiles(
            "late", 4, lists, words, own, last, total, current, (sums, cross), finish
        )
        if own_next:
            (own,) = own_next
    return current


def solution(mesh):
    torus = Mesh(mesh.devices.reshape(4, 4, 4, 2), ALL)
    return jax.shard_map(
        per_device,
        mesh=torus,
        in_specs=(P(ALL, None), P(ALL, None), P(ALL, None), P(ALL, None), P(ALL), P(), P()),
        out_specs=P(ALL, None),
        check_vma=False,
    )
```

```python
import functools

import jax
import jax.numpy as jnp
from jax import lax
from jax.experimental import pallas as pl
from jax.experimental.pallas import tpu as pltpu
from jax.sharding import Mesh
from jax.sharding import PartitionSpec as P

C = 512
BLOCK = 128
STEPS = 2
BPD = 8
SIDE = 4
CAP = 4
N_COLS = 8
NODES = 131072
UNIT = 1572864
PATTERNS = 192
TILES = 240
PARTS = 6
GROUP = (4, 4, 4, 4, 4, 4)
KEYS = PARTS * BPD
SLOTS = TILES + sum(BPD * (g - 1) + 2 * g for g in GROUP) // 16 * 16 + 16
STARTS = SLOTS + SLOTS // 2
LIST = STARTS + 8
EMPTY = PATTERNS * 64
FLOOR = 0.001
STEP_SIZE = 0.3 / NODES
OWN_ROWS = BPD * BLOCK
SENT_ROWS = OWN_ROWS + 16
PICKED = SIDE * CAP
HALF_ROWS = OWN_ROWS // 2

ALL = ("rows_0", "rows_1", "cols_0", "cols_1")
VMEM = pl.BlockSpec(memory_space=pltpu.VMEM)
SMEM = pl.BlockSpec(memory_space=pltpu.SMEM)
HBM = pl.BlockSpec(memory_space=pltpu.HBM)


def pairs(first, second):
    out = []
    for y in range(SIDE):
        for x in range(SIDE):
            for z in range(4):
                for core in range(2):
                    dx, dy = (first, second) if core == 0 else (second, first)
                    sy, sx = (y + dy) % SIDE, (x + dx) % SIDE
                    out.append((((sy * 4 + sx) * 4 + z) * 2 + core, ((y * 4 + x) * 4 + z) * 2 + core))
    return out


def fetch(value, first, second):
    return lax.ppermute(value, ALL, pairs(first, second))


def swap(value, axis, step):
    return lax.ppermute(value, axis, [(i, i ^ step) for i in range(lax.axis_size(axis))])


OWNERS = (
    ((0, 1), (0, 3)),
    ((1, 0), (1, 1), (1, 3), (0, 2)),
    ((3, 0), (3, 1), (3, 3)),
    ((2, 0), (2, 1), (2, 3)),
    ((1, 2), (3, 2)),
    ((2, 2),),
)


def clear(ref, start, size, value):
    def body(i, _):
        for j in range(8):
            ref[start + 8 * i + j] = value
        return 0

    lax.fori_loop(0, size // 8, body, 0)


def ask_kernel(place, blocks, targets, count, home, requests, codes, rank, fill, base):
    first, second, core = place[0], place[1], place[2]
    clear(rank, 0, 128, -1)
    clear(fill, 0, 16, 0)
    clear(requests, 0, 64, 0)
    base[0] = 0
    for part, owners in enumerate(OWNERS):
        for i, (m, k) in enumerate(owners):
            base[m * SIDE + k] = part * 512 + i * CAP

    def note(t, _):
        slot = home[blocks[t]]
        row = slot >> 6
        local = slot & (BPD - 1)
        y, x = row >> 2, row & (SIDE - 1)
        owner_first = jnp.where(core == 0, x, y)
        owner_second = jnp.where(core == 0, y, x)
        k = (owner_first - first) & (SIDE - 1)
        m = (owner_second - second) & (SIDE - 1)
        pair = m * SIDE + k
        seen = rank[pair * BPD + local]
        held = fill[pair]
        mine = jnp.minimum(jnp.where(seen < 0, held, seen), CAP - 1)
        rank[pair * BPD + local] = mine
        fill[pair] = jnp.where(seen < 0, held + 1, held)
        requests[pair * CAP + mine] = local
        codes[t] = base[pair] + mine + targets[t] * 64
        return 0

    lax.fori_loop(0, count[0], note, 0)


def ask(place, blocks, targets, count, home):
    i32 = jnp.int32
    return pl.pallas_call(
        ask_kernel,
        out_shape=(jax.ShapeDtypeStruct((64,), i32), jax.ShapeDtypeStruct((TILES,), i32)),
        in_specs=[SMEM] * 5,
        out_specs=(SMEM,) * 2,
        scratch_shapes=[pltpu.SMEM((128,), i32), pltpu.SMEM((16,), i32), pltpu.SMEM((16,), i32)],
        compiler_params=pltpu.CompilerParams(vmem_limit_bytes=2 << 20),
        name="ask",
    )(place, blocks, targets, count, home)


def sort_kernel(codes, pattern_ids, count, lists, per_key):
    clear(per_key, 0, KEYS, 0)
    clear(lists, 0, SLOTS, EMPTY)
    clear(lists, SLOTS, SLOTS // 2, 0)

    def tally(t, _):
        key = codes[t] >> 6
        per_key[key] = per_key[key] + 1
        return 0

    lax.fori_loop(0, count[0], tally, 0)
    slot = jnp.int32(0)
    for part, size in enumerate(GROUP):
        lists[STARTS + part] = slot
        start = slot
        for target in range(BPD):
            key = part * BPD + target
            tiles = per_key[key]
            per_key[key] = slot
            slot = slot + ((tiles + size - 1) & -size)
        slot = start + jnp.maximum(2 * size, (slot - start + 2 * size - 1) & -(2 * size))
    lists[STARTS + PARTS] = slot

    def put(t, _):
        code = codes[t]
        key = code >> 6
        at = per_key[key]
        per_key[key] = at + 1
        lists[at] = pattern_ids[t] * 64 + (code & 63)
        lists[SLOTS + (at >> 1)] = key & (BPD - 1)
        return 0

    lax.fori_loop(0, count[0], put, 0)


def sort_tiles(codes, pattern_ids, count):
    i32 = jnp.int32
    return pl.pallas_call(
        sort_kernel,
        out_shape=jax.ShapeDtypeStruct((LIST,), i32),
        in_specs=[SMEM] * 3,
        out_specs=SMEM,
        scratch_shapes=[pltpu.SMEM((KEYS,), i32)],
        compiler_params=pltpu.CompilerParams(vmem_limit_bytes=2 << 20),
        name="sort_tiles",
    )(codes, pattern_ids, count)


def sum_rows(total):
    high = total.astype(jnp.bfloat16).astype(jnp.float32)
    rest = total - high
    middle = rest.astype(jnp.bfloat16).astype(jnp.float32)
    low = rest - middle
    row = lax.broadcasted_iota(jnp.int32, (16, C), 0)
    out = jnp.where(row == 0, high, jnp.where(row == 1, middle, jnp.where(row == 2, low, 0.0)))
    return out.astype(jnp.bfloat16)


def first_kernel(current, sent):
    total = jnp.zeros((8, C), jnp.float32)
    for j in range(BPD):
        rows = current[pl.ds(j * BLOCK, BLOCK), :]
        sent[pl.ds(j * BLOCK, BLOCK), :] = rows.astype(jnp.bfloat16)
        total = total + jnp.sum(rows.reshape(BLOCK // 8, 8, C), axis=0)
    sent[pl.ds(OWN_ROWS, 16), :] = sum_rows(jnp.sum(total, axis=0, keepdims=True))


def first(current):
    return pl.pallas_call(
        first_kernel,
        out_shape=jax.ShapeDtypeStruct((SENT_ROWS, C), jnp.bfloat16),
        in_specs=[VMEM],
        out_specs=VMEM,
        compiler_params=pltpu.CompilerParams(vmem_limit_bytes=20 << 20),
        name="first",
    )(current)


def move(table, local, out, at):
    rows = pl.ds(pl.multiple_of(local * BLOCK, BLOCK), BLOCK)
    out[pl.ds(at * BLOCK, BLOCK), :] = table[rows, :]


def pick_early_kernel(asked, wanted, own, far1, far3, near, pass1, pass3, out1, out3):
    pass1[...] = far1[pl.ds(0, HALF_ROWS), :]
    pass3[...] = far3[pl.ds(HALF_ROWS, HALF_ROWS + 16), :]
    for m, out in ((1, out1), (3, out3)):
        for i, (k, table) in enumerate(((0, own), (1, far1), (3, far3))):
            for r in range(CAP):
                move(table, asked[m - 1, k * CAP + r], out, i * CAP + r)
    for r in range(CAP):
        move(far1, wanted[CAP + r], near, r)
        move(far3, wanted[3 * CAP + r], near, CAP + r)


def pick_early(asked, wanted, own, far1, far3):
    b16 = jnp.bfloat16
    out = jax.ShapeDtypeStruct((3 * CAP * BLOCK, C), b16)
    return pl.pallas_call(
        pick_early_kernel,
        out_shape=(
            jax.ShapeDtypeStruct((2 * CAP * BLOCK, C), b16),
            jax.ShapeDtypeStruct((HALF_ROWS, C), b16),
            jax.ShapeDtypeStruct((HALF_ROWS + 16, C), b16),
            out,
            out,
        ),
        in_specs=[SMEM] * 2 + [VMEM] * 3,
        out_specs=(VMEM,) * 5,
        compiler_params=pltpu.CompilerParams(vmem_limit_bytes=20 << 20),
        name="pick_early",
    )(asked, wanted, own, far1, far3)


def pick_late_kernel(asked, wanted, own, far1, far3, low2, high2, near, out1, out3, out2a, out2b, line, far2):
    far2[pl.ds(0, HALF_ROWS), :] = low2[...]
    far2[pl.ds(HALF_ROWS, HALF_ROWS + 16), :] = high2[...]
    tables = ((0, own), (1, far1), (3, far3), (2, far2))
    for r in range(CAP):
        move(far2, asked[0, 2 * CAP + r], out1, r)
        move(far2, asked[2, 2 * CAP + r], out3, r)
        move(far2, wanted[2 * CAP + r], near, r)
    for i, (k, table) in enumerate(tables):
        for r in range(CAP):
            out, at = (out2a, i) if i < 3 else (out2b, 0)
            move(table, asked[1, k * CAP + r], out, at * CAP + r)
    rows = sum(t[pl.ds(OWN_ROWS, 16), :].astype(jnp.float32) for _, t in tables)
    sums = jnp.sum(rows, axis=0, keepdims=True)
    line[...] = jnp.broadcast_to(sums, (8, C))


def pick_late(asked, wanted, own, far1, far3, low2, high2):
    b16 = jnp.bfloat16
    piece = jax.ShapeDtypeStruct((CAP * BLOCK, C), b16)
    return pl.pallas_call(
        pick_late_kernel,
        out_shape=(
            piece,
            piece,
            piece,
            jax.ShapeDtypeStruct((3 * CAP * BLOCK, C), b16),
            piece,
            jax.ShapeDtypeStruct((8, C), jnp.float32),
        ),
        in_specs=[SMEM] * 2 + [VMEM] * 5,
        out_specs=(VMEM,) * 6,
        scratch_shapes=[pltpu.VMEM((SENT_ROWS, C), b16)],
        compiler_params=pltpu.CompilerParams(vmem_limit_bytes=20 << 20),
        name="pick_late",
    )(asked, wanted, own, far1, far3, low2, high2)


def tile_kernel(part, table_count, resume, finish, *refs):
    refs = list(refs)
    lists, words, own = refs[:3]
    tables = refs[3 : 3 + table_count]
    refs = refs[3 + table_count :]
    if resume:
        earlier = refs.pop(0)
    if finish:
        current, all_sums, fresh = refs[:3]
        refs = refs[3:]
        if finish == "more":
            sent = refs.pop(0)
    if finish == "end":
        ready, sems = refs[:2]
        refs = refs[2:]
    total, score_a, score_b, bits = refs[:4]

    row = lax.broadcasted_iota(jnp.int32, (BLOCK, BLOCK), 0)
    bits[...] = lax.shift_left(jnp.ones_like(row), lax.rem(row, 30))
    total[...] = earlier[...] if resume else jnp.zeros_like(total)
    sub = lax.broadcasted_iota(jnp.int32, (8, BLOCK), 0)
    if table_count == 1:
        held = tables[0]
    else:
        held = refs[4]
        at = 0
        for table in tables:
            held[pl.ds(at, table.shape[0]), :] = table[...]
            at += table.shape[0]

    def rows_of(index):
        return pl.ds(pl.multiple_of(index * BLOCK, BLOCK), BLOCK)

    def word_rows(pattern):
        rows = []
        for v in range(BLOCK // 8):
            low, high = 8 * v // 30, (8 * v + 7) // 30
            chunk = jnp.broadcast_to(words[pattern, low : low + 1, :], (8, BLOCK))
            if high != low:
                other = jnp.broadcast_to(words[pattern, high : high + 1, :], (8, BLOCK))
                chunk = jnp.where(sub + 8 * v < 30 * high, chunk, other)
            rows.append(chunk)
        return jnp.concatenate(rows, axis=0)

    size = GROUP[part]

    def target(slot):
        return rows_of(lists[SLOTS + (slot >> 1)])

    def remote(slot, i):
        return held[rows_of(lists[slot + i] & 63), :]

    def score(slot, out):
        mine = own[target(slot), :]
        for i in range(size):
            out[:, i * BLOCK : (i + 1) * BLOCK] = lax.dot_general(
                mine,
                remote(slot, i),
                (((1,), (1,)), ((), ())),
                preferred_element_type=jnp.float32,
            )

    def add(slot, scores):
        weights = []
        for i in range(size):
            packed = word_rows(lists[slot + i] >> 6)
            negative = jnp.minimum(scores[:, i * BLOCK : (i + 1) * BLOCK] * (-1.0 / UNIT), -FLOOR)
            weight = 1.0 / (1.0 - jnp.exp(negative))
            linked = (packed & bits[...]) != 0
            weights.append(jnp.where(linked, weight, 0.0).astype(jnp.bfloat16))
        total[target(slot), :] += jnp.dot(
            jnp.concatenate(weights, axis=1),
            jnp.concatenate([remote(slot, i) for i in range(size)], axis=0),
            preferred_element_type=jnp.float32,
        )

    start, stop = lists[STARTS + part], lists[STARTS + part + 1]
    score(start, score_a)

    def two(i, _):
        slot = pl.multiple_of(start + 2 * size * i, size)
        score(slot + size, score_b)
        add(slot, score_a)
        score(jnp.minimum(slot + 2 * size, stop - size), score_a)
        add(slot + size, score_b)
        return 0

    lax.fori_loop(0, lax.shift_right_logical(stop - start, size.bit_length()), two, 0)

    if not finish:
        return
    col_sums = all_sums[0:1, :]
    moved_sums = jnp.zeros((8, C), jnp.float32)
    copies = []
    for j in range(BPD):
        at = pl.ds(j * BLOCK, BLOCK)
        moved = jnp.maximum(current[at, :] + STEP_SIZE * (total[at, :] - col_sums), 0.0)
        if finish == "more":
            fresh[at, :] = moved
            sent[at, :] = moved.astype(jnp.bfloat16)
            moved_sums = moved_sums + jnp.sum(moved.reshape(BLOCK // 8, 8, C), axis=0)
        else:
            ready[at, :] = moved
            copies.append(pltpu.make_async_copy(ready.at[at, :], fresh.at[at, :], sems.at[j]))
            copies[j].start()
    if finish == "more":
        sent[pl.ds(OWN_ROWS, 16), :] = sum_rows(jnp.sum(moved_sums, axis=0, keepdims=True))
    for copy in copies:
        copy.wait()


def run_tiles(name, part, lists, words, own, tables, earlier=None, current=None, sums=None, finish=""):
    f32 = jnp.float32
    blocks = jax.ShapeDtypeStruct((OWN_ROWS, C), f32)
    args = [lists, words, own, *tables]
    specs = [SMEM] + [VMEM] * (2 + len(tables))
    scratch = []
    out = [blocks]
    if earlier is not None:
        args.append(earlier)
        specs.append(VMEM)
    if finish:
        args += [current, sums]
        specs += [VMEM] * 2
        if finish == "end":
            scratch += [pltpu.VMEM((OWN_ROWS, C), f32), pltpu.SemaphoreType.DMA((BPD,))]
        scratch.append(pltpu.VMEM((OWN_ROWS, C), f32))
        if finish == "more":
            out.append(jax.ShapeDtypeStruct((SENT_ROWS, C), jnp.bfloat16))
    scratch += [
        pltpu.VMEM((BLOCK, GROUP[part] * BLOCK), f32),
        pltpu.VMEM((BLOCK, GROUP[part] * BLOCK), f32),
        pltpu.VMEM((BLOCK, BLOCK), jnp.int32),
    ]
    if len(tables) > 1:
        scratch.append(pltpu.VMEM((sum(t.shape[0] for t in tables), C), jnp.bfloat16))
    return pl.pallas_call(
        functools.partial(tile_kernel, part, len(tables), earlier is not None, finish),
        out_shape=tuple(out),
        in_specs=specs,
        out_specs=(HBM,) if finish == "end" else (VMEM,) * len(out),
        scratch_shapes=scratch,
        compiler_params=pltpu.CompilerParams(vmem_limit_bytes=24 << 20),
        name=name,
    )(*args)


def per_device(affiliations, tile_block, tile_target, tile_pattern, tile_count, block_home, patterns):
    y, x = lax.axis_index("rows_0"), lax.axis_index("rows_1")
    core = lax.axis_index("cols_1")
    place = jnp.stack([jnp.where(core == 0, x, y), jnp.where(core == 0, y, x), core])
    current = affiliations
    own = first(current)
    requests, codes = ask(
        place.astype(jnp.int32), tile_block[0], tile_target[0], tile_count, block_home
    )
    requests = requests.reshape(SIDE, PICKED)
    asked = jnp.stack([fetch(requests[m], 0, SIDE - m) for m in (1, 2, 3)])
    words = jnp.concatenate([patterns, jnp.zeros((1, *patterns.shape[1:]), jnp.int32)], axis=0)

    lists = sort_tiles(codes, tile_pattern[0], tile_count)
    for step in range(STEPS):
        far1, far3 = fetch(own, 1, 0), fetch(own, 3, 0)
        near, pass1, pass3, out1, out3 = pick_early(asked, requests[0], own, far1, far3)
        low2, high2 = fetch(pass1, 1, 0), fetch(pass3, 3, 0)
        side1, side3 = fetch(out1, 0, 1), fetch(out3, 0, 3)
        (total,) = run_tiles("near", 0, lists, words, own, (near,))
        total, low2, high2 = lax.optimization_barrier((total, low2, high2))
        near, out1, out3, out2a, out2b, line = pick_late(asked, requests[0], own, far1, far3, low2, high2)
        lines = tuple(fetch(line, 0, m) for m in (1, 3, 2))
        lines, out2a, out2b, side1, side3 = lax.optimization_barrier(
            (lines, out2a, out2b, side1, side3)
        )
        side2a, side2b = fetch(out2a, 0, 2), fetch(out2b, 0, 2)
        late1, late3 = fetch(out1, 0, 1), fetch(out3, 0, 3)
        sums = line + lines[0] + lines[1] + lines[2]
        other = swap(sums, "cols_1", 1)
        (total,) = run_tiles("sides_1", 1, lists, words, own, (side1, near), total)
        total, other = lax.optimization_barrier((total, other))
        sums = sums + other
        other = swap(sums, "cols_0", 1)
        (total,) = run_tiles("sides_3", 2, lists, words, own, (side3,), total)
        total, other = lax.optimization_barrier((total, other))
        sums = sums + other
        col_sums = sums + swap(sums, "cols_0", 2)
        (total,) = run_tiles("across", 3, lists, words, own, (side2a,), total)
        total, late1, late3 = lax.optimization_barrier((total, late1, late3))
        (total,) = run_tiles("late", 4, lists, words, own, (late1, late3), total)
        total, side2b = lax.optimization_barrier((total, side2b))
        finish = "more" if step < STEPS - 1 else "end"
        current, *own_next = run_tiles(
            "last", 5, lists, words, own, (side2b,), total, current, col_sums, finish
        )
        if own_next:
            (own,) = own_next
    return current


def solution(mesh):
    torus = Mesh(mesh.devices.reshape(4, 4, 4, 2), ALL)
    return jax.shard_map(
        per_device,
        mesh=torus,
        in_specs=(P(ALL, None), P(ALL, None), P(ALL, None), P(ALL, None), P(ALL), P(), P()),
        out_specs=P(ALL, None),
        check_vma=False,
    )
```

```python
import functools

import jax
import jax.numpy as jnp
from jax import lax
from jax.experimental import pallas as pl
from jax.experimental.pallas import tpu as pltpu
from jax.sharding import Mesh
from jax.sharding import PartitionSpec as P

C = 512
BLOCK = 128
STEPS = 2
BPD = 8
SIDE = 4
CAP = 4
N_COLS = 8
NODES = 131072
UNIT = 1572864
PATTERNS = 192
TILES = 240
PARTS = 6
GROUP = (4, 4, 4, 4, 4, 2)
KEYS = PARTS * BPD
SLOTS = TILES + sum(BPD * (g - 1) + 2 * g for g in GROUP) // 16 * 16 + 16
STARTS = SLOTS + SLOTS // 2
LIST = STARTS + 8
EMPTY = PATTERNS * 64
FLOOR = 0.001
STEP_SIZE = 0.3 / NODES
OWN_ROWS = BPD * BLOCK
SENT_ROWS = OWN_ROWS + 16
PICKED = SIDE * CAP
HALF_ROWS = OWN_ROWS // 2

ALL = ("rows_0", "rows_1", "cols_0", "cols_1")
VMEM = pl.BlockSpec(memory_space=pltpu.VMEM)
SMEM = pl.BlockSpec(memory_space=pltpu.SMEM)
HBM = pl.BlockSpec(memory_space=pltpu.HBM)


def pairs(first, second):
    out = []
    for y in range(SIDE):
        for x in range(SIDE):
            for z in range(4):
                for core in range(2):
                    dx, dy = (first, second) if core == 0 else (second, first)
                    sy, sx = (y + dy) % SIDE, (x + dx) % SIDE
                    out.append((((sy * 4 + sx) * 4 + z) * 2 + core, ((y * 4 + x) * 4 + z) * 2 + core))
    return out


def fetch(value, first, second):
    return lax.ppermute(value, ALL, pairs(first, second))


def swap(value, axis, step):
    return lax.ppermute(value, axis, [(i, i ^ step) for i in range(lax.axis_size(axis))])


OWNERS = (
    ((0, 1), (0, 3)),
    ((1, 0), (1, 1), (1, 3), (0, 2)),
    ((3, 0), (3, 1), (3, 3)),
    ((2, 0), (2, 1), (2, 3)),
    ((1, 2), (3, 2)),
    ((2, 2),),
)


def clear(ref, start, size, value):
    def body(i, _):
        for j in range(8):
            ref[start + 8 * i + j] = value
        return 0

    lax.fori_loop(0, size // 8, body, 0)


def ask_kernel(place, blocks, targets, count, home, requests, codes, rank, fill, base):
    first, second, core = place[0], place[1], place[2]
    clear(rank, 0, 128, -1)
    clear(fill, 0, 16, 0)
    clear(requests, 0, 64, 0)
    base[0] = 0
    for part, owners in enumerate(OWNERS):
        for i, (m, k) in enumerate(owners):
            base[m * SIDE + k] = part * 512 + i * CAP

    def note(t, _):
        slot = home[blocks[t]]
        row = slot >> 6
        local = slot & (BPD - 1)
        y, x = row >> 2, row & (SIDE - 1)
        owner_first = jnp.where(core == 0, x, y)
        owner_second = jnp.where(core == 0, y, x)
        k = (owner_first - first) & (SIDE - 1)
        m = (owner_second - second) & (SIDE - 1)
        pair = m * SIDE + k
        seen = rank[pair * BPD + local]
        held = fill[pair]
        mine = jnp.minimum(jnp.where(seen < 0, held, seen), CAP - 1)
        rank[pair * BPD + local] = mine
        fill[pair] = jnp.where(seen < 0, held + 1, held)
        requests[pair * CAP + mine] = local
        codes[t] = base[pair] + mine + targets[t] * 64
        return 0

    lax.fori_loop(0, count[0], note, 0)


def ask(place, blocks, targets, count, home):
    i32 = jnp.int32
    return pl.pallas_call(
        ask_kernel,
        out_shape=(jax.ShapeDtypeStruct((64,), i32), jax.ShapeDtypeStruct((TILES,), i32)),
        in_specs=[SMEM] * 5,
        out_specs=(SMEM,) * 2,
        scratch_shapes=[pltpu.SMEM((128,), i32), pltpu.SMEM((16,), i32), pltpu.SMEM((16,), i32)],
        compiler_params=pltpu.CompilerParams(vmem_limit_bytes=2 << 20),
        name="ask",
    )(place, blocks, targets, count, home)


def sort_kernel(codes, pattern_ids, count, lists, per_key):
    clear(per_key, 0, KEYS, 0)
    clear(lists, 0, SLOTS, EMPTY)
    clear(lists, SLOTS, SLOTS // 2, 0)

    def tally(t, _):
        key = codes[t] >> 6
        per_key[key] = per_key[key] + 1
        return 0

    lax.fori_loop(0, count[0], tally, 0)
    slot = jnp.int32(0)
    for part, size in enumerate(GROUP):
        lists[STARTS + part] = slot
        start = slot
        for target in range(BPD):
            key = part * BPD + target
            tiles = per_key[key]
            per_key[key] = slot
            slot = slot + ((tiles + size - 1) & -size)
        slot = start + jnp.maximum(2 * size, (slot - start + 2 * size - 1) & -(2 * size))
    lists[STARTS + PARTS] = slot

    def put(t, _):
        code = codes[t]
        key = code >> 6
        at = per_key[key]
        per_key[key] = at + 1
        lists[at] = pattern_ids[t] * 64 + (code & 63)
        lists[SLOTS + (at >> 1)] = key & (BPD - 1)
        return 0

    lax.fori_loop(0, count[0], put, 0)


def sort_tiles(codes, pattern_ids, count):
    i32 = jnp.int32
    return pl.pallas_call(
        sort_kernel,
        out_shape=jax.ShapeDtypeStruct((LIST,), i32),
        in_specs=[SMEM] * 3,
        out_specs=SMEM,
        scratch_shapes=[pltpu.SMEM((KEYS,), i32)],
        compiler_params=pltpu.CompilerParams(vmem_limit_bytes=2 << 20),
        name="sort_tiles",
    )(codes, pattern_ids, count)


def sum_rows(total):
    high = total.astype(jnp.bfloat16).astype(jnp.float32)
    rest = total - high
    middle = rest.astype(jnp.bfloat16).astype(jnp.float32)
    low = rest - middle
    row = lax.broadcasted_iota(jnp.int32, (16, C), 0)
    out = jnp.where(row == 0, high, jnp.where(row == 1, middle, jnp.where(row == 2, low, 0.0)))
    return out.astype(jnp.bfloat16)


def first_kernel(current, sent):
    total = jnp.zeros((8, C), jnp.float32)
    for j in range(BPD):
        rows = current[pl.ds(j * BLOCK, BLOCK), :]
        sent[pl.ds(j * BLOCK, BLOCK), :] = rows.astype(jnp.bfloat16)
        total = total + jnp.sum(rows.reshape(BLOCK // 8, 8, C), axis=0)
    sent[pl.ds(OWN_ROWS, 16), :] = sum_rows(jnp.sum(total, axis=0, keepdims=True))


def first(current):
    return pl.pallas_call(
        first_kernel,
        out_shape=jax.ShapeDtypeStruct((SENT_ROWS, C), jnp.bfloat16),
        in_specs=[VMEM],
        out_specs=VMEM,
        compiler_params=pltpu.CompilerParams(vmem_limit_bytes=20 << 20),
        name="first",
    )(current)


def move(table, local, out, at):
    rows = pl.ds(pl.multiple_of(local * BLOCK, BLOCK), BLOCK)
    out[pl.ds(at * BLOCK, BLOCK), :] = table[rows, :]


def pick_early_kernel(asked, wanted, own, far1, far3, near, pass1, pass3, out1, out3):
    pass1[...] = far1[pl.ds(0, HALF_ROWS), :]
    pass3[...] = far3[pl.ds(HALF_ROWS, HALF_ROWS + 16), :]
    for m, out in ((1, out1), (3, out3)):
        for i, (k, table) in enumerate(((0, own), (1, far1), (3, far3))):
            for r in range(CAP):
                move(table, asked[m - 1, k * CAP + r], out, i * CAP + r)
    for r in range(CAP):
        move(far1, wanted[CAP + r], near, r)
        move(far3, wanted[3 * CAP + r], near, CAP + r)


def pick_early(asked, wanted, own, far1, far3):
    b16 = jnp.bfloat16
    out = jax.ShapeDtypeStruct((3 * CAP * BLOCK, C), b16)
    return pl.pallas_call(
        pick_early_kernel,
        out_shape=(
            jax.ShapeDtypeStruct((2 * CAP * BLOCK, C), b16),
            jax.ShapeDtypeStruct((HALF_ROWS, C), b16),
            jax.ShapeDtypeStruct((HALF_ROWS + 16, C), b16),
            out,
            out,
        ),
        in_specs=[SMEM] * 2 + [VMEM] * 3,
        out_specs=(VMEM,) * 5,
        compiler_params=pltpu.CompilerParams(vmem_limit_bytes=20 << 20),
        name="pick_early",
    )(asked, wanted, own, far1, far3)


def pick_late_kernel(asked, wanted, own, far1, far3, low2, high2, near, out1, out3, out2a, out2b, line, far2):
    far2[pl.ds(0, HALF_ROWS), :] = low2[...]
    far2[pl.ds(HALF_ROWS, HALF_ROWS + 16), :] = high2[...]
    tables = ((0, own), (1, far1), (3, far3), (2, far2))
    for r in range(CAP):
        move(far2, asked[0, 2 * CAP + r], out1, r)
        move(far2, asked[2, 2 * CAP + r], out3, r)
        move(far2, wanted[2 * CAP + r], near, r)
    for i, (k, table) in enumerate(tables):
        for r in range(CAP):
            out, at = (out2a, i) if i < 3 else (out2b, 0)
            move(table, asked[1, k * CAP + r], out, at * CAP + r)
    rows = sum(t[pl.ds(OWN_ROWS, 16), :].astype(jnp.float32) for _, t in tables)
    sums = jnp.sum(rows, axis=0, keepdims=True)
    line[...] = jnp.broadcast_to(sums, (8, C))


def pick_late(asked, wanted, own, far1, far3, low2, high2):
    b16 = jnp.bfloat16
    piece = jax.ShapeDtypeStruct((CAP * BLOCK, C), b16)
    return pl.pallas_call(
        pick_late_kernel,
        out_shape=(
            piece,
            piece,
            piece,
            jax.ShapeDtypeStruct((3 * CAP * BLOCK, C), b16),
            piece,
            jax.ShapeDtypeStruct((8, C), jnp.float32),
        ),
        in_specs=[SMEM] * 2 + [VMEM] * 5,
        out_specs=(VMEM,) * 6,
        scratch_shapes=[pltpu.VMEM((SENT_ROWS, C), b16)],
        compiler_params=pltpu.CompilerParams(vmem_limit_bytes=20 << 20),
        name="pick_late",
    )(asked, wanted, own, far1, far3, low2, high2)


def tile_kernel(part, table_count, resume, finish, *refs):
    refs = list(refs)
    lists, words, own = refs[:3]
    tables = refs[3 : 3 + table_count]
    refs = refs[3 + table_count :]
    if resume:
        earlier = refs.pop(0)
    if finish:
        current, all_sums, fresh = refs[:3]
        refs = refs[3:]
        if finish == "more":
            sent = refs.pop(0)
    if finish == "end":
        ready, sems = refs[:2]
        refs = refs[2:]
    total, score_a, score_b, bits = refs[:4]

    row = lax.broadcasted_iota(jnp.int32, (BLOCK, BLOCK), 0)
    bits[...] = lax.shift_left(jnp.ones_like(row), lax.rem(row, 30))
    total[...] = earlier[...] if resume else jnp.zeros_like(total)
    sub = lax.broadcasted_iota(jnp.int32, (8, BLOCK), 0)
    if table_count == 1:
        held = tables[0]
    else:
        held = refs[4]
        at = 0
        for table in tables:
            held[pl.ds(at, table.shape[0]), :] = table[...]
            at += table.shape[0]

    def rows_of(index):
        return pl.ds(pl.multiple_of(index * BLOCK, BLOCK), BLOCK)

    def word_rows(pattern):
        rows = []
        for v in range(BLOCK // 8):
            low, high = 8 * v // 30, (8 * v + 7) // 30
            chunk = jnp.broadcast_to(words[pattern, low : low + 1, :], (8, BLOCK))
            if high != low:
                other = jnp.broadcast_to(words[pattern, high : high + 1, :], (8, BLOCK))
                chunk = jnp.where(sub + 8 * v < 30 * high, chunk, other)
            rows.append(chunk)
        return jnp.concatenate(rows, axis=0)

    size = GROUP[part]

    def target(slot):
        return rows_of(lists[SLOTS + (slot >> 1)])

    def remote(slot, i):
        return held[rows_of(lists[slot + i] & 63), :]

    def score(slot, out):
        mine = own[target(slot), :]
        for i in range(size):
            out[:, i * BLOCK : (i + 1) * BLOCK] = lax.dot_general(
                mine,
                remote(slot, i),
                (((1,), (1,)), ((), ())),
                preferred_element_type=jnp.float32,
            )

    def add(slot, scores):
        weights = []
        for i in range(size):
            packed = word_rows(lists[slot + i] >> 6)
            negative = jnp.minimum(scores[:, i * BLOCK : (i + 1) * BLOCK] * (-1.0 / UNIT), -FLOOR)
            weight = 1.0 / (1.0 - jnp.exp(negative))
            linked = (packed & bits[...]) != 0
            weights.append(jnp.where(linked, weight, 0.0).astype(jnp.bfloat16))
        total[target(slot), :] += jnp.dot(
            jnp.concatenate(weights, axis=1),
            jnp.concatenate([remote(slot, i) for i in range(size)], axis=0),
            preferred_element_type=jnp.float32,
        )

    start, stop = lists[STARTS + part], lists[STARTS + part + 1]
    score(start, score_a)

    def two(i, _):
        slot = pl.multiple_of(start + 2 * size * i, size)
        score(slot + size, score_b)
        add(slot, score_a)
        score(jnp.minimum(slot + 2 * size, stop - size), score_a)
        add(slot + size, score_b)
        return 0

    lax.fori_loop(0, lax.shift_right_logical(stop - start, size.bit_length()), two, 0)

    if not finish:
        return
    col_sums = all_sums[0:1, :]
    moved_sums = jnp.zeros((8, C), jnp.float32)
    copies = []
    for j in range(BPD):
        at = pl.ds(j * BLOCK, BLOCK)
        moved = jnp.maximum(current[at, :] + STEP_SIZE * (total[at, :] - col_sums), 0.0)
        if finish == "more":
            fresh[at, :] = moved
            sent[at, :] = moved.astype(jnp.bfloat16)
            moved_sums = moved_sums + jnp.sum(moved.reshape(BLOCK // 8, 8, C), axis=0)
        else:
            ready[at, :] = moved
            copies.append(pltpu.make_async_copy(ready.at[at, :], fresh.at[at, :], sems.at[j]))
            copies[j].start()
    if finish == "more":
        sent[pl.ds(OWN_ROWS, 16), :] = sum_rows(jnp.sum(moved_sums, axis=0, keepdims=True))
    for copy in copies:
        copy.wait()


def run_tiles(name, part, lists, words, own, tables, earlier=None, current=None, sums=None, finish=""):
    f32 = jnp.float32
    blocks = jax.ShapeDtypeStruct((OWN_ROWS, C), f32)
    args = [lists, words, own, *tables]
    specs = [SMEM] + [VMEM] * (2 + len(tables))
    scratch = []
    out = [blocks]
    if earlier is not None:
        args.append(earlier)
        specs.append(VMEM)
    if finish:
        args += [current, sums]
        specs += [VMEM] * 2
        if finish == "end":
            scratch += [pltpu.VMEM((OWN_ROWS, C), f32), pltpu.SemaphoreType.DMA((BPD,))]
        scratch.append(pltpu.VMEM((OWN_ROWS, C), f32))
        if finish == "more":
            out.append(jax.ShapeDtypeStruct((SENT_ROWS, C), jnp.bfloat16))
    scratch += [
        pltpu.VMEM((BLOCK, GROUP[part] * BLOCK), f32),
        pltpu.VMEM((BLOCK, GROUP[part] * BLOCK), f32),
        pltpu.VMEM((BLOCK, BLOCK), jnp.int32),
    ]
    if len(tables) > 1:
        scratch.append(pltpu.VMEM((sum(t.shape[0] for t in tables), C), jnp.bfloat16))
    return pl.pallas_call(
        functools.partial(tile_kernel, part, len(tables), earlier is not None, finish),
        out_shape=tuple(out),
        in_specs=specs,
        out_specs=(HBM,) if finish == "end" else (VMEM,) * len(out),
        scratch_shapes=scratch,
        compiler_params=pltpu.CompilerParams(vmem_limit_bytes=24 << 20),
        name=name,
    )(*args)


def per_device(affiliations, tile_block, tile_target, tile_pattern, tile_count, block_home, patterns):
    y, x = lax.axis_index("rows_0"), lax.axis_index("rows_1")
    core = lax.axis_index("cols_1")
    place = jnp.stack([jnp.where(core == 0, x, y), jnp.where(core == 0, y, x), core])
    current = affiliations
    own = first(current)
    requests, codes = ask(
        place.astype(jnp.int32), tile_block[0], tile_target[0], tile_count, block_home
    )
    requests = requests.reshape(SIDE, PICKED)
    asked = jnp.stack([fetch(requests[m], 0, SIDE - m) for m in (1, 2, 3)])
    words = jnp.concatenate([patterns, jnp.zeros((1, *patterns.shape[1:]), jnp.int32)], axis=0)

    lists = sort_tiles(codes, tile_pattern[0], tile_count)
    for step in range(STEPS):
        far1, far3 = fetch(own, 1, 0), fetch(own, 3, 0)
        near, pass1, pass3, out1, out3 = pick_early(asked, requests[0], own, far1, far3)
        low2, high2 = fetch(pass1, 1, 0), fetch(pass3, 3, 0)
        side1, side3 = fetch(out1, 0, 1), fetch(out3, 0, 3)
        (total,) = run_tiles("near", 0, lists, words, own, (near,))
        total, low2, high2 = lax.optimization_barrier((total, low2, high2))
        near, out1, out3, out2a, out2b, line = pick_late(asked, requests[0], own, far1, far3, low2, high2)
        lines = tuple(fetch(line, 0, m) for m in (1, 3, 2))
        lines, out2a, out2b, side1, side3 = lax.optimization_barrier(
            (lines, out2a, out2b, side1, side3)
        )
        side2a, side2b = fetch(out2a, 0, 2), fetch(out2b, 0, 2)
        late1, late3 = fetch(out1, 0, 1), fetch(out3, 0, 3)
        sums = line + lines[0] + lines[1] + lines[2]
        other = swap(sums, "cols_1", 1)
        (total,) = run_tiles("sides_1", 1, lists, words, own, (side1, near), total)
        total, other = lax.optimization_barrier((total, other))
        sums = sums + other
        other = swap(sums, "cols_0", 1)
        (total,) = run_tiles("sides_3", 2, lists, words, own, (side3,), total)
        total, other = lax.optimization_barrier((total, other))
        sums = sums + other
        col_sums = sums + swap(sums, "cols_0", 2)
        (total,) = run_tiles("across", 3, lists, words, own, (side2a,), total)
        total, late1, late3 = lax.optimization_barrier((total, late1, late3))
        (total,) = run_tiles("late", 4, lists, words, own, (late1, late3), total)
        total, side2b = lax.optimization_barrier((total, side2b))
        finish = "more" if step < STEPS - 1 else "end"
        current, *own_next = run_tiles(
            "last", 5, lists, words, own, (side2b,), total, current, col_sums, finish
        )
        if own_next:
            (own,) = own_next
    return current


def solution(mesh):
    torus = Mesh(mesh.devices.reshape(4, 4, 4, 2), ALL)
    return jax.shard_map(
        per_device,
        mesh=torus,
        in_specs=(P(ALL, None), P(ALL, None), P(ALL, None), P(ALL, None), P(ALL), P(), P()),
        out_specs=P(ALL, None),
        check_vma=False,
    )
```

```python
import functools

import jax
import jax.numpy as jnp
from jax import lax
from jax.experimental import pallas as pl
from jax.experimental.pallas import tpu as pltpu
from jax.sharding import Mesh
from jax.sharding import PartitionSpec as P

C = 512
BLOCK = 128
STEPS = 2
BPD = 8
SIDE = 4
CAP = 4
N_COLS = 8
NODES = 131072
UNIT = 1572864
PATTERNS = 192
TILES = 240
PARTS = 6
GROUP = (4, 4, 4, 4, 4, 2)
KEYS = PARTS * BPD
SLOTS = TILES + sum(BPD * (g - 1) + 2 * g for g in GROUP) // 16 * 16 + 16
STARTS = SLOTS + SLOTS // 2
LIST = STARTS + 8
EMPTY = PATTERNS * 64
FLOOR = 0.001
STEP_SIZE = 0.3 / NODES
OWN_ROWS = BPD * BLOCK
SENT_ROWS = OWN_ROWS + 16
PICKED = SIDE * CAP
HALF_ROWS = OWN_ROWS // 2

ALL = ("rows_0", "rows_1", "cols_0", "cols_1")
VMEM = pl.BlockSpec(memory_space=pltpu.VMEM)
SMEM = pl.BlockSpec(memory_space=pltpu.SMEM)
HBM = pl.BlockSpec(memory_space=pltpu.HBM)


def pairs(first, second):
    out = []
    for y in range(SIDE):
        for x in range(SIDE):
            for z in range(4):
                for core in range(2):
                    dx, dy = (first, second) if core == 0 else (second, first)
                    sy, sx = (y + dy) % SIDE, (x + dx) % SIDE
                    out.append((((sy * 4 + sx) * 4 + z) * 2 + core, ((y * 4 + x) * 4 + z) * 2 + core))
    return out


def fetch(value, first, second):
    return lax.ppermute(value, ALL, pairs(first, second))


def swap(value, axis, step):
    return lax.ppermute(value, axis, [(i, i ^ step) for i in range(lax.axis_size(axis))])


OWNERS = (
    ((0, 1), (0, 3)),
    ((1, 0), (1, 1), (1, 3), (0, 2)),
    ((3, 0), (3, 1), (3, 3)),
    ((2, 0), (2, 1), (2, 3)),
    ((1, 2), (3, 2)),
    ((2, 2),),
)


def clear(ref, start, size, value):
    def body(i, _):
        for j in range(8):
            ref[start + 8 * i + j] = value
        return 0

    lax.fori_loop(0, size // 8, body, 0)


def ask_kernel(place, blocks, targets, count, home, requests, codes, rank, fill, base):
    first, second, core = place[0], place[1], place[2]
    clear(rank, 0, 128, -1)
    clear(fill, 0, 16, 0)
    clear(requests, 0, 64, 0)
    base[0] = 0
    for part, owners in enumerate(OWNERS):
        for i, (m, k) in enumerate(owners):
            base[m * SIDE + k] = part * 512 + i * CAP

    def note(t, _):
        slot = home[blocks[t]]
        row = slot >> 6
        local = slot & (BPD - 1)
        y, x = row >> 2, row & (SIDE - 1)
        owner_first = jnp.where(core == 0, x, y)
        owner_second = jnp.where(core == 0, y, x)
        k = (owner_first - first) & (SIDE - 1)
        m = (owner_second - second) & (SIDE - 1)
        pair = m * SIDE + k
        seen = rank[pair * BPD + local]
        held = fill[pair]
        mine = jnp.minimum(jnp.where(seen < 0, held, seen), CAP - 1)
        rank[pair * BPD + local] = mine
        fill[pair] = jnp.where(seen < 0, held + 1, held)
        requests[pair * CAP + mine] = local
        codes[t] = base[pair] + mine + targets[t] * 64
        return 0

    lax.fori_loop(0, count[0], note, 0)


def ask(place, blocks, targets, count, home):
    i32 = jnp.int32
    return pl.pallas_call(
        ask_kernel,
        out_shape=(jax.ShapeDtypeStruct((64,), i32), jax.ShapeDtypeStruct((TILES,), i32)),
        in_specs=[SMEM] * 5,
        out_specs=(SMEM,) * 2,
        scratch_shapes=[pltpu.SMEM((128,), i32), pltpu.SMEM((16,), i32), pltpu.SMEM((16,), i32)],
        compiler_params=pltpu.CompilerParams(vmem_limit_bytes=2 << 20),
        name="ask",
    )(place, blocks, targets, count, home)


def sort_kernel(codes, pattern_ids, count, lists, per_key):
    clear(per_key, 0, KEYS, 0)
    clear(lists, 0, SLOTS, EMPTY)
    clear(lists, SLOTS, SLOTS // 2, 0)

    def tally(t, _):
        key = codes[t] >> 6
        per_key[key] = per_key[key] + 1
        return 0

    lax.fori_loop(0, count[0], tally, 0)
    slot = jnp.int32(0)
    for part, size in enumerate(GROUP):
        lists[STARTS + part] = slot
        start = slot
        for target in range(BPD):
            key = part * BPD + target
            tiles = per_key[key]
            per_key[key] = slot
            slot = slot + ((tiles + size - 1) & -size)
        slot = start + jnp.maximum(2 * size, (slot - start + 2 * size - 1) & -(2 * size))
    lists[STARTS + PARTS] = slot

    def put(t, _):
        code = codes[t]
        key = code >> 6
        at = per_key[key]
        per_key[key] = at + 1
        lists[at] = pattern_ids[t] * 64 + (code & 63)
        lists[SLOTS + (at >> 1)] = key & (BPD - 1)
        return 0

    lax.fori_loop(0, count[0], put, 0)


def sort_tiles(codes, pattern_ids, count):
    i32 = jnp.int32
    return pl.pallas_call(
        sort_kernel,
        out_shape=jax.ShapeDtypeStruct((LIST,), i32),
        in_specs=[SMEM] * 3,
        out_specs=SMEM,
        scratch_shapes=[pltpu.SMEM((KEYS,), i32)],
        compiler_params=pltpu.CompilerParams(vmem_limit_bytes=2 << 20),
        name="sort_tiles",
    )(codes, pattern_ids, count)


def sum_rows(total):
    high = total.astype(jnp.bfloat16).astype(jnp.float32)
    rest = total - high
    middle = rest.astype(jnp.bfloat16).astype(jnp.float32)
    low = rest - middle
    row = lax.broadcasted_iota(jnp.int32, (16, C), 0)
    out = jnp.where(row == 0, high, jnp.where(row == 1, middle, jnp.where(row == 2, low, 0.0)))
    return out.astype(jnp.bfloat16)


def first_kernel(current, sent):
    total = jnp.zeros((8, C), jnp.float32)
    for j in range(BPD):
        rows = current[pl.ds(j * BLOCK, BLOCK), :]
        sent[pl.ds(j * BLOCK, BLOCK), :] = rows.astype(jnp.bfloat16)
        total = total + jnp.sum(rows.reshape(BLOCK // 8, 8, C), axis=0)
    sent[pl.ds(OWN_ROWS, 16), :] = sum_rows(jnp.sum(total, axis=0, keepdims=True))


def first(current):
    return pl.pallas_call(
        first_kernel,
        out_shape=jax.ShapeDtypeStruct((SENT_ROWS, C), jnp.bfloat16),
        in_specs=[VMEM],
        out_specs=VMEM,
        compiler_params=pltpu.CompilerParams(vmem_limit_bytes=20 << 20),
        name="first",
    )(current)


def move(table, local, out, at):
    rows = pl.ds(pl.multiple_of(local * BLOCK, BLOCK), BLOCK)
    out[pl.ds(at * BLOCK, BLOCK), :] = table[rows, :]


def pick_early_kernel(asked, wanted, own, far1, far3, near, pass1, pass3, out1, out3):
    pass1[...] = far1[pl.ds(0, HALF_ROWS), :]
    pass3[...] = far3[pl.ds(HALF_ROWS, HALF_ROWS + 16), :]
    for m, out in ((1, out1), (3, out3)):
        for i, (k, table) in enumerate(((0, own), (1, far1), (3, far3))):
            for r in range(CAP):
                move(table, asked[m - 1, k * CAP + r], out, i * CAP + r)
    for r in range(CAP):
        move(far1, wanted[CAP + r], near, r)
        move(far3, wanted[3 * CAP + r], near, CAP + r)


def pick_early(asked, wanted, own, far1, far3):
    b16 = jnp.bfloat16
    out = jax.ShapeDtypeStruct((3 * CAP * BLOCK, C), b16)
    return pl.pallas_call(
        pick_early_kernel,
        out_shape=(
            jax.ShapeDtypeStruct((2 * CAP * BLOCK, C), b16),
            jax.ShapeDtypeStruct((HALF_ROWS, C), b16),
            jax.ShapeDtypeStruct((HALF_ROWS + 16, C), b16),
            out,
            out,
        ),
        in_specs=[SMEM] * 2 + [VMEM] * 3,
        out_specs=(VMEM,) * 5,
        compiler_params=pltpu.CompilerParams(vmem_limit_bytes=20 << 20),
        name="pick_early",
    )(asked, wanted, own, far1, far3)


def pick_late_kernel(asked, wanted, own, far1, far3, low2, high2, near, out1, out3, out2a, out2b, line, far2):
    far2[pl.ds(0, HALF_ROWS), :] = low2[...]
    far2[pl.ds(HALF_ROWS, HALF_ROWS + 16), :] = high2[...]
    tables = ((0, own), (1, far1), (3, far3), (2, far2))
    for r in range(CAP):
        move(far2, asked[0, 2 * CAP + r], out1, r)
        move(far2, asked[2, 2 * CAP + r], out3, r)
        move(far2, wanted[2 * CAP + r], near, r)
    for i, (k, table) in enumerate(tables):
        for r in range(CAP):
            out, at = (out2a, i) if i < 3 else (out2b, 0)
            move(table, asked[1, k * CAP + r], out, at * CAP + r)
    rows = sum(t[pl.ds(OWN_ROWS, 16), :].astype(jnp.float32) for _, t in tables)
    sums = jnp.sum(rows, axis=0, keepdims=True)
    line[...] = jnp.broadcast_to(sums, (8, C))


def pick_late(asked, wanted, own, far1, far3, low2, high2):
    b16 = jnp.bfloat16
    piece = jax.ShapeDtypeStruct((CAP * BLOCK, C), b16)
    return pl.pallas_call(
        pick_late_kernel,
        out_shape=(
            piece,
            piece,
            piece,
            jax.ShapeDtypeStruct((3 * CAP * BLOCK, C), b16),
            piece,
            jax.ShapeDtypeStruct((8, C), jnp.float32),
        ),
        in_specs=[SMEM] * 2 + [VMEM] * 5,
        out_specs=(VMEM,) * 6,
        scratch_shapes=[pltpu.VMEM((SENT_ROWS, C), b16)],
        compiler_params=pltpu.CompilerParams(vmem_limit_bytes=20 << 20),
        name="pick_late",
    )(asked, wanted, own, far1, far3, low2, high2)


def tile_kernel(part, table_count, resume, finish, *refs):
    refs = list(refs)
    lists, words, own = refs[:3]
    tables = refs[3 : 3 + table_count]
    refs = refs[3 + table_count :]
    if resume:
        earlier = refs.pop(0)
    if finish:
        current, all_sums, fresh = refs[:3]
        refs = refs[3:]
        if finish == "more":
            sent = refs.pop(0)
    if finish == "end":
        ready, sems = refs[:2]
        refs = refs[2:]
    total, score_a, score_b, bits = refs[:4]

    row = lax.broadcasted_iota(jnp.int32, (BLOCK, BLOCK), 0)
    bits[...] = lax.shift_left(jnp.ones_like(row), lax.rem(row, 30))
    total[...] = earlier[...] if resume else jnp.zeros_like(total)
    sub = lax.broadcasted_iota(jnp.int32, (8, BLOCK), 0)
    if table_count == 1:
        held = tables[0]
    else:
        held = refs[4]
        at = 0
        for table in tables:
            held[pl.ds(at, table.shape[0]), :] = table[...]
            at += table.shape[0]

    def rows_of(index):
        return pl.ds(pl.multiple_of(index * BLOCK, BLOCK), BLOCK)

    def word_rows(pattern):
        rows = []
        for v in range(BLOCK // 8):
            low, high = 8 * v // 30, (8 * v + 7) // 30
            chunk = jnp.broadcast_to(words[pattern, low : low + 1, :], (8, BLOCK))
            if high != low:
                other = jnp.broadcast_to(words[pattern, high : high + 1, :], (8, BLOCK))
                chunk = jnp.where(sub + 8 * v < 30 * high, chunk, other)
            rows.append(chunk)
        return jnp.concatenate(rows, axis=0)

    size = GROUP[part]

    def target(slot):
        return rows_of(lists[SLOTS + (slot >> 1)])

    def remote(slot, i):
        return held[rows_of(lists[slot + i] & 63), :]

    def score(slot, out):
        mine = own[target(slot), :]
        for i in range(size):
            out[:, i * BLOCK : (i + 1) * BLOCK] = lax.dot_general(
                mine,
                remote(slot, i),
                (((1,), (1,)), ((), ())),
                preferred_element_type=jnp.float32,
            )

    def add(slot, scores):
        weights = []
        for i in range(size):
            packed = word_rows(lists[slot + i] >> 6)
            negative = jnp.minimum(scores[:, i * BLOCK : (i + 1) * BLOCK] * (-1.0 / UNIT), -FLOOR)
            weight = 1.0 / (1.0 - jnp.exp(negative))
            linked = (packed & bits[...]) != 0
            weights.append(jnp.where(linked, weight, 0.0).astype(jnp.bfloat16))
        total[target(slot), :] += jnp.dot(
            jnp.concatenate(weights, axis=1),
            jnp.concatenate([remote(slot, i) for i in range(size)], axis=0),
            preferred_element_type=jnp.float32,
        )

    start, stop = lists[STARTS + part], lists[STARTS + part + 1]
    score(start, score_a)

    def two(i, _):
        slot = pl.multiple_of(start + 2 * size * i, size)
        score(slot + size, score_b)
        add(slot, score_a)
        score(jnp.minimum(slot + 2 * size, stop - size), score_a)
        add(slot + size, score_b)
        return 0

    lax.fori_loop(0, lax.shift_right_logical(stop - start, size.bit_length()), two, 0)

    if not finish:
        return
    col_sums = all_sums[0:1, :]
    moved_sums = jnp.zeros((8, C), jnp.float32)
    copies = []
    for j in range(BPD):
        at = pl.ds(j * BLOCK, BLOCK)
        moved = jnp.maximum(current[at, :] + STEP_SIZE * (total[at, :] - col_sums), 0.0)
        if finish == "more":
            fresh[at, :] = moved
            sent[at, :] = moved.astype(jnp.bfloat16)
            moved_sums = moved_sums + jnp.sum(moved.reshape(BLOCK // 8, 8, C), axis=0)
        else:
            ready[at, :] = moved
            copies.append(pltpu.make_async_copy(ready.at[at, :], fresh.at[at, :], sems.at[j]))
            copies[j].start()
    if finish == "more":
        sent[pl.ds(OWN_ROWS, 16), :] = sum_rows(jnp.sum(moved_sums, axis=0, keepdims=True))
    for copy in copies:
        copy.wait()


def run_tiles(name, part, lists, words, own, tables, earlier=None, current=None, sums=None, finish=""):
    f32 = jnp.float32
    blocks = jax.ShapeDtypeStruct((OWN_ROWS, C), f32)
    args = [lists, words, own, *tables]
    specs = [SMEM] + [VMEM] * (2 + len(tables))
    scratch = []
    out = [blocks]
    if earlier is not None:
        args.append(earlier)
        specs.append(VMEM)
    if finish:
        args += [current, sums]
        specs += [VMEM] * 2
        if finish == "end":
            scratch += [pltpu.VMEM((OWN_ROWS, C), f32), pltpu.SemaphoreType.DMA((BPD,))]
        scratch.append(pltpu.VMEM((OWN_ROWS, C), f32))
        if finish == "more":
            out.append(jax.ShapeDtypeStruct((SENT_ROWS, C), jnp.bfloat16))
    scratch += [
        pltpu.VMEM((BLOCK, GROUP[part] * BLOCK), f32),
        pltpu.VMEM((BLOCK, GROUP[part] * BLOCK), f32),
        pltpu.VMEM((BLOCK, BLOCK), jnp.int32),
    ]
    if len(tables) > 1:
        scratch.append(pltpu.VMEM((sum(t.shape[0] for t in tables), C), jnp.bfloat16))
    return pl.pallas_call(
        functools.partial(tile_kernel, part, len(tables), earlier is not None, finish),
        out_shape=tuple(out),
        in_specs=specs,
        out_specs=(HBM,) if finish == "end" else (VMEM,) * len(out),
        scratch_shapes=scratch,
        compiler_params=pltpu.CompilerParams(vmem_limit_bytes=24 << 20),
        name=name,
    )(*args)


def per_device(affiliations, tile_block, tile_target, tile_pattern, tile_count, block_home, patterns):
    y, x = lax.axis_index("rows_0"), lax.axis_index("rows_1")
    core = lax.axis_index("cols_1")
    place = jnp.stack([jnp.where(core == 0, x, y), jnp.where(core == 0, y, x), core])
    current = affiliations
    own = first(current)
    requests, codes = ask(
        place.astype(jnp.int32), tile_block[0], tile_target[0], tile_count, block_home
    )
    requests = requests.reshape(SIDE, PICKED)
    asked = jnp.stack([fetch(requests[m], 0, SIDE - m) for m in (1, 2, 3)])
    words = jnp.concatenate([patterns, jnp.zeros((1, *patterns.shape[1:]), jnp.int32)], axis=0)

    lists = sort_tiles(codes, tile_pattern[0], tile_count)
    for step in range(STEPS):
        far1, far3 = fetch(own, 1, 0), fetch(own, 3, 0)
        near, pass1, pass3, out1, out3 = pick_early(asked, requests[0], own, far1, far3)
        low2, high2 = fetch(pass1, 1, 0), fetch(pass3, 3, 0)
        side1, side3 = fetch(out1, 0, 1), fetch(out3, 0, 3)
        (total,) = run_tiles("near", 0, lists, words, own, (near,))
        total, low2, high2 = lax.optimization_barrier((total, low2, high2))
        near, out1, out3, out2a, out2b, line = pick_late(asked, requests[0], own, far1, far3, low2, high2)
        lines = tuple(fetch(line, 0, m) for m in (1, 3, 2))
        lines, out2a, out2b, side1, side3 = lax.optimization_barrier(
            (lines, out2a, out2b, side1, side3)
        )
        side2a, side2b = fetch(out2a, 0, 2), fetch(out2b, 0, 2)
        late1, late3 = fetch(out1, 0, 1), fetch(out3, 0, 3)
        sums = line + lines[0] + lines[1] + lines[2]
        other = swap(sums, "cols_1", 1)
        (total,) = run_tiles("sides_1", 1, lists, words, own, (side1, near), total)
        total, other = lax.optimization_barrier((total, other))
        sums = sums + other
        other = swap(sums, "cols_0", 1)
        (total,) = run_tiles("sides_3", 2, lists, words, own, (side3,), total)
        total, other = lax.optimization_barrier((total, other))
        sums = sums + other
        other = swap(sums, "cols_0", 2)
        (total,) = run_tiles("across", 3, lists, words, own, (side2a,), total)
        total, other, late1, late3 = lax.optimization_barrier((total, other, late1, late3))
        col_sums = sums + other
        (total,) = run_tiles("late", 4, lists, words, own, (late1, late3), total)
        total, side2b = lax.optimization_barrier((total, side2b))
        finish = "more" if step < STEPS - 1 else "end"
        current, *own_next = run_tiles(
            "last", 5, lists, words, own, (side2b,), total, current, col_sums, finish
        )
        if own_next:
            (own,) = own_next
    return current


def solution(mesh):
    torus = Mesh(mesh.devices.reshape(4, 4, 4, 2), ALL)
    return jax.shard_map(
        per_device,
        mesh=torus,
        in_specs=(P(ALL, None), P(ALL, None), P(ALL, None), P(ALL, None), P(ALL), P(), P()),
        out_specs=P(ALL, None),
        check_vma=False,
    )
```

```python
import functools

import jax
import jax.numpy as jnp
from jax import lax
from jax.experimental import pallas as pl
from jax.experimental.pallas import tpu as pltpu
from jax.sharding import Mesh
from jax.sharding import PartitionSpec as P

C = 512
BLOCK = 128
STEPS = 2
BPD = 8
SIDE = 4
CAP = 4
N_COLS = 8
NODES = 131072
UNIT = 1572864
PATTERNS = 192
TILES = 240
PARTS = 6
GROUP = (4, 4, 4, 4, 4, 2)
KEYS = PARTS * BPD
SLOTS = TILES + sum(BPD * (g - 1) + 2 * g for g in GROUP) // 16 * 16 + 16
STARTS = SLOTS + SLOTS // 2
LIST = STARTS + 8
EMPTY = PATTERNS * 64
FLOOR = 0.001
STEP_SIZE = 0.3 / NODES
OWN_ROWS = BPD * BLOCK
SENT_ROWS = OWN_ROWS + 16
PICKED = SIDE * CAP
HALF_ROWS = OWN_ROWS // 2

ALL = ("rows_0", "rows_1", "cols_0", "cols_1")
VMEM = pl.BlockSpec(memory_space=pltpu.VMEM)
SMEM = pl.BlockSpec(memory_space=pltpu.SMEM)
HBM = pl.BlockSpec(memory_space=pltpu.HBM)


def pairs(first, second):
    out = []
    for y in range(SIDE):
        for x in range(SIDE):
            for z in range(4):
                for core in range(2):
                    dx, dy = (first, second) if core == 0 else (second, first)
                    sy, sx = (y + dy) % SIDE, (x + dx) % SIDE
                    out.append((((sy * 4 + sx) * 4 + z) * 2 + core, ((y * 4 + x) * 4 + z) * 2 + core))
    return out


def fetch(value, first, second):
    return lax.ppermute(value, ALL, pairs(first, second))


def swap(value, axis, step):
    return lax.ppermute(value, axis, [(i, i ^ step) for i in range(lax.axis_size(axis))])


OWNERS = (
    ((0, 1), (0, 3)),
    ((1, 0), (1, 1), (1, 3), (0, 2)),
    ((3, 0), (3, 1), (3, 3)),
    ((2, 0), (2, 1), (2, 3)),
    ((1, 2), (3, 2)),
    ((2, 2),),
)


def clear(ref, start, size, value):
    def body(i, _):
        for j in range(8):
            ref[start + 8 * i + j] = value
        return 0

    lax.fori_loop(0, size // 8, body, 0)


def ask_kernel(place, blocks, targets, count, home, requests, codes, rank, fill, base):
    first, second, core = place[0], place[1], place[2]
    clear(rank, 0, 128, -1)
    clear(fill, 0, 16, 0)
    clear(requests, 0, 64, 0)
    base[0] = 0
    for part, owners in enumerate(OWNERS):
        for i, (m, k) in enumerate(owners):
            base[m * SIDE + k] = part * 512 + i * CAP

    def note(t, _):
        slot = home[blocks[t]]
        row = slot >> 6
        local = slot & (BPD - 1)
        y, x = row >> 2, row & (SIDE - 1)
        owner_first = jnp.where(core == 0, x, y)
        owner_second = jnp.where(core == 0, y, x)
        k = (owner_first - first) & (SIDE - 1)
        m = (owner_second - second) & (SIDE - 1)
        pair = m * SIDE + k
        seen = rank[pair * BPD + local]
        held = fill[pair]
        mine = jnp.minimum(jnp.where(seen < 0, held, seen), CAP - 1)
        rank[pair * BPD + local] = mine
        fill[pair] = jnp.where(seen < 0, held + 1, held)
        requests[pair * CAP + mine] = local
        codes[t] = base[pair] + mine + targets[t] * 64
        return 0

    lax.fori_loop(0, count[0], note, 0)


def ask(place, blocks, targets, count, home):
    i32 = jnp.int32
    return pl.pallas_call(
        ask_kernel,
        out_shape=(jax.ShapeDtypeStruct((64,), i32), jax.ShapeDtypeStruct((TILES,), i32)),
        in_specs=[SMEM] * 5,
        out_specs=(SMEM,) * 2,
        scratch_shapes=[pltpu.SMEM((128,), i32), pltpu.SMEM((16,), i32), pltpu.SMEM((16,), i32)],
        compiler_params=pltpu.CompilerParams(vmem_limit_bytes=2 << 20),
        name="ask",
    )(place, blocks, targets, count, home)


def sort_kernel(codes, pattern_ids, count, lists, per_key):
    clear(per_key, 0, KEYS, 0)
    clear(lists, 0, SLOTS, EMPTY)
    clear(lists, SLOTS, SLOTS // 2, 0)

    def tally(t, _):
        key = codes[t] >> 6
        per_key[key] = per_key[key] + 1
        return 0

    lax.fori_loop(0, count[0], tally, 0)
    slot = jnp.int32(0)
    for part, size in enumerate(GROUP):
        lists[STARTS + part] = slot
        start = slot
        for target in range(BPD):
            key = part * BPD + target
            tiles = per_key[key]
            per_key[key] = slot
            slot = slot + ((tiles + size - 1) & -size)
        slot = start + jnp.maximum(2 * size, (slot - start + 2 * size - 1) & -(2 * size))
    lists[STARTS + PARTS] = slot

    def put(t, _):
        code = codes[t]
        key = code >> 6
        at = per_key[key]
        per_key[key] = at + 1
        lists[at] = pattern_ids[t] * 64 + (code & 63)
        lists[SLOTS + (at >> 1)] = key & (BPD - 1)
        return 0

    lax.fori_loop(0, count[0], put, 0)


def sort_tiles(codes, pattern_ids, count):
    i32 = jnp.int32
    return pl.pallas_call(
        sort_kernel,
        out_shape=jax.ShapeDtypeStruct((LIST,), i32),
        in_specs=[SMEM] * 3,
        out_specs=SMEM,
        scratch_shapes=[pltpu.SMEM((KEYS,), i32)],
        compiler_params=pltpu.CompilerParams(vmem_limit_bytes=2 << 20),
        name="sort_tiles",
    )(codes, pattern_ids, count)


def sum_rows(total):
    high = total.astype(jnp.bfloat16).astype(jnp.float32)
    rest = total - high
    middle = rest.astype(jnp.bfloat16).astype(jnp.float32)
    low = rest - middle
    row = lax.broadcasted_iota(jnp.int32, (16, C), 0)
    out = jnp.where(row == 0, high, jnp.where(row == 1, middle, jnp.where(row == 2, low, 0.0)))
    return out.astype(jnp.bfloat16)


def first_kernel(current, sent):
    total = jnp.zeros((8, C), jnp.float32)
    for j in range(BPD):
        rows = current[pl.ds(j * BLOCK, BLOCK), :]
        sent[pl.ds(j * BLOCK, BLOCK), :] = rows.astype(jnp.bfloat16)
        total = total + jnp.sum(rows.reshape(BLOCK // 8, 8, C), axis=0)
    sent[pl.ds(OWN_ROWS, 16), :] = sum_rows(jnp.sum(total, axis=0, keepdims=True))


def first(current):
    return pl.pallas_call(
        first_kernel,
        out_shape=jax.ShapeDtypeStruct((SENT_ROWS, C), jnp.bfloat16),
        in_specs=[VMEM],
        out_specs=VMEM,
        compiler_params=pltpu.CompilerParams(vmem_limit_bytes=20 << 20),
        name="first",
    )(current)


def move(table, local, out, at):
    rows = pl.ds(pl.multiple_of(local * BLOCK, BLOCK), BLOCK)
    out[pl.ds(at * BLOCK, BLOCK), :] = table[rows, :]


def pick_early_kernel(asked, own, far1, far3, out1, out3):
    for m, out in ((1, out1), (3, out3)):
        for i, (k, table) in enumerate(((0, own), (1, far1), (3, far3))):
            for r in range(CAP):
                move(table, asked[m - 1, k * CAP + r], out, i * CAP + r)


def pick_early(asked, own, far1, far3):
    out = jax.ShapeDtypeStruct((3 * CAP * BLOCK, C), jnp.bfloat16)
    return pl.pallas_call(
        pick_early_kernel,
        out_shape=(out, out),
        in_specs=[SMEM] + [VMEM] * 3,
        out_specs=(VMEM,) * 2,
        compiler_params=pltpu.CompilerParams(vmem_limit_bytes=20 << 20),
        name="pick_early",
    )(asked, own, far1, far3)


def pick_pass_kernel(wanted, far1, far3, near, pass1, pass3):
    pass1[...] = far1[pl.ds(0, HALF_ROWS), :]
    pass3[...] = far3[pl.ds(HALF_ROWS, HALF_ROWS + 16), :]
    for r in range(CAP):
        move(far1, wanted[CAP + r], near, r)
        move(far3, wanted[3 * CAP + r], near, CAP + r)


def pick_pass(wanted, far1, far3):
    shape = lambda rows: jax.ShapeDtypeStruct((rows, C), jnp.bfloat16)
    return pl.pallas_call(
        pick_pass_kernel,
        out_shape=(shape(2 * CAP * BLOCK), shape(HALF_ROWS), shape(HALF_ROWS + 16)),
        in_specs=[SMEM] + [VMEM] * 2,
        out_specs=(VMEM,) * 3,
        compiler_params=pltpu.CompilerParams(vmem_limit_bytes=20 << 20),
        name="pick_pass",
    )(wanted, far1, far3)


def pick_late_kernel(asked, wanted, own, far1, far3, low2, high2, near, out1, out3, out2a, out2b, line, far2):
    far2[pl.ds(0, HALF_ROWS), :] = low2[...]
    far2[pl.ds(HALF_ROWS, HALF_ROWS + 16), :] = high2[...]
    tables = ((0, own), (1, far1), (3, far3), (2, far2))
    for r in range(CAP):
        move(far2, asked[0, 2 * CAP + r], out1, r)
        move(far2, asked[2, 2 * CAP + r], out3, r)
        move(far2, wanted[2 * CAP + r], near, r)
    for i, (k, table) in enumerate(tables):
        for r in range(CAP):
            out, at = (out2a, i) if i < 3 else (out2b, 0)
            move(table, asked[1, k * CAP + r], out, at * CAP + r)
    rows = sum(t[pl.ds(OWN_ROWS, 16), :].astype(jnp.float32) for _, t in tables)
    sums = jnp.sum(rows, axis=0, keepdims=True)
    line[...] = jnp.broadcast_to(sums, (8, C))


def pick_late(asked, wanted, own, far1, far3, low2, high2):
    b16 = jnp.bfloat16
    piece = jax.ShapeDtypeStruct((CAP * BLOCK, C), b16)
    return pl.pallas_call(
        pick_late_kernel,
        out_shape=(
            piece,
            piece,
            piece,
            jax.ShapeDtypeStruct((3 * CAP * BLOCK, C), b16),
            piece,
            jax.ShapeDtypeStruct((8, C), jnp.float32),
        ),
        in_specs=[SMEM] * 2 + [VMEM] * 5,
        out_specs=(VMEM,) * 6,
        scratch_shapes=[pltpu.VMEM((SENT_ROWS, C), b16)],
        compiler_params=pltpu.CompilerParams(vmem_limit_bytes=20 << 20),
        name="pick_late",
    )(asked, wanted, own, far1, far3, low2, high2)


def tile_kernel(part, table_count, resume, finish, *refs):
    refs = list(refs)
    lists, words, own = refs[:3]
    tables = refs[3 : 3 + table_count]
    refs = refs[3 + table_count :]
    if resume:
        earlier = refs.pop(0)
    if finish:
        current, all_sums, fresh = refs[:3]
        refs = refs[3:]
        if finish == "more":
            sent = refs.pop(0)
    if finish == "end":
        ready, sems = refs[:2]
        refs = refs[2:]
    total, score_a, score_b, bits = refs[:4]

    row = lax.broadcasted_iota(jnp.int32, (BLOCK, BLOCK), 0)
    bits[...] = lax.shift_left(jnp.ones_like(row), lax.rem(row, 30))
    total[...] = earlier[...] if resume else jnp.zeros_like(total)
    sub = lax.broadcasted_iota(jnp.int32, (8, BLOCK), 0)
    if table_count == 1:
        held = tables[0]
    else:
        held = refs[4]
        at = 0
        for table in tables:
            held[pl.ds(at, table.shape[0]), :] = table[...]
            at += table.shape[0]

    def rows_of(index):
        return pl.ds(pl.multiple_of(index * BLOCK, BLOCK), BLOCK)

    def word_rows(pattern):
        rows = []
        for v in range(BLOCK // 8):
            low, high = 8 * v // 30, (8 * v + 7) // 30
            chunk = jnp.broadcast_to(words[pattern, low : low + 1, :], (8, BLOCK))
            if high != low:
                other = jnp.broadcast_to(words[pattern, high : high + 1, :], (8, BLOCK))
                chunk = jnp.where(sub + 8 * v < 30 * high, chunk, other)
            rows.append(chunk)
        return jnp.concatenate(rows, axis=0)

    size = GROUP[part]

    def target(slot):
        return rows_of(lists[SLOTS + (slot >> 1)])

    def remote(slot, i):
        return held[rows_of(lists[slot + i] & 63), :]

    def score(slot, out):
        mine = own[target(slot), :]
        for i in range(size):
            out[:, i * BLOCK : (i + 1) * BLOCK] = lax.dot_general(
                mine,
                remote(slot, i),
                (((1,), (1,)), ((), ())),
                preferred_element_type=jnp.float32,
            )

    def add(slot, scores):
        weights = []
        for i in range(size):
            packed = word_rows(lists[slot + i] >> 6)
            negative = jnp.minimum(scores[:, i * BLOCK : (i + 1) * BLOCK] * (-1.0 / UNIT), -FLOOR)
            weight = 1.0 / (1.0 - jnp.exp(negative))
            linked = (packed & bits[...]) != 0
            weights.append(jnp.where(linked, weight, 0.0).astype(jnp.bfloat16))
        total[target(slot), :] += jnp.dot(
            jnp.concatenate(weights, axis=1),
            jnp.concatenate([remote(slot, i) for i in range(size)], axis=0),
            preferred_element_type=jnp.float32,
        )

    start, stop = lists[STARTS + part], lists[STARTS + part + 1]
    score(start, score_a)

    def two(i, _):
        slot = pl.multiple_of(start + 2 * size * i, size)
        score(slot + size, score_b)
        add(slot, score_a)
        score(jnp.minimum(slot + 2 * size, stop - size), score_a)
        add(slot + size, score_b)
        return 0

    lax.fori_loop(0, lax.shift_right_logical(stop - start, size.bit_length()), two, 0)

    if not finish:
        return
    col_sums = all_sums[0:1, :]
    moved_sums = jnp.zeros((8, C), jnp.float32)
    copies = []
    for j in range(BPD):
        at = pl.ds(j * BLOCK, BLOCK)
        moved = jnp.maximum(current[at, :] + STEP_SIZE * (total[at, :] - col_sums), 0.0)
        if finish == "more":
            fresh[at, :] = moved
            sent[at, :] = moved.astype(jnp.bfloat16)
            moved_sums = moved_sums + jnp.sum(moved.reshape(BLOCK // 8, 8, C), axis=0)
        else:
            ready[at, :] = moved
            copies.append(pltpu.make_async_copy(ready.at[at, :], fresh.at[at, :], sems.at[j]))
            copies[j].start()
    if finish == "more":
        sent[pl.ds(OWN_ROWS, 16), :] = sum_rows(jnp.sum(moved_sums, axis=0, keepdims=True))
    for copy in copies:
        copy.wait()


def run_tiles(name, part, lists, words, own, tables, earlier=None, current=None, sums=None, finish=""):
    f32 = jnp.float32
    blocks = jax.ShapeDtypeStruct((OWN_ROWS, C), f32)
    args = [lists, words, own, *tables]
    specs = [SMEM] + [VMEM] * (2 + len(tables))
    scratch = []
    out = [blocks]
    if earlier is not None:
        args.append(earlier)
        specs.append(VMEM)
    if finish:
        args += [current, sums]
        specs += [VMEM] * 2
        if finish == "end":
            scratch += [pltpu.VMEM((OWN_ROWS, C), f32), pltpu.SemaphoreType.DMA((BPD,))]
        scratch.append(pltpu.VMEM((OWN_ROWS, C), f32))
        if finish == "more":
            out.append(jax.ShapeDtypeStruct((SENT_ROWS, C), jnp.bfloat16))
    scratch += [
        pltpu.VMEM((BLOCK, GROUP[part] * BLOCK), f32),
        pltpu.VMEM((BLOCK, GROUP[part] * BLOCK), f32),
        pltpu.VMEM((BLOCK, BLOCK), jnp.int32),
    ]
    if len(tables) > 1:
        scratch.append(pltpu.VMEM((sum(t.shape[0] for t in tables), C), jnp.bfloat16))
    return pl.pallas_call(
        functools.partial(tile_kernel, part, len(tables), earlier is not None, finish),
        out_shape=tuple(out),
        in_specs=specs,
        out_specs=(HBM,) if finish == "end" else (VMEM,) * len(out),
        scratch_shapes=scratch,
        compiler_params=pltpu.CompilerParams(vmem_limit_bytes=24 << 20),
        name=name,
    )(*args)


def per_device(affiliations, tile_block, tile_target, tile_pattern, tile_count, block_home, patterns):
    y, x = lax.axis_index("rows_0"), lax.axis_index("rows_1")
    core = lax.axis_index("cols_1")
    place = jnp.stack([jnp.where(core == 0, x, y), jnp.where(core == 0, y, x), core])
    current = affiliations
    own = first(current)
    requests, codes = ask(
        place.astype(jnp.int32), tile_block[0], tile_target[0], tile_count, block_home
    )
    requests = requests.reshape(SIDE, PICKED)
    asked = jnp.stack([fetch(requests[m], 0, SIDE - m) for m in (1, 2, 3)])
    words = jnp.concatenate([patterns, jnp.zeros((1, *patterns.shape[1:]), jnp.int32)], axis=0)

    lists = sort_tiles(codes, tile_pattern[0], tile_count)
    for step in range(STEPS):
        far1, far3 = fetch(own, 1, 0), fetch(own, 3, 0)
        out1, out3 = pick_early(asked, own, far1, far3)
        near, pass1, pass3 = pick_pass(requests[0], far1, far3)
        low2, high2 = fetch(pass1, 1, 0), fetch(pass3, 3, 0)
        side1, side3 = fetch(out1, 0, 1), fetch(out3, 0, 3)
        (total,) = run_tiles("near", 0, lists, words, own, (near,))
        total, low2, high2 = lax.optimization_barrier((total, low2, high2))
        near, out1, out3, out2a, out2b, line = pick_late(asked, requests[0], own, far1, far3, low2, high2)
        lines = tuple(fetch(line, 0, m) for m in (1, 3, 2))
        lines, out2a, out2b, side1, side3 = lax.optimization_barrier(
            (lines, out2a, out2b, side1, side3)
        )
        side2a, side2b = fetch(out2a, 0, 2), fetch(out2b, 0, 2)
        late1, late3 = fetch(out1, 0, 1), fetch(out3, 0, 3)
        sums = line + lines[0] + lines[1] + lines[2]
        other = swap(sums, "cols_1", 1)
        (total,) = run_tiles("sides_1", 1, lists, words, own, (side1, near), total)
        total, other = lax.optimization_barrier((total, other))
        sums = sums + other
        other = swap(sums, "cols_0", 1)
        (total,) = run_tiles("sides_3", 2, lists, words, own, (side3,), total)
        total, other = lax.optimization_barrier((total, other))
        sums = sums + other
        other = swap(sums, "cols_0", 2)
        (total,) = run_tiles("across", 3, lists, words, own, (side2a,), total)
        total, other, late1, late3 = lax.optimization_barrier((total, other, late1, late3))
        col_sums = sums + other
        (total,) = run_tiles("late", 4, lists, words, own, (late1, late3), total)
        total, side2b = lax.optimization_barrier((total, side2b))
        finish = "more" if step < STEPS - 1 else "end"
        current, *own_next = run_tiles(
            "last", 5, lists, words, own, (side2b,), total, current, col_sums, finish
        )
        if own_next:
            (own,) = own_next
    return current


def solution(mesh):
    torus = Mesh(mesh.devices.reshape(4, 4, 4, 2), ALL)
    return jax.shard_map(
        per_device,
        mesh=torus,
        in_specs=(P(ALL, None), P(ALL, None), P(ALL, None), P(ALL, None), P(ALL), P(), P()),
        out_specs=P(ALL, None),
        check_vma=False,
    )
```

```python
import functools

import jax
import jax.numpy as jnp
from jax import lax
from jax.experimental import pallas as pl
from jax.experimental.pallas import tpu as pltpu
from jax.sharding import Mesh
from jax.sharding import PartitionSpec as P

C = 512
BLOCK = 128
STEPS = 2
BPD = 8
SIDE = 4
CAP = 4
N_COLS = 8
NODES = 131072
UNIT = 1572864
PATTERNS = 192
TILES = 240
PARTS = 6
GROUP = (4, 4, 4, 4, 4, 2)
KEYS = PARTS * BPD
SLOTS = TILES + sum(BPD * (g - 1) + 2 * g for g in GROUP) // 16 * 16 + 16
STARTS = SLOTS + SLOTS // 2
LIST = STARTS + 8
EMPTY = PATTERNS * 64
FLOOR = 0.001
STEP_SIZE = 0.3 / NODES
OWN_ROWS = BPD * BLOCK
SENT_ROWS = OWN_ROWS + 16
PICKED = SIDE * CAP
HALF_ROWS = OWN_ROWS // 2

ALL = ("rows_0", "rows_1", "cols_0", "cols_1")
VMEM = pl.BlockSpec(memory_space=pltpu.VMEM)
SMEM = pl.BlockSpec(memory_space=pltpu.SMEM)
HBM = pl.BlockSpec(memory_space=pltpu.HBM)


def pairs(first, second):
    out = []
    for y in range(SIDE):
        for x in range(SIDE):
            for z in range(4):
                for core in range(2):
                    dx, dy = (first, second) if core == 0 else (second, first)
                    sy, sx = (y + dy) % SIDE, (x + dx) % SIDE
                    out.append((((sy * 4 + sx) * 4 + z) * 2 + core, ((y * 4 + x) * 4 + z) * 2 + core))
    return out


def fetch(value, first, second):
    return lax.ppermute(value, ALL, pairs(first, second))


def swap(value, axis, step):
    return lax.ppermute(value, axis, [(i, i ^ step) for i in range(lax.axis_size(axis))])


OWNERS = (
    ((0, 1), (0, 3)),
    ((1, 0), (1, 1), (1, 3), (0, 2)),
    ((3, 0), (3, 1), (3, 3)),
    ((2, 0), (2, 1), (2, 3)),
    ((1, 2), (3, 2)),
    ((2, 2),),
)


def clear(ref, start, size, value):
    def body(i, _):
        for j in range(8):
            ref[start + 8 * i + j] = value
        return 0

    lax.fori_loop(0, size // 8, body, 0)


def ask_kernel(place, blocks, targets, count, home, requests, codes, rank, fill, base):
    first, second, core = place[0], place[1], place[2]
    clear(rank, 0, 128, -1)
    clear(fill, 0, 16, 0)
    clear(requests, 0, 64, 0)
    base[0] = 0
    for part, owners in enumerate(OWNERS):
        for i, (m, k) in enumerate(owners):
            base[m * SIDE + k] = part * 512 + i * CAP

    def note(t, _):
        slot = home[blocks[t]]
        row = slot >> 6
        local = slot & (BPD - 1)
        y, x = row >> 2, row & (SIDE - 1)
        owner_first = jnp.where(core == 0, x, y)
        owner_second = jnp.where(core == 0, y, x)
        k = (owner_first - first) & (SIDE - 1)
        m = (owner_second - second) & (SIDE - 1)
        pair = m * SIDE + k
        seen = rank[pair * BPD + local]
        held = fill[pair]
        mine = jnp.minimum(jnp.where(seen < 0, held, seen), CAP - 1)
        rank[pair * BPD + local] = mine
        fill[pair] = jnp.where(seen < 0, held + 1, held)
        requests[pair * CAP + mine] = local
        codes[t] = base[pair] + mine + targets[t] * 64
        return 0

    lax.fori_loop(0, count[0], note, 0)


def ask(place, blocks, targets, count, home):
    i32 = jnp.int32
    return pl.pallas_call(
        ask_kernel,
        out_shape=(jax.ShapeDtypeStruct((64,), i32), jax.ShapeDtypeStruct((TILES,), i32)),
        in_specs=[SMEM] * 5,
        out_specs=(SMEM,) * 2,
        scratch_shapes=[pltpu.SMEM((128,), i32), pltpu.SMEM((16,), i32), pltpu.SMEM((16,), i32)],
        compiler_params=pltpu.CompilerParams(vmem_limit_bytes=2 << 20),
        name="ask",
    )(place, blocks, targets, count, home)


def sort_kernel(codes, pattern_ids, count, lists, per_key):
    clear(per_key, 0, KEYS, 0)
    clear(lists, 0, SLOTS, EMPTY)
    clear(lists, SLOTS, SLOTS // 2, 0)

    def tally(t, _):
        key = codes[t] >> 6
        per_key[key] = per_key[key] + 1
        return 0

    lax.fori_loop(0, count[0], tally, 0)
    slot = jnp.int32(0)
    for part, size in enumerate(GROUP):
        lists[STARTS + part] = slot
        start = slot
        for target in range(BPD):
            key = part * BPD + target
            tiles = per_key[key]
            per_key[key] = slot
            slot = slot + ((tiles + size - 1) & -size)
        slot = start + jnp.maximum(2 * size, (slot - start + 2 * size - 1) & -(2 * size))
    lists[STARTS + PARTS] = slot

    def put(t, _):
        code = codes[t]
        key = code >> 6
        at = per_key[key]
        per_key[key] = at + 1
        lists[at] = pattern_ids[t] * 64 + (code & 63)
        lists[SLOTS + (at >> 1)] = key & (BPD - 1)
        return 0

    lax.fori_loop(0, count[0], put, 0)


def sort_tiles(codes, pattern_ids, count):
    i32 = jnp.int32
    return pl.pallas_call(
        sort_kernel,
        out_shape=jax.ShapeDtypeStruct((LIST,), i32),
        in_specs=[SMEM] * 3,
        out_specs=SMEM,
        scratch_shapes=[pltpu.SMEM((KEYS,), i32)],
        compiler_params=pltpu.CompilerParams(vmem_limit_bytes=2 << 20),
        name="sort_tiles",
    )(codes, pattern_ids, count)


def sum_rows(total):
    high = total.astype(jnp.bfloat16).astype(jnp.float32)
    rest = total - high
    middle = rest.astype(jnp.bfloat16).astype(jnp.float32)
    low = rest - middle
    row = lax.broadcasted_iota(jnp.int32, (16, C), 0)
    out = jnp.where(row == 0, high, jnp.where(row == 1, middle, jnp.where(row == 2, low, 0.0)))
    return out.astype(jnp.bfloat16)


def first_kernel(current, sent):
    total = jnp.zeros((8, C), jnp.float32)
    for j in range(BPD):
        rows = current[pl.ds(j * BLOCK, BLOCK), :]
        sent[pl.ds(j * BLOCK, BLOCK), :] = rows.astype(jnp.bfloat16)
        total = total + jnp.sum(rows.reshape(BLOCK // 8, 8, C), axis=0)
    sent[pl.ds(OWN_ROWS, 16), :] = sum_rows(jnp.sum(total, axis=0, keepdims=True))


def first(current):
    return pl.pallas_call(
        first_kernel,
        out_shape=jax.ShapeDtypeStruct((SENT_ROWS, C), jnp.bfloat16),
        in_specs=[VMEM],
        out_specs=VMEM,
        compiler_params=pltpu.CompilerParams(vmem_limit_bytes=20 << 20),
        name="first",
    )(current)


def move(table, local, out, at):
    rows = pl.ds(pl.multiple_of(local * BLOCK, BLOCK), BLOCK)
    out[pl.ds(at * BLOCK, BLOCK), :] = table[rows, :]


def pick_early_kernel(asked, own, far1, far3, pass1, pass3, out1, out3):
    pass1[...] = far1[pl.ds(0, HALF_ROWS), :]
    pass3[...] = far3[pl.ds(HALF_ROWS, HALF_ROWS + 16), :]
    for m, out in ((1, out1), (3, out3)):
        for i, (k, table) in enumerate(((0, own), (1, far1), (3, far3))):
            for r in range(CAP):
                move(table, asked[m - 1, k * CAP + r], out, i * CAP + r)


def pick_early(asked, own, far1, far3):
    b16 = jnp.bfloat16
    out = jax.ShapeDtypeStruct((3 * CAP * BLOCK, C), b16)
    return pl.pallas_call(
        pick_early_kernel,
        out_shape=(
            jax.ShapeDtypeStruct((HALF_ROWS, C), b16),
            jax.ShapeDtypeStruct((HALF_ROWS + 16, C), b16),
            out,
            out,
        ),
        in_specs=[SMEM] + [VMEM] * 3,
        out_specs=(VMEM,) * 4,
        compiler_params=pltpu.CompilerParams(vmem_limit_bytes=20 << 20),
        name="pick_early",
    )(asked, own, far1, far3)


def pick_near_kernel(wanted, far1, far3, near):
    for r in range(CAP):
        move(far1, wanted[CAP + r], near, r)
        move(far3, wanted[3 * CAP + r], near, CAP + r)


def pick_near(wanted, far1, far3):
    return pl.pallas_call(
        pick_near_kernel,
        out_shape=jax.ShapeDtypeStruct((2 * CAP * BLOCK, C), jnp.bfloat16),
        in_specs=[SMEM] + [VMEM] * 2,
        out_specs=VMEM,
        compiler_params=pltpu.CompilerParams(vmem_limit_bytes=20 << 20),
        name="pick_near",
    )(wanted, far1, far3)


def pick_late_kernel(asked, wanted, own, far1, far3, low2, high2, near, out1, out3, out2a, out2b, line, far2):
    far2[pl.ds(0, HALF_ROWS), :] = low2[...]
    far2[pl.ds(HALF_ROWS, HALF_ROWS + 16), :] = high2[...]
    tables = ((0, own), (1, far1), (3, far3), (2, far2))
    for r in range(CAP):
        move(far2, asked[0, 2 * CAP + r], out1, r)
        move(far2, asked[2, 2 * CAP + r], out3, r)
        move(far2, wanted[2 * CAP + r], near, r)
    for i, (k, table) in enumerate(tables):
        for r in range(CAP):
            out, at = (out2a, i) if i < 3 else (out2b, 0)
            move(table, asked[1, k * CAP + r], out, at * CAP + r)
    rows = sum(t[pl.ds(OWN_ROWS, 16), :].astype(jnp.float32) for _, t in tables)
    sums = jnp.sum(rows, axis=0, keepdims=True)
    line[...] = jnp.broadcast_to(sums, (8, C))


def pick_late(asked, wanted, own, far1, far3, low2, high2):
    b16 = jnp.bfloat16
    piece = jax.ShapeDtypeStruct((CAP * BLOCK, C), b16)
    return pl.pallas_call(
        pick_late_kernel,
        out_shape=(
            piece,
            piece,
            piece,
            jax.ShapeDtypeStruct((3 * CAP * BLOCK, C), b16),
            piece,
            jax.ShapeDtypeStruct((8, C), jnp.float32),
        ),
        in_specs=[SMEM] * 2 + [VMEM] * 5,
        out_specs=(VMEM,) * 6,
        scratch_shapes=[pltpu.VMEM((SENT_ROWS, C), b16)],
        compiler_params=pltpu.CompilerParams(vmem_limit_bytes=20 << 20),
        name="pick_late",
    )(asked, wanted, own, far1, far3, low2, high2)


def tile_kernel(part, table_count, resume, finish, *refs):
    refs = list(refs)
    lists, words, own = refs[:3]
    tables = refs[3 : 3 + table_count]
    refs = refs[3 + table_count :]
    if resume:
        earlier = refs.pop(0)
    if finish:
        current, all_sums, fresh = refs[:3]
        refs = refs[3:]
        if finish == "more":
            sent = refs.pop(0)
    if finish == "end":
        ready, sems = refs[:2]
        refs = refs[2:]
    total, score_a, score_b, bits = refs[:4]

    row = lax.broadcasted_iota(jnp.int32, (BLOCK, BLOCK), 0)
    bits[...] = lax.shift_left(jnp.ones_like(row), lax.rem(row, 30))
    total[...] = earlier[...] if resume else jnp.zeros_like(total)
    sub = lax.broadcasted_iota(jnp.int32, (8, BLOCK), 0)
    if table_count == 1:
        held = tables[0]
    else:
        held = refs[4]
        at = 0
        for table in tables:
            held[pl.ds(at, table.shape[0]), :] = table[...]
            at += table.shape[0]

    def rows_of(index):
        return pl.ds(pl.multiple_of(index * BLOCK, BLOCK), BLOCK)

    def word_rows(pattern):
        rows = []
        for v in range(BLOCK // 8):
            low, high = 8 * v // 30, (8 * v + 7) // 30
            chunk = jnp.broadcast_to(words[pattern, low : low + 1, :], (8, BLOCK))
            if high != low:
                other = jnp.broadcast_to(words[pattern, high : high + 1, :], (8, BLOCK))
                chunk = jnp.where(sub + 8 * v < 30 * high, chunk, other)
            rows.append(chunk)
        return jnp.concatenate(rows, axis=0)

    size = GROUP[part]

    def target(slot):
        return rows_of(lists[SLOTS + (slot >> 1)])

    def remote(slot, i):
        return held[rows_of(lists[slot + i] & 63), :]

    def score(slot, out):
        mine = own[target(slot), :]
        for i in range(size):
            out[:, i * BLOCK : (i + 1) * BLOCK] = lax.dot_general(
                mine,
                remote(slot, i),
                (((1,), (1,)), ((), ())),
                preferred_element_type=jnp.float32,
            )

    def add(slot, scores):
        weights = []
        for i in range(size):
            packed = word_rows(lists[slot + i] >> 6)
            negative = jnp.minimum(scores[:, i * BLOCK : (i + 1) * BLOCK] * (-1.0 / UNIT), -FLOOR)
            weight = 1.0 / (1.0 - jnp.exp(negative))
            linked = (packed & bits[...]) != 0
            weights.append(jnp.where(linked, weight, 0.0).astype(jnp.bfloat16))
        total[target(slot), :] += jnp.dot(
            jnp.concatenate(weights, axis=1),
            jnp.concatenate([remote(slot, i) for i in range(size)], axis=0),
            preferred_element_type=jnp.float32,
        )

    start, stop = lists[STARTS + part], lists[STARTS + part + 1]
    score(start, score_a)

    def two(i, _):
        slot = pl.multiple_of(start + 2 * size * i, size)
        score(slot + size, score_b)
        add(slot, score_a)
        score(jnp.minimum(slot + 2 * size, stop - size), score_a)
        add(slot + size, score_b)
        return 0

    lax.fori_loop(0, lax.shift_right_logical(stop - start, size.bit_length()), two, 0)

    if not finish:
        return
    col_sums = all_sums[0:1, :]
    moved_sums = jnp.zeros((8, C), jnp.float32)
    copies = []
    for j in range(BPD):
        at = pl.ds(j * BLOCK, BLOCK)
        moved = jnp.maximum(current[at, :] + STEP_SIZE * (total[at, :] - col_sums), 0.0)
        if finish == "more":
            fresh[at, :] = moved
            sent[at, :] = moved.astype(jnp.bfloat16)
            moved_sums = moved_sums + jnp.sum(moved.reshape(BLOCK // 8, 8, C), axis=0)
        else:
            ready[at, :] = moved
            copies.append(pltpu.make_async_copy(ready.at[at, :], fresh.at[at, :], sems.at[j]))
            copies[j].start()
    if finish == "more":
        sent[pl.ds(OWN_ROWS, 16), :] = sum_rows(jnp.sum(moved_sums, axis=0, keepdims=True))
    for copy in copies:
        copy.wait()


def run_tiles(name, part, lists, words, own, tables, earlier=None, current=None, sums=None, finish=""):
    f32 = jnp.float32
    blocks = jax.ShapeDtypeStruct((OWN_ROWS, C), f32)
    args = [lists, words, own, *tables]
    specs = [SMEM] + [VMEM] * (2 + len(tables))
    scratch = []
    out = [blocks]
    if earlier is not None:
        args.append(earlier)
        specs.append(VMEM)
    if finish:
        args += [current, sums]
        specs += [VMEM] * 2
        if finish == "end":
            scratch += [pltpu.VMEM((OWN_ROWS, C), f32), pltpu.SemaphoreType.DMA((BPD,))]
        scratch.append(pltpu.VMEM((OWN_ROWS, C), f32))
        if finish == "more":
            out.append(jax.ShapeDtypeStruct((SENT_ROWS, C), jnp.bfloat16))
    scratch += [
        pltpu.VMEM((BLOCK, GROUP[part] * BLOCK), f32),
        pltpu.VMEM((BLOCK, GROUP[part] * BLOCK), f32),
        pltpu.VMEM((BLOCK, BLOCK), jnp.int32),
    ]
    if len(tables) > 1:
        scratch.append(pltpu.VMEM((sum(t.shape[0] for t in tables), C), jnp.bfloat16))
    return pl.pallas_call(
        functools.partial(tile_kernel, part, len(tables), earlier is not None, finish),
        out_shape=tuple(out),
        in_specs=specs,
        out_specs=(HBM,) if finish == "end" else (VMEM,) * len(out),
        scratch_shapes=scratch,
        compiler_params=pltpu.CompilerParams(vmem_limit_bytes=24 << 20),
        name=name,
    )(*args)


def per_device(affiliations, tile_block, tile_target, tile_pattern, tile_count, block_home, patterns):
    y, x = lax.axis_index("rows_0"), lax.axis_index("rows_1")
    core = lax.axis_index("cols_1")
    place = jnp.stack([jnp.where(core == 0, x, y), jnp.where(core == 0, y, x), core])
    current = affiliations
    own = first(current)
    requests, codes = ask(
        place.astype(jnp.int32), tile_block[0], tile_target[0], tile_count, block_home
    )
    requests = requests.reshape(SIDE, PICKED)
    asked = jnp.stack([fetch(requests[m], 0, SIDE - m) for m in (1, 2, 3)])
    words = jnp.concatenate([patterns, jnp.zeros((1, *patterns.shape[1:]), jnp.int32)], axis=0)

    lists = sort_tiles(codes, tile_pattern[0], tile_count)
    for step in range(STEPS):
        far1, far3 = fetch(own, 1, 0), fetch(own, 3, 0)
        pass1, pass3, out1, out3 = pick_early(asked, own, far1, far3)
        near = pick_near(requests[0], far1, far3)
        low2, high2 = fetch(pass1, 1, 0), fetch(pass3, 3, 0)
        side1, side3 = fetch(out1, 0, 1), fetch(out3, 0, 3)
        (total,) = run_tiles("near", 0, lists, words, own, (near,))
        total, low2, high2 = lax.optimization_barrier((total, low2, high2))
        near, out1, out3, out2a, out2b, line = pick_late(asked, requests[0], own, far1, far3, low2, high2)
        lines = tuple(fetch(line, 0, m) for m in (1, 3, 2))
        lines, out2a, out2b, side1, side3 = lax.optimization_barrier(
            (lines, out2a, out2b, side1, side3)
        )
        side2a, side2b = fetch(out2a, 0, 2), fetch(out2b, 0, 2)
        late1, late3 = fetch(out1, 0, 1), fetch(out3, 0, 3)
        sums = line + lines[0] + lines[1] + lines[2]
        other = swap(sums, "cols_1", 1)
        (total,) = run_tiles("sides_1", 1, lists, words, own, (side1, near), total)
        total, other = lax.optimization_barrier((total, other))
        sums = sums + other
        other = swap(sums, "cols_0", 1)
        (total,) = run_tiles("sides_3", 2, lists, words, own, (side3,), total)
        total, other = lax.optimization_barrier((total, other))
        sums = sums + other
        other = swap(sums, "cols_0", 2)
        (total,) = run_tiles("across", 3, lists, words, own, (side2a,), total)
        total, other, late1, late3 = lax.optimization_barrier((total, other, late1, late3))
        col_sums = sums + other
        (total,) = run_tiles("late", 4, lists, words, own, (late1, late3), total)
        total, side2b = lax.optimization_barrier((total, side2b))
        finish = "more" if step < STEPS - 1 else "end"
        current, *own_next = run_tiles(
            "last", 5, lists, words, own, (side2b,), total, current, col_sums, finish
        )
        if own_next:
            (own,) = own_next
    return current


def solution(mesh):
    torus = Mesh(mesh.devices.reshape(4, 4, 4, 2), ALL)
    return jax.shard_map(
        per_device,
        mesh=torus,
        in_specs=(P(ALL, None), P(ALL, None), P(ALL, None), P(ALL, None), P(ALL), P(), P()),
        out_specs=P(ALL, None),
        check_vma=False,
    )
```

```python
import functools

import jax
import jax.numpy as jnp
from jax import lax
from jax.experimental import pallas as pl
from jax.experimental.pallas import tpu as pltpu
from jax.sharding import Mesh
from jax.sharding import PartitionSpec as P

C = 512
BLOCK = 128
STEPS = 2
BPD = 8
SIDE = 4
CAP = 4
N_COLS = 8
NODES = 131072
UNIT = 1572864
PATTERNS = 192
TILES = 240
PARTS = 6
GROUP = (4, 4, 4, 4, 2, 2)
KEYS = PARTS * BPD
SLOTS = TILES + sum(BPD * (g - 1) + 2 * g for g in GROUP) // 16 * 16 + 16
STARTS = SLOTS + SLOTS // 2
LIST = STARTS + 8
EMPTY = PATTERNS * 64
FLOOR = 0.001
STEP_SIZE = 0.3 / NODES
OWN_ROWS = BPD * BLOCK
SENT_ROWS = OWN_ROWS + 16
PICKED = SIDE * CAP
HALF_ROWS = OWN_ROWS // 2

ALL = ("rows_0", "rows_1", "cols_0", "cols_1")
VMEM = pl.BlockSpec(memory_space=pltpu.VMEM)
SMEM = pl.BlockSpec(memory_space=pltpu.SMEM)
HBM = pl.BlockSpec(memory_space=pltpu.HBM)


def pairs(first, second):
    out = []
    for y in range(SIDE):
        for x in range(SIDE):
            for z in range(4):
                for core in range(2):
                    dx, dy = (first, second) if core == 0 else (second, first)
                    sy, sx = (y + dy) % SIDE, (x + dx) % SIDE
                    out.append((((sy * 4 + sx) * 4 + z) * 2 + core, ((y * 4 + x) * 4 + z) * 2 + core))
    return out


def fetch(value, first, second):
    return lax.ppermute(value, ALL, pairs(first, second))


def swap(value, axis, step):
    return lax.ppermute(value, axis, [(i, i ^ step) for i in range(lax.axis_size(axis))])


OWNERS = (
    ((0, 1), (0, 3)),
    ((1, 0), (1, 1), (1, 3), (0, 2)),
    ((3, 0), (3, 1), (3, 3)),
    ((2, 0), (2, 1), (2, 3)),
    ((1, 2), (3, 2)),
    ((2, 2),),
)


def clear(ref, start, size, value):
    def body(i, _):
        for j in range(8):
            ref[start + 8 * i + j] = value
        return 0

    lax.fori_loop(0, size // 8, body, 0)


def ask_kernel(place, blocks, targets, count, home, requests, codes, rank, fill, base):
    first, second, core = place[0], place[1], place[2]
    clear(rank, 0, 128, -1)
    clear(fill, 0, 16, 0)
    clear(requests, 0, 64, 0)
    base[0] = 0
    for part, owners in enumerate(OWNERS):
        for i, (m, k) in enumerate(owners):
            base[m * SIDE + k] = part * 512 + i * CAP

    def note(t, _):
        slot = home[blocks[t]]
        row = slot >> 6
        local = slot & (BPD - 1)
        y, x = row >> 2, row & (SIDE - 1)
        owner_first = jnp.where(core == 0, x, y)
        owner_second = jnp.where(core == 0, y, x)
        k = (owner_first - first) & (SIDE - 1)
        m = (owner_second - second) & (SIDE - 1)
        pair = m * SIDE + k
        seen = rank[pair * BPD + local]
        held = fill[pair]
        mine = jnp.minimum(jnp.where(seen < 0, held, seen), CAP - 1)
        rank[pair * BPD + local] = mine
        fill[pair] = jnp.where(seen < 0, held + 1, held)
        requests[pair * CAP + mine] = local
        codes[t] = base[pair] + mine + targets[t] * 64
        return 0

    lax.fori_loop(0, count[0], note, 0)


def ask(place, blocks, targets, count, home):
    i32 = jnp.int32
    return pl.pallas_call(
        ask_kernel,
        out_shape=(jax.ShapeDtypeStruct((64,), i32), jax.ShapeDtypeStruct((TILES,), i32)),
        in_specs=[SMEM] * 5,
        out_specs=(SMEM,) * 2,
        scratch_shapes=[pltpu.SMEM((128,), i32), pltpu.SMEM((16,), i32), pltpu.SMEM((16,), i32)],
        compiler_params=pltpu.CompilerParams(vmem_limit_bytes=2 << 20),
        name="ask",
    )(place, blocks, targets, count, home)


def sort_kernel(codes, pattern_ids, count, lists, per_key):
    clear(per_key, 0, KEYS, 0)
    clear(lists, 0, SLOTS, EMPTY)
    clear(lists, SLOTS, SLOTS // 2, 0)

    def tally(t, _):
        key = codes[t] >> 6
        per_key[key] = per_key[key] + 1
        return 0

    lax.fori_loop(0, count[0], tally, 0)
    slot = jnp.int32(0)
    for part, size in enumerate(GROUP):
        lists[STARTS + part] = slot
        start = slot
        for target in range(BPD):
            key = part * BPD + target
            tiles = per_key[key]
            per_key[key] = slot
            slot = slot + ((tiles + size - 1) & -size)
        slot = start + jnp.maximum(2 * size, (slot - start + 2 * size - 1) & -(2 * size))
    lists[STARTS + PARTS] = slot

    def put(t, _):
        code = codes[t]
        key = code >> 6
        at = per_key[key]
        per_key[key] = at + 1
        lists[at] = pattern_ids[t] * 64 + (code & 63)
        lists[SLOTS + (at >> 1)] = key & (BPD - 1)
        return 0

    lax.fori_loop(0, count[0], put, 0)


def sort_tiles(codes, pattern_ids, count):
    i32 = jnp.int32
    return pl.pallas_call(
        sort_kernel,
        out_shape=jax.ShapeDtypeStruct((LIST,), i32),
        in_specs=[SMEM] * 3,
        out_specs=SMEM,
        scratch_shapes=[pltpu.SMEM((KEYS,), i32)],
        compiler_params=pltpu.CompilerParams(vmem_limit_bytes=2 << 20),
        name="sort_tiles",
    )(codes, pattern_ids, count)


def sum_rows(total):
    high = total.astype(jnp.bfloat16).astype(jnp.float32)
    rest = total - high
    middle = rest.astype(jnp.bfloat16).astype(jnp.float32)
    low = rest - middle
    row = lax.broadcasted_iota(jnp.int32, (16, C), 0)
    out = jnp.where(row == 0, high, jnp.where(row == 1, middle, jnp.where(row == 2, low, 0.0)))
    return out.astype(jnp.bfloat16)


def first_kernel(current, sent):
    total = jnp.zeros((8, C), jnp.float32)
    for j in range(BPD):
        rows = current[pl.ds(j * BLOCK, BLOCK), :]
        sent[pl.ds(j * BLOCK, BLOCK), :] = rows.astype(jnp.bfloat16)
        total = total + jnp.sum(rows.reshape(BLOCK // 8, 8, C), axis=0)
    sent[pl.ds(OWN_ROWS, 16), :] = sum_rows(jnp.sum(total, axis=0, keepdims=True))


def first(current):
    return pl.pallas_call(
        first_kernel,
        out_shape=jax.ShapeDtypeStruct((SENT_ROWS, C), jnp.bfloat16),
        in_specs=[VMEM],
        out_specs=VMEM,
        compiler_params=pltpu.CompilerParams(vmem_limit_bytes=20 << 20),
        name="first",
    )(current)


def move(table, local, out, at):
    rows = pl.ds(pl.multiple_of(local * BLOCK, BLOCK), BLOCK)
    out[pl.ds(at * BLOCK, BLOCK), :] = table[rows, :]


def pick_early_kernel(asked, own, far1, far3, pass1, pass3, out1, out3):
    pass1[...] = far1[pl.ds(0, HALF_ROWS), :]
    pass3[...] = far3[pl.ds(HALF_ROWS, HALF_ROWS + 16), :]
    for m, out in ((1, out1), (3, out3)):
        for i, (k, table) in enumerate(((0, own), (1, far1), (3, far3))):
            for r in range(CAP):
                move(table, asked[m - 1, k * CAP + r], out, i * CAP + r)


def pick_early(asked, own, far1, far3):
    b16 = jnp.bfloat16
    out = jax.ShapeDtypeStruct((3 * CAP * BLOCK, C), b16)
    return pl.pallas_call(
        pick_early_kernel,
        out_shape=(
            jax.ShapeDtypeStruct((HALF_ROWS, C), b16),
            jax.ShapeDtypeStruct((HALF_ROWS + 16, C), b16),
            out,
            out,
        ),
        in_specs=[SMEM] + [VMEM] * 3,
        out_specs=(VMEM,) * 4,
        compiler_params=pltpu.CompilerParams(vmem_limit_bytes=20 << 20),
        name="pick_early",
    )(asked, own, far1, far3)


def pick_near_kernel(wanted, far1, far3, near):
    for r in range(CAP):
        move(far1, wanted[CAP + r], near, r)
        move(far3, wanted[3 * CAP + r], near, CAP + r)


def pick_near(wanted, far1, far3):
    return pl.pallas_call(
        pick_near_kernel,
        out_shape=jax.ShapeDtypeStruct((2 * CAP * BLOCK, C), jnp.bfloat16),
        in_specs=[SMEM] + [VMEM] * 2,
        out_specs=VMEM,
        compiler_params=pltpu.CompilerParams(vmem_limit_bytes=20 << 20),
        name="pick_near",
    )(wanted, far1, far3)


def pick_late_kernel(asked, wanted, own, far1, far3, low2, high2, near, out1, out3, out2a, out2b, line, far2):
    far2[pl.ds(0, HALF_ROWS), :] = low2[...]
    far2[pl.ds(HALF_ROWS, HALF_ROWS + 16), :] = high2[...]
    tables = ((0, own), (1, far1), (3, far3), (2, far2))
    for r in range(CAP):
        move(far2, asked[0, 2 * CAP + r], out1, r)
        move(far2, asked[2, 2 * CAP + r], out3, r)
        move(far2, wanted[2 * CAP + r], near, r)
    for i, (k, table) in enumerate(tables):
        for r in range(CAP):
            out, at = (out2a, i) if i < 3 else (out2b, 0)
            move(table, asked[1, k * CAP + r], out, at * CAP + r)
    rows = sum(t[pl.ds(OWN_ROWS, 16), :].astype(jnp.float32) for _, t in tables)
    sums = jnp.sum(rows, axis=0, keepdims=True)
    line[...] = jnp.broadcast_to(sums, (8, C))


def pick_late(asked, wanted, own, far1, far3, low2, high2):
    b16 = jnp.bfloat16
    piece = jax.ShapeDtypeStruct((CAP * BLOCK, C), b16)
    return pl.pallas_call(
        pick_late_kernel,
        out_shape=(
            piece,
            piece,
            piece,
            jax.ShapeDtypeStruct((3 * CAP * BLOCK, C), b16),
            piece,
            jax.ShapeDtypeStruct((8, C), jnp.float32),
        ),
        in_specs=[SMEM] * 2 + [VMEM] * 5,
        out_specs=(VMEM,) * 6,
        scratch_shapes=[pltpu.VMEM((SENT_ROWS, C), b16)],
        compiler_params=pltpu.CompilerParams(vmem_limit_bytes=20 << 20),
        name="pick_late",
    )(asked, wanted, own, far1, far3, low2, high2)


def tile_kernel(part, table_count, resume, finish, *refs):
    refs = list(refs)
    lists, words, own = refs[:3]
    tables = refs[3 : 3 + table_count]
    refs = refs[3 + table_count :]
    if resume:
        earlier = refs.pop(0)
    if finish:
        current, all_sums, fresh = refs[:3]
        refs = refs[3:]
        if finish == "more":
            sent = refs.pop(0)
    if finish == "end":
        ready, sems = refs[:2]
        refs = refs[2:]
    total, score_a, score_b, bits = refs[:4]

    row = lax.broadcasted_iota(jnp.int32, (BLOCK, BLOCK), 0)
    bits[...] = lax.shift_left(jnp.ones_like(row), lax.rem(row, 30))
    total[...] = earlier[...] if resume else jnp.zeros_like(total)
    sub = lax.broadcasted_iota(jnp.int32, (8, BLOCK), 0)
    if table_count == 1:
        held = tables[0]
    else:
        held = refs[4]
        at = 0
        for table in tables:
            held[pl.ds(at, table.shape[0]), :] = table[...]
            at += table.shape[0]

    def rows_of(index):
        return pl.ds(pl.multiple_of(index * BLOCK, BLOCK), BLOCK)

    def word_rows(pattern):
        rows = []
        for v in range(BLOCK // 8):
            low, high = 8 * v // 30, (8 * v + 7) // 30
            chunk = jnp.broadcast_to(words[pattern, low : low + 1, :], (8, BLOCK))
            if high != low:
                other = jnp.broadcast_to(words[pattern, high : high + 1, :], (8, BLOCK))
                chunk = jnp.where(sub + 8 * v < 30 * high, chunk, other)
            rows.append(chunk)
        return jnp.concatenate(rows, axis=0)

    size = GROUP[part]

    def target(slot):
        return rows_of(lists[SLOTS + (slot >> 1)])

    def remote(slot, i):
        return held[rows_of(lists[slot + i] & 63), :]

    def score(slot, out):
        mine = own[target(slot), :]
        for i in range(size):
            out[:, i * BLOCK : (i + 1) * BLOCK] = lax.dot_general(
                mine,
                remote(slot, i),
                (((1,), (1,)), ((), ())),
                preferred_element_type=jnp.float32,
            )

    def add(slot, scores):
        weights = []
        for i in range(size):
            packed = word_rows(lists[slot + i] >> 6)
            negative = jnp.minimum(scores[:, i * BLOCK : (i + 1) * BLOCK] * (-1.0 / UNIT), -FLOOR)
            weight = 1.0 / (1.0 - jnp.exp(negative))
            linked = (packed & bits[...]) != 0
            weights.append(jnp.where(linked, weight, 0.0).astype(jnp.bfloat16))
        total[target(slot), :] += jnp.dot(
            jnp.concatenate(weights, axis=1),
            jnp.concatenate([remote(slot, i) for i in range(size)], axis=0),
            preferred_element_type=jnp.float32,
        )

    start, stop = lists[STARTS + part], lists[STARTS + part + 1]
    score(start, score_a)

    def two(i, _):
        slot = pl.multiple_of(start + 2 * size * i, size)
        score(slot + size, score_b)
        add(slot, score_a)
        score(jnp.minimum(slot + 2 * size, stop - size), score_a)
        add(slot + size, score_b)
        return 0

    lax.fori_loop(0, lax.shift_right_logical(stop - start, size.bit_length()), two, 0)

    if not finish:
        return
    col_sums = all_sums[0:1, :]
    moved_sums = jnp.zeros((8, C), jnp.float32)
    copies = []
    for j in range(BPD):
        at = pl.ds(j * BLOCK, BLOCK)
        moved = jnp.maximum(current[at, :] + STEP_SIZE * (total[at, :] - col_sums), 0.0)
        if finish == "more":
            fresh[at, :] = moved
            sent[at, :] = moved.astype(jnp.bfloat16)
            moved_sums = moved_sums + jnp.sum(moved.reshape(BLOCK // 8, 8, C), axis=0)
        else:
            ready[at, :] = moved
            copies.append(pltpu.make_async_copy(ready.at[at, :], fresh.at[at, :], sems.at[j]))
            copies[j].start()
    if finish == "more":
        sent[pl.ds(OWN_ROWS, 16), :] = sum_rows(jnp.sum(moved_sums, axis=0, keepdims=True))
    for copy in copies:
        copy.wait()


def run_tiles(name, part, lists, words, own, tables, earlier=None, current=None, sums=None, finish=""):
    f32 = jnp.float32
    blocks = jax.ShapeDtypeStruct((OWN_ROWS, C), f32)
    args = [lists, words, own, *tables]
    specs = [SMEM] + [VMEM] * (2 + len(tables))
    scratch = []
    out = [blocks]
    if earlier is not None:
        args.append(earlier)
        specs.append(VMEM)
    if finish:
        args += [current, sums]
        specs += [VMEM] * 2
        if finish == "end":
            scratch += [pltpu.VMEM((OWN_ROWS, C), f32), pltpu.SemaphoreType.DMA((BPD,))]
        scratch.append(pltpu.VMEM((OWN_ROWS, C), f32))
        if finish == "more":
            out.append(jax.ShapeDtypeStruct((SENT_ROWS, C), jnp.bfloat16))
    scratch += [
        pltpu.VMEM((BLOCK, GROUP[part] * BLOCK), f32),
        pltpu.VMEM((BLOCK, GROUP[part] * BLOCK), f32),
        pltpu.VMEM((BLOCK, BLOCK), jnp.int32),
    ]
    if len(tables) > 1:
        scratch.append(pltpu.VMEM((sum(t.shape[0] for t in tables), C), jnp.bfloat16))
    return pl.pallas_call(
        functools.partial(tile_kernel, part, len(tables), earlier is not None, finish),
        out_shape=tuple(out),
        in_specs=specs,
        out_specs=(HBM,) if finish == "end" else (VMEM,) * len(out),
        scratch_shapes=scratch,
        compiler_params=pltpu.CompilerParams(vmem_limit_bytes=24 << 20),
        name=name,
    )(*args)


def per_device(affiliations, tile_block, tile_target, tile_pattern, tile_count, block_home, patterns):
    y, x = lax.axis_index("rows_0"), lax.axis_index("rows_1")
    core = lax.axis_index("cols_1")
    place = jnp.stack([jnp.where(core == 0, x, y), jnp.where(core == 0, y, x), core])
    current = affiliations
    own = first(current)
    requests, codes = ask(
        place.astype(jnp.int32), tile_block[0], tile_target[0], tile_count, block_home
    )
    requests = requests.reshape(SIDE, PICKED)
    asked = jnp.stack([fetch(requests[m], 0, SIDE - m) for m in (1, 2, 3)])
    words = jnp.concatenate([patterns, jnp.zeros((1, *patterns.shape[1:]), jnp.int32)], axis=0)

    lists = sort_tiles(codes, tile_pattern[0], tile_count)
    for step in range(STEPS):
        far1, far3 = fetch(own, 1, 0), fetch(own, 3, 0)
        pass1, pass3, out1, out3 = pick_early(asked, own, far1, far3)
        near = pick_near(requests[0], far1, far3)
        low2, high2 = fetch(pass1, 1, 0), fetch(pass3, 3, 0)
        side1, side3 = fetch(out1, 0, 1), fetch(out3, 0, 3)
        (total,) = run_tiles("near", 0, lists, words, own, (near,))
        total, low2, high2 = lax.optimization_barrier((total, low2, high2))
        near, out1, out3, out2a, out2b, line = pick_late(asked, requests[0], own, far1, far3, low2, high2)
        lines = tuple(fetch(line, 0, m) for m in (1, 3, 2))
        lines, out2a, out2b, side1, side3 = lax.optimization_barrier(
            (lines, out2a, out2b, side1, side3)
        )
        side2a, side2b = fetch(out2a, 0, 2), fetch(out2b, 0, 2)
        late1, late3 = fetch(out1, 0, 1), fetch(out3, 0, 3)
        sums = line + lines[0] + lines[1] + lines[2]
        other = swap(sums, "cols_1", 1)
        (total,) = run_tiles("sides_1", 1, lists, words, own, (side1, near), total)
        total, other = lax.optimization_barrier((total, other))
        sums = sums + other
        other = swap(sums, "cols_0", 1)
        (total,) = run_tiles("sides_3", 2, lists, words, own, (side3,), total)
        total, other = lax.optimization_barrier((total, other))
        sums = sums + other
        other = swap(sums, "cols_0", 2)
        (total,) = run_tiles("across", 3, lists, words, own, (side2a,), total)
        total, other, late1, late3 = lax.optimization_barrier((total, other, late1, late3))
        col_sums = sums + other
        (total,) = run_tiles("late", 4, lists, words, own, (late1, late3), total)
        total, side2b = lax.optimization_barrier((total, side2b))
        finish = "more" if step < STEPS - 1 else "end"
        current, *own_next = run_tiles(
            "last", 5, lists, words, own, (side2b,), total, current, col_sums, finish
        )
        if own_next:
            (own,) = own_next
    return current


def solution(mesh):
    torus = Mesh(mesh.devices.reshape(4, 4, 4, 2), ALL)
    return jax.shard_map(
        per_device,
        mesh=torus,
        in_specs=(P(ALL, None), P(ALL, None), P(ALL, None), P(ALL, None), P(ALL), P(), P()),
        out_specs=P(ALL, None),
        check_vma=False,
    )
```
